32 devices in a mesh: ctx: 8 (over y, x, core), chan: 4 (over z).
Axes of the slice: x: 2, y: 2, z: 4, core: 2. Of those that a mesh axis runs over, the one named last changes fastest.
Arguments:
- signal: float32 [2048, 2048], P('chan', 'ctx'), may hold values from -6 to 6
- gate_in: float32 [2048, 2048], P('chan', 'ctx'), may hold values from -6 to 6
- filter_raw: float32 [2048, 2048], P('chan', 'ctx'), may hold values from -6 to 6
- short_kernel: float32 [2048, 7], P('chan'), may hold values from -2 to 2
- skip_gain: float32 [2048], P('chan'), may hold values from -4 to 4
- out_weight: float32 [2048, 2048], P(None, 'chan'), may hold values from -0.125 to 0.125
- cotangent: float32 [2048, 2048], P('chan', 'ctx'), may hold values from -6 to 6
Outputs:
- grad_gate: float32 [2048, 2048], P('chan', 'ctx')
- grad_signal: float32 [2048, 2048], P('chan', 'ctx')
- grad_filter: float32 [2048, 2048], P('chan', 'ctx')
- grad_kernel: float32 [2048, 7], P('chan')
- grad_skip: float32 [2048], P('chan')
The draws below stay inside these ranges and needn't reach their ends.
All inputs are finite; a program needn't handle non-finite values.
Results may differ from the reference program's by a relative error of at most 0.00011.
Values sent between devices are 32-bit elements; how exact they have to be, the bound alone decides.
A program may use at most 128 MiB of HBM per device.

```python
import math
import jax
import jax.numpy as jnp
from jax import lax

CH = 2048
KW = 7
TOKENS = 2048


def block_scale(key, shape, pieces, smallest, high):
    level, own = 1.0, jax.random.fold_in(key, 6)
    for dim, parts in pieces:
        heights = jnp.exp(jax.random.uniform(jax.random.fold_in(own, dim), (parts,), jnp.float32, smallest / len(pieces), high / len(pieces)))
        level = level * jnp.repeat(heights, shape[dim] // parts).reshape([-1 if axis == dim else 1 for axis in range(len(shape))])
    return level


def normal_values(own_key, shape, scale, most, cuts=(), dtype=jnp.bfloat16):
    entries = scale * jax.random.normal(own_key, shape, jnp.float32)
    if cuts:
        entries = entries * block_scale(own_key, shape, cuts, -0.22, 0.18)
    return jnp.clip(entries, -most, most).astype(dtype)


def setup_inputs(seed: int = 0) -> dict:
    key_list = jax.random.split(jax.random.key(seed), 8)
    return {
        "signal": normal_values(key_list[0], (CH, TOKENS), 1.0, 6.0, ((0, 4), (1, 8)), jnp.float32),
        "gate_in": normal_values(key_list[1], (CH, TOKENS), 1.0, 6.0, ((0, 4), (1, 8)), jnp.float32),
        "filter_raw": normal_values(key_list[2], (CH, TOKENS), 1.0, 6.0, ((0, 4), (1, 8)), jnp.float32),
        "short_kernel": normal_values(key_list[3], (CH, KW), KW ** -0.5, 2.0, ((0, 4),), jnp.float32),
        "skip_gain": normal_values(key_list[4], (CH,), 1.0, 4.0, ((0, 4),), jnp.float32),
        "out_weight": normal_values(key_list[5], (CH, CH), CH ** -0.5, 0.125, ((1, 4),), jnp.float32),
        "cotangent": normal_values(key_list[6], (CH, TOKENS), 1.0, 6.0, ((0, 4), (1, 8)), jnp.float32),
    }


def causal_taps(series, short_kernel):
    kernel_taps = short_kernel.shape[1]
    length = series.shape[1]
    padded = jnp.pad(series, ((0, 0), (kernel_taps - 1, 0)))
    result = jnp.zeros_like(series)
    for j in range(kernel_taps):
        result = result + short_kernel[:, j:j + 1] * padded[:, kernel_taps - 1 - j:kernel_taps - 1 - j + length]
    return (result, padded)

def channel_block(operands):
    signal, gate_in, filter_raw, short_kernel, skip_gain, grad_mix = operands
    scale_factor = 1.0 / math.sqrt(TOKENS)
    kernel_taps = short_kernel.shape[1]
    length = signal.shape[1]
    doubled = 2 * length
    conv_in, padded = causal_taps(signal, short_kernel)
    long_filter = filter_raw * scale_factor
    filter_spec = jnp.fft.rfft(long_filter, n=doubled, axis=1)
    value_spec = jnp.fft.rfft(conv_in, n=doubled, axis=1)
    long_conv = jnp.fft.irfft(filter_spec * value_spec, n=doubled, axis=1)[:, :length]
    response = long_conv + skip_gain[:, None] * conv_in
    grad_gate = grad_mix * response
    grad_resp = grad_mix * gate_in
    grad_spec = jnp.fft.rfft(grad_resp, n=doubled, axis=1)
    grad_value = jnp.fft.irfft(jnp.conj(filter_spec) * grad_spec, n=doubled, axis=1)[:, :length]
    grad_value = grad_value + skip_gain[:, None] * grad_resp
    grad_filter = jnp.fft.irfft(jnp.conj(value_spec) * grad_spec, n=doubled, axis=1)[:, :length] * scale_factor
    extended = jnp.pad(grad_value, ((0, 0), (0, kernel_taps - 1)))
    grad_signal = jnp.zeros_like(grad_value)
    for j in range(kernel_taps):
        grad_signal = grad_signal + short_kernel[:, j:j + 1] * extended[:, j:j + length]
    grad_kernel = jnp.stack([lax.optimization_barrier(jnp.sum(grad_value * padded[:, kernel_taps - 1 - j:kernel_taps - 1 - j + length], axis=1)) for j in range(kernel_taps)], axis=1) * scale_factor
    grad_skip = lax.optimization_barrier(jnp.sum(grad_resp * conv_in, axis=1)) * scale_factor
    return (grad_gate, grad_signal, grad_filter, grad_kernel, grad_skip)

def reference(signal, gate_in, filter_raw, short_kernel, skip_gain, out_weight, cotangent):
    grad_mix = jnp.dot(out_weight.T, cotangent, precision=lax.Precision.HIGHEST, preferred_element_type=jnp.float32)
    block_size = 16 if CH % 16 == 0 else CH
    groups = CH // block_size

    def split_rows(array):
        return array.reshape((groups, block_size) + array.shape[1:])
    results = lax.map(channel_block, tuple((split_rows(array) for array in (signal, gate_in, filter_raw, short_kernel, skip_gain, grad_mix))))
    grad_gate, grad_signal, grad_filter, grad_kernel, grad_skip = results
    return (grad_gate.reshape(CH, TOKENS), grad_signal.reshape(CH, TOKENS), grad_filter.reshape(CH, TOKENS), grad_kernel.reshape(CH, KW), grad_skip.reshape(CH))
```

```python
import functools
import math

import jax
import jax.numpy as jnp
import numpy as np
from jax import lax
from jax.experimental import pallas as pl
from jax.experimental.pallas import tpu as pltpu
from jax.sharding import PartitionSpec as P

MESH = pl.DeviceIdType.MESH
F32 = jnp.float32
BF16 = jnp.bfloat16


def split_bf16(value):
    high = value.astype(BF16)
    return high, (value - high.astype(F32)).astype(BF16)


def tables(blocks, length, scale):
    total = 2 * blocks * length
    turn = np.arange(blocks + 1)[:, None] * np.arange(length)[None, :] % total
    angle = 2.0 * np.pi / total * turn
    weight = np.full((blocks + 1, 1), 2.0)
    weight[0] = weight[blocks] = 1.0
    weight = weight * (scale / total)
    twiddle = np.stack(
        (np.cos(angle), np.sin(angle), weight * np.cos(angle), weight * np.sin(angle))
    ).astype(np.float32)
    turn = np.arange(length)[:, None] * np.arange(length)[None, :] % length
    angle = 2.0 * np.pi / length * turn
    cosine, sine = np.cos(angle), np.sin(angle)
    matrix = np.block([[cosine, -sine], [sine, cosine]]).astype(np.float32)
    high = matrix.astype(jnp.bfloat16)
    low = (matrix - high.astype(np.float32)).astype(jnp.bfloat16)
    return twiddle, high, low


def weighted_sum(terms):
    total = None
    for factor, value in terms:
        if abs(factor) < 1e-12:
            continue
        if abs(factor - 1.0) < 1e-12:
            part = value
        elif abs(factor + 1.0) < 1e-12:
            part = -value
        else:
            part = np.float32(factor) * value
        total = part if total is None else total + part
    return total


def forward_blocks(parts, twiddle, store):
    blocks = len(parts)

    def put(q, real, imag):
        cosine, sine = twiddle[0, q : q + 1, :], twiddle[1, q : q + 1, :]
        if imag is None:
            store(q, real * cosine, -real * sine)
        else:
            store(q, real * cosine + imag * sine, imag * cosine - real * sine)

    for q in range(blocks // 2 + 1):
        def gather(first, trig, sign):
            return weighted_sum(
                [(sign * trig(math.pi * a * q / blocks), parts[a]) for a in range(first, blocks, 2)]
            )

        even_re, even_im = gather(0, math.cos, 1.0), gather(0, math.sin, -1.0)
        odd_re, odd_im = gather(1, math.cos, 1.0), gather(1, math.sin, -1.0)

        def add(a, b, sign_a, sign_b):
            return weighted_sum([(s, v) for s, v in ((sign_a, a), (sign_b, b)) if v is not None])

        put(q, add(even_re, odd_re, 1.0, 1.0), add(even_im, odd_im, 1.0, 1.0))
        if q != blocks - q:
            put(blocks - q, add(even_re, odd_re, 1.0, -1.0), add(even_im, odd_im, -1.0, 1.0))


def inverse_blocks(blocks, length, twiddle, load):
    def real_imag(q):
        pair = load(q)
        real, minus = pair[:, :length], pair[:, length:]
        cosine, sine = twiddle[2, q : q + 1, :], twiddle[3, q : q + 1, :]
        return real * cosine + minus * sine, real * sine - minus * cosine

    first, last = real_imag(0)[0], real_imag(blocks)[0]
    half_re, half_im = real_imag(blocks // 2)
    pairs = []
    for q in range(1, blocks // 2):
        (re_a, im_a), (re_b, im_b) = real_imag(q), real_imag(blocks - q)
        pairs.append((re_a + re_b, im_a - im_b, re_a - re_b, im_a + im_b))
    result = []
    for a in range(blocks):
        odd = a % 2
        terms = [(1.0, first - last if odd else first + last)]
        terms.append((math.cos(math.pi * a / 2), half_re))
        terms.append((-math.sin(math.pi * a / 2), half_im))
        for q in range(1, blocks // 2):
            angle = math.pi * a * q / blocks
            terms.append((math.cos(angle), pairs[q - 1][2 * odd]))
            terms.append((-math.sin(angle), pairs[q - 1][2 * odd + 1]))
        result.append(weighted_sum(terms))
    return result


def kernel(
    dims,
    sig_in, gate_in, fil_in, taps_in, skip_in, w_in, cot_in, twiddle_in, high_in, low_in,
    gate_out, gsig_out, gfil_out, small_out,
    w_buf, wt_hi, wt_lo, cot_all, mix, gate_buf, sig_buf, fil_buf, conv_buf,
    resp_send, resp_buf, grad_send, grad_buf, gsig_send, gfil_send, taps_ref, small_buf, small_send, small_land,
    stage, fil_spec, val_spec, grad_spec, work, twiddle, high_ref, low_ref, taps_buf, skip_buf,
    up_sem, down_sem, line_sem, send_sem, recv_sem, local_sem, load_sem,
):
    devices, groups, rows, length, taps, halves, early, late, scale = dims
    me, chan = lax.axis_index("ctx"), lax.axis_index("chan")
    half_len = length // halves
    group_rows = min(8, rows)
    classes = devices + 1

    barrier = pltpu.get_barrier_semaphore()

    @pl.loop(1, devices)
    def _(k):
        pl.semaphore_signal(
            barrier, inc=1, device_id={"ctx": lax.rem(me + k, devices)}, device_id_type=MESH
        )

    @pl.loop(1, groups)
    def _(k):
        pl.semaphore_signal(
            barrier, inc=1, device_id={"chan": lax.rem(chan + k, groups)}, device_id_type=MESH
        )

    w_copy = pltpu.make_async_copy(w_in, w_buf, load_sem.at[0])
    gate_copy = pltpu.make_async_copy(gate_in, gate_buf, load_sem.at[1])
    cot_copy = pltpu.make_async_copy(cot_in, cot_all.at[chan], load_sem.at[2])
    table_copies = [
        pltpu.make_async_copy(source, target, load_sem.at[3 + i])
        for i, (source, target) in enumerate(
            (
                (taps_in, taps_buf), (skip_in, skip_buf), (twiddle_in, twiddle),
                (high_in, high_ref), (low_in, low_ref),
            )
        )
    ]
    w_copy.start()
    cot_copy.start()
    for copy in table_copies:
        copy.start()
    gate_copy.start()

    pl.semaphore_wait(barrier, devices + groups - 2)

    def lanes(h):
        return pl.ds(h * half_len, half_len)

    def hop(step, h, up):
        block = chan - step if up else chan + step
        source = cot_in if step == 0 else cot_all.at[block]
        sems = up_sem if up else down_sem
        return pltpu.make_async_remote_copy(
            src_ref=source.at[:, lanes(h)],
            dst_ref=cot_all.at[block, :, lanes(h)],
            send_sem=sems.at[h, step],
            recv_sem=line_sem.at[h, block],
            device_id={"chan": chan + 1 if up else chan - 1},
            device_id_type=MESH,
        )

    def sends(step, up):
        if up:
            return jnp.logical_and(chan - step >= 0, chan + 1 < groups)
        return jnp.logical_and(chan + step < groups, chan >= 1)

    def arrives(step, up):
        return chan - step >= 0 if up else chan + step < groups

    def line_start(step, h):
        for up in (True, False):
            @pl.when(sends(step, up))
            def _():
                hop(step, h, up).start()

    def line_arrive(step, h):
        for up in (True, False):
            @pl.when(arrives(step, up))
            def _():
                block = chan - step if up else chan + step
                slot = cot_all.at[block, :, lanes(h)]
                pltpu.make_async_remote_copy(
                    src_ref=slot,
                    dst_ref=slot,
                    send_sem=up_sem.at[h, step],
                    recv_sem=line_sem.at[h, block],
                    device_id={"chan": chan - 1 if up else chan + 1},
                    device_id_type=MESH,
                ).wait_recv()

                @pl.when(sends(step, up))
                def _():
                    hop(step, h, up).start()

    moves = []

    def all_to_all(source, target):
        index = len(moves)

        def piece(k):
            peer = lax.rem(me + k, devices)
            return pltpu.make_async_remote_copy(
                src_ref=source(peer),
                dst_ref=target(me),
                send_sem=send_sem.at[index, k],
                recv_sem=recv_sem.at[index, k],
                device_id={"ctx": peer},
                device_id_type=MESH,
            )

        own = pltpu.make_async_copy(source(me), target(me), local_sem.at[index])

        def start():
            @pl.loop(1, devices)
            def _(k):
                piece(k).start()

            own.start()

        def arrive():
            @pl.loop(1, devices)
            def _(k):
                piece(k).wait_recv()

            own.wait()

        def sent():
            @pl.loop(1, devices)
            def _(k):
                piece(k).wait_send()

        moves.append(sent)
        return start, arrive

    def by_part(source, target, part, lane=slice(None)):
        at = pl.ds(*part)
        return all_to_all(lambda p: source.at[p, at, lane], lambda p: target.at[p, at, lane])

    sig_moves = [by_part(sig_in, sig_buf, part) for part in early]
    fil_moves = [by_part(fil_in, fil_buf, part) for part in early]
    resp_moves = [by_part(resp_send, resp_buf, part) for part in early]
    grad_moves = [
        [by_part(grad_send, grad_buf, part, lanes(h)) for part in late] for h in range(halves)
    ]
    gfil_moves = [by_part(gfil_send, gfil_out, part) for part in late]
    gsig_moves = [by_part(gsig_send, gsig_out, part) for part in late]
    small_start, small_arrive = all_to_all(lambda p: small_send, lambda p: small_land.at[p])

    for h in range(halves):
        line_start(0, h)
    for sig_move, fil_move in zip(sig_moves, fil_moves):
        sig_move[0]()
        fil_move[0]()

    def dft(read, target, part):
        span = max(part[1], 8)
        at = (slice(None), slice(part[0], part[0] + span))
        high, low = split_bf16(read(at).reshape(classes * span, 2 * length))
        result = jnp.dot(high, low_ref[...], preferred_element_type=F32)
        result = result + jnp.dot(low, high_ref[...], preferred_element_type=F32)
        result = result + jnp.dot(high, high_ref[...], preferred_element_type=F32)
        target[at] = result.reshape(classes, span, 2 * length)

    def plain(at):
        return stage[at]

    def product(first, second, conjugate):
        def read(at):
            a_re, a_im = first[at][:, :, :length], first[at][:, :, length:]
            b_re, b_im = second[at][:, :, :length], second[at][:, :, length:]
            if conjugate:
                real, minus = a_re * b_re + a_im * b_im, a_im * b_re - a_re * b_im
            else:
                real, minus = a_re * b_re - a_im * b_im, -(a_re * b_im + a_im * b_re)
            return jnp.concatenate((real, minus), axis=2)

        return read

    def over_rows(body, part):
        first = part[0] // group_rows

        @pl.loop(first, first + part[1] // group_rows)
        def _(r):
            body(pl.ds(pl.multiple_of(r * group_rows, group_rows), group_rows))

    def stage_store(at):
        def store(q, real, imag):
            stage[q, at, :length] = real
            stage[q, at, length:] = imag

        return store

    def tap_rows(at):
        return taps_ref[me, at, :]

    def delayed(parts, a, j):
        if j == 0:
            return parts[a]
        before = jnp.zeros_like(parts[a][:, :128]) if a == 0 else parts[a - 1][:, length - 128 :]
        joined = jnp.concatenate((before, parts[a]), axis=1)
        return pltpu.roll(joined, j, 1)[:, 128:]

    def advanced(parts, a, j):
        if j == 0:
            return parts[a]
        after = jnp.zeros_like(parts[a][:, :128]) if a == devices - 1 else parts[a + 1][:, :128]
        joined = jnp.concatenate((parts[a], after), axis=1)
        return pltpu.roll(joined, length + 128 - j, 1)[:, :length]

    w_copy.wait()

    @pl.loop(0, groups)
    def _(g):
        turned = w_buf[g].T
        high, low = split_bf16(turned)
        wt_hi[g] = high
        wt_lo[g] = low

    cot_copy.wait()
    for copy in table_copies:
        copy.wait()

    channels = devices * rows
    table = jnp.concatenate(
        (taps_buf[...], skip_buf[...], jnp.zeros((128 - taps - 1, channels), F32)), axis=0
    )
    table = table.T
    for d in range(devices):
        taps_ref[d] = table[d * rows : (d + 1) * rows, :]

    def mix_add(block, h, first):
        high, low = split_bf16(cot_all[block, :, h * half_len : (h + 1) * half_len])
        result = jnp.dot(wt_lo[block], high, preferred_element_type=F32)
        result = result + jnp.dot(wt_hi[block], low, preferred_element_type=F32)
        result = result + jnp.dot(wt_hi[block], high, preferred_element_type=F32)
        at = (slice(None), slice(h * half_len, (h + 1) * half_len))
        mix[at] = result if first else mix[at] + result

    def mix_step(step, h):
        for up in (True, False):
            @pl.when(arrives(step, up))
            def _():
                mix_add(chan - step if up else chan + step, h, False)

    for h in range(halves):
        mix_add(chan, h, True)

    def conv_rows(at):
        tap = tap_rows(at)
        parts = [sig_buf[a, at, :] for a in range(devices)]
        conv = []
        for a in range(devices):
            total = tap[:, :1] * parts[a]
            for j in range(1, taps):
                total = total + tap[:, j : j + 1] * delayed(parts, a, j)
            conv_buf[a, at, :] = total
            conv.append(total)
        forward_blocks(conv, twiddle, stage_store(at))

    def forward_rows(source):
        def body(at):
            forward_blocks(
                [source[a, at, :] for a in range(devices)], twiddle, stage_store(at)
            )

        return body

    def resp_rows(at):
        skip = tap_rows(at)[:, taps : taps + 1]
        conv = inverse_blocks(devices, length, twiddle, lambda q: work[q, at, :])
        for a in range(devices):
            resp_send[a, at, :] = conv[a] + skip * conv_buf[a, at, :]

    for i, part in enumerate(early):
        sig_moves[i][1]()
        over_rows(conv_rows, part)
        dft(plain, val_spec, part)
        fil_moves[i][1]()
        over_rows(forward_rows(fil_buf), part)
        dft(plain, fil_spec, part)
        if groups > 1 and i == 0:
            line_arrive(1, 0)
        dft(product(fil_spec, val_spec, False), work, part)
        over_rows(resp_rows, part)
        resp_moves[i][0]()
        if groups > 1 and i == 0:
            for h in range(1, halves):
                line_arrive(1, h)
    if groups > 1:
        for h in range(halves):
            mix_step(1, h)

    gate_copy.wait()
    for h in range(halves):
        for step in range(2, groups):
            line_arrive(step, h)
            mix_step(step, h)
        here = slice(h * half_len, (h + 1) * half_len)
        for d in range(devices):
            grad_send[d, :, here] = mix[d * rows : (d + 1) * rows, here] * gate_buf[d, :, here]
        for move in grad_moves[h]:
            move[0]()

    for move in resp_moves:
        move[1]()
    for d in range(devices):
        gate_buf[d] = mix[d * rows : (d + 1) * rows, :] * resp_buf[d]
    gate_store = pltpu.make_async_copy(gate_buf, gate_out, load_sem.at[1])
    gate_store.start()

    def filter_rows(at):
        parts = inverse_blocks(devices, length, twiddle, lambda q: work[q, at, :])
        for a in range(devices):
            gfil_send[a, at, :] = parts[a]

    def value_rows(at):
        tap = tap_rows(at)
        skip = tap[:, taps : taps + 1]
        value = inverse_blocks(devices, length, twiddle, lambda q: work[q, at, :])
        grad = [grad_buf[a, at, :] for a in range(devices)]
        value = [value[a] + skip * grad[a] for a in range(devices)]
        sums = [None] * taps
        for a in range(devices):
            signal = sig_buf[a, at, :]
            total = None
            for j in range(taps):
                ahead = advanced(value, a, j)
                term, part_sum = tap[:, j : j + 1] * ahead, ahead * signal
                total = term if total is None else total + term
                sums[j] = part_sum if sums[j] is None else sums[j] + part_sum
            gsig_send[a, at, :] = total
        skip_sum = grad[0] * conv_buf[0, at, :]
        for a in range(1, devices):
            skip_sum = skip_sum + grad[a] * conv_buf[a, at, :]
        lane = lax.broadcasted_iota(jnp.int32, (group_rows, 128), 1)
        placed = jnp.zeros((group_rows, 128), F32)
        for j, each in enumerate(sums + [skip_sum]):
            total = jnp.sum(each, axis=1, keepdims=True) * np.float32(scale)
            placed = jnp.where(lane == j, total, placed)
        small_buf[at, :] = placed

    small_buf[...] = jnp.zeros_like(small_buf)
    for i, part in enumerate(late):
        for h in range(halves):
            grad_moves[h][i][1]()
        over_rows(forward_rows(grad_buf), part)
        dft(plain, grad_spec, part)
        dft(product(val_spec, grad_spec, True), work, part)
        over_rows(filter_rows, part)
        gfil_moves[i][0]()
        dft(product(fil_spec, grad_spec, True), work, part)
        over_rows(value_rows, part)
        if i == len(late) - 1:
            small_send[...] = small_buf[...].T[:8, :]
            small_start()
        gsig_moves[i][0]()

    for step in range(groups):
        for up in (True, False):
            @pl.when(sends(step, up))
            def _():
                for h in range(halves):
                    hop(step, h, up).wait_send()

    small_arrive()
    per_tile = 128 // rows
    for tile in range(-(-channels // 128)):
        total = None
        for i in range(min(per_tile, devices - tile * per_tile)):
            each = small_land[tile * per_tile + i]
            each = each if i == 0 else pltpu.roll(each, i * rows, 1)
            total = each if total is None else total + each
        width = min(128, channels - tile * 128)
        small_out[:, tile * 128 : tile * 128 + width] = total[:, :width]
    gate_store.wait()
    for sent in moves:
        sent()
    for move in gfil_moves + gsig_moves:
        move[1]()


def handed_on(small_in, *refs):
    count = (len(refs) - 4) // 2
    arrays, results = refs[:count], refs[count : 2 * count]
    taps_out, skip_out, held, sems = refs[2 * count :]
    loads = [
        pltpu.make_async_copy(arrays[i], held.at[i], sems.at[0, i]) for i in range(count)
    ]
    stores = [
        pltpu.make_async_copy(held.at[i], results[i], sems.at[1, i]) for i in range(count)
    ]
    for load in loads:
        load.start()
    taps = taps_out.shape[0]
    taps_out[...] = small_in[:taps, :]
    skip_out[...] = small_in[taps : taps + 1, :]
    for load, store in zip(loads, stores):
        load.wait()
        store.start()
    for store in stores:
        store.wait()


def per_device(signal, gate_in, filter_raw, short_kernel, skip_gain, out_weight, cotangent):
    channels, length = signal.shape
    taps = short_kernel.shape[1]
    devices, groups = lax.axis_size("ctx"), lax.axis_size("chan")
    rows = channels // devices
    rows_pad = max(rows, 8)
    halves = 2
    scale = 1.0 / math.sqrt(length * devices)
    twiddle, high, low = tables(devices, length, scale)
    shape = (devices, rows, length)
    out_rows = cotangent.shape[0]
    early = [(0, rows // 2), (rows // 2, rows // 2)] if rows % 16 == 0 else [(0, rows)]
    late = [(0, rows // 4), (rows // 4, rows // 4), (rows // 2, rows // 2)] if rows % 32 == 0 else [(0, rows)]
    spec_shape = (devices + 1, rows_pad, 2 * length)
    dims = (devices, groups, rows, length, taps, halves, early, late, scale)
    moves = 3 * len(early) + (halves + 2) * len(late) + 1

    def vmem(*size, dtype=F32):
        return pltpu.VMEM(size, dtype)

    in_vmem, anywhere = pl.BlockSpec(memory_space=pltpu.VMEM), pl.BlockSpec(memory_space=pl.ANY)
    block = jax.ShapeDtypeStruct(shape, F32)
    grad_gate, grad_signal, grad_filter, small = pl.pallas_call(
        functools.partial(kernel, dims),
        out_shape=(block, block, block, jax.ShapeDtypeStruct((8, channels), F32)),
        in_specs=[anywhere] * 10,
        out_specs=(anywhere, anywhere, anywhere, in_vmem),
        scratch_shapes=[
            vmem(groups, out_rows, channels),
            vmem(groups, channels, out_rows, dtype=BF16),
            vmem(groups, channels, out_rows, dtype=BF16),
            vmem(groups, out_rows, length),
            vmem(channels, length),
            *[vmem(*shape) for _ in range(10)],
            vmem(devices, rows, 128),
            vmem(128, 128),
            vmem(8, 128),
            vmem(devices, 8, 128),
            *[vmem(*spec_shape) for _ in range(5)],
            vmem(*twiddle.shape),
            vmem(*high.shape, dtype=BF16),
            vmem(*low.shape, dtype=BF16),
            vmem(taps, channels),
            vmem(1, channels),
            pltpu.SemaphoreType.DMA((halves, groups)),
            pltpu.SemaphoreType.DMA((halves, groups)),
            pltpu.SemaphoreType.DMA((halves, groups)),
            pltpu.SemaphoreType.DMA((moves, devices)),
            pltpu.SemaphoreType.DMA((moves, devices)),
            pltpu.SemaphoreType.DMA((moves,)),
            pltpu.SemaphoreType.DMA((8,)),
        ],
        compiler_params=pltpu.CompilerParams(
            collective_id=0, has_side_effects=True, vmem_limit_bytes=56 * 2**20
        ),
    )(
        signal.reshape(shape),
        gate_in.reshape(shape),
        filter_raw.reshape(shape),
        short_kernel.T,
        skip_gain[None, :],
        out_weight.reshape(groups, out_rows, channels),
        cotangent,
        jnp.asarray(twiddle),
        jnp.asarray(high),
        jnp.asarray(low),
    )
    grad_gate, grad_signal, grad_filter, grad_kernel, grad_skip = pl.pallas_call(
        handed_on,
        out_shape=(block,) * 3
        + (
            jax.ShapeDtypeStruct((taps, channels), F32),
            jax.ShapeDtypeStruct((1, channels), F32),
        ),
        in_specs=[in_vmem] + [anywhere] * 3,
        out_specs=(anywhere,) * 3 + (in_vmem,) * 2,
        scratch_shapes=[vmem(3, *shape), pltpu.SemaphoreType.DMA((2, 3))],
    )(small, grad_gate, grad_signal, grad_filter)
    whole = (channels, length)
    return (
        grad_gate.reshape(whole),
        grad_signal.reshape(whole),
        grad_filter.reshape(whole),
        grad_kernel.T,
        grad_skip[0],
    )


def solution(mesh):
    placed = (
        P("chan", "ctx"),
        P("chan", "ctx"),
        P("chan", "ctx"),
        P("chan", None),
        P("chan"),
        P(None, "chan"),
        P("chan", "ctx"),
    )
    return jax.shard_map(
        per_device,
        mesh=mesh,
        in_specs=placed,
        out_specs=(
            P("chan", "ctx"),
            P("chan", "ctx"),
            P("chan", "ctx"),
            P("chan", None),
            P("chan"),
        ),
        check_vma=False,
    )
```

```python
import functools
import math

import jax
import jax.numpy as jnp
import numpy as np
from jax import lax
from jax.experimental import pallas as pl
from jax.experimental.pallas import tpu as pltpu
from jax.sharding import PartitionSpec as P

MESH = pl.DeviceIdType.MESH
F32 = jnp.float32
BF16 = jnp.bfloat16


def split_bf16(value):
    high = value.astype(BF16)
    return high, (value - high.astype(F32)).astype(BF16)


def tables(blocks, length, scale):
    total = 2 * blocks * length
    turn = np.arange(blocks + 1)[:, None] * np.arange(length)[None, :] % total
    angle = 2.0 * np.pi / total * turn
    weight = np.full((blocks + 1, 1), 2.0)
    weight[0] = weight[blocks] = 1.0
    weight = weight * (scale / total)
    twiddle = np.stack(
        (np.cos(angle), np.sin(angle), weight * np.cos(angle), weight * np.sin(angle))
    ).astype(np.float32)
    turn = np.arange(length)[:, None] * np.arange(length)[None, :] % length
    angle = 2.0 * np.pi / length * turn
    cosine, sine = np.cos(angle), np.sin(angle)
    matrix = np.block([[cosine, -sine], [sine, cosine]]).astype(np.float32)
    high = matrix.astype(jnp.bfloat16)
    low = (matrix - high.astype(np.float32)).astype(jnp.bfloat16)
    return twiddle, high, low


def weighted_sum(terms):
    total = None
    for factor, value in terms:
        if abs(factor) < 1e-12:
            continue
        if abs(factor - 1.0) < 1e-12:
            part = value
        elif abs(factor + 1.0) < 1e-12:
            part = -value
        else:
            part = np.float32(factor) * value
        total = part if total is None else total + part
    return total


def forward_blocks(parts, twiddle, store):
    blocks = len(parts)

    def put(q, real, imag):
        cosine, sine = twiddle[0, q : q + 1, :], twiddle[1, q : q + 1, :]
        if imag is None:
            store(q, real * cosine, -real * sine)
        else:
            store(q, real * cosine + imag * sine, imag * cosine - real * sine)

    for q in range(blocks // 2 + 1):
        def gather(first, trig, sign):
            return weighted_sum(
                [(sign * trig(math.pi * a * q / blocks), parts[a]) for a in range(first, blocks, 2)]
            )

        even_re, even_im = gather(0, math.cos, 1.0), gather(0, math.sin, -1.0)
        odd_re, odd_im = gather(1, math.cos, 1.0), gather(1, math.sin, -1.0)

        def add(a, b, sign_a, sign_b):
            return weighted_sum([(s, v) for s, v in ((sign_a, a), (sign_b, b)) if v is not None])

        put(q, add(even_re, odd_re, 1.0, 1.0), add(even_im, odd_im, 1.0, 1.0))
        if q != blocks - q:
            put(blocks - q, add(even_re, odd_re, 1.0, -1.0), add(even_im, odd_im, -1.0, 1.0))


def inverse_blocks(blocks, length, twiddle, load):
    def real_imag(q):
        pair = load(q)
        real, minus = pair[:, :length], pair[:, length:]
        cosine, sine = twiddle[2, q : q + 1, :], twiddle[3, q : q + 1, :]
        return real * cosine + minus * sine, real * sine - minus * cosine

    first, last = real_imag(0)[0], real_imag(blocks)[0]
    half_re, half_im = real_imag(blocks // 2)
    pairs = []
    for q in range(1, blocks // 2):
        (re_a, im_a), (re_b, im_b) = real_imag(q), real_imag(blocks - q)
        pairs.append((re_a + re_b, im_a - im_b, re_a - re_b, im_a + im_b))
    result = []
    for a in range(blocks):
        odd = a % 2
        terms = [(1.0, first - last if odd else first + last)]
        terms.append((math.cos(math.pi * a / 2), half_re))
        terms.append((-math.sin(math.pi * a / 2), half_im))
        for q in range(1, blocks // 2):
            angle = math.pi * a * q / blocks
            terms.append((math.cos(angle), pairs[q - 1][2 * odd]))
            terms.append((-math.sin(angle), pairs[q - 1][2 * odd + 1]))
        result.append(weighted_sum(terms))
    return result


def kernel(
    dims,
    sig_in, gate_in, fil_in, taps_in, skip_in, w_in, cot_in, twiddle_in, high_in, low_in,
    gate_out, gsig_out, gfil_out, small_out,
    w_buf, wt_hi, wt_lo, cot_all, mix, gate_buf, sig_buf, fil_buf, conv_buf,
    resp_send, resp_buf, grad_send, grad_buf, gsig_send, gfil_send, taps_ref, small_buf, small_send, small_land,
    stage, fil_spec, val_spec, grad_spec, work, twiddle, high_ref, low_ref, taps_buf, skip_buf, small_all,
    up_sem, down_sem, line_sem, send_sem, recv_sem, load_sem,
):
    devices, groups, rows, length, taps, halves, early, late, scale = dims
    me, chan = lax.axis_index("ctx"), lax.axis_index("chan")
    half_len = length // halves
    group_rows = min(8, rows)
    classes = devices + 1

    barrier = pltpu.get_barrier_semaphore()

    @pl.loop(1, devices)
    def _(k):
        pl.semaphore_signal(
            barrier, inc=1, device_id={"ctx": lax.rem(me + k, devices)}, device_id_type=MESH
        )

    @pl.loop(1, groups)
    def _(k):
        pl.semaphore_signal(
            barrier, inc=1, device_id={"chan": lax.rem(chan + k, groups)}, device_id_type=MESH
        )

    w_copy = pltpu.make_async_copy(w_in, w_buf, load_sem.at[0])
    gate_copy = pltpu.make_async_copy(gate_in, gate_buf, load_sem.at[1])
    cot_copy = pltpu.make_async_copy(cot_in, cot_all.at[chan], load_sem.at[2])
    table_copies = [
        pltpu.make_async_copy(source, target, load_sem.at[3 + i])
        for i, (source, target) in enumerate(
            (
                (taps_in, taps_buf), (skip_in, skip_buf), (twiddle_in, twiddle),
                (high_in, high_ref), (low_in, low_ref),
            )
        )
    ]
    w_copy.start()
    cot_copy.start()
    for copy in table_copies:
        copy.start()
    gate_copy.start()

    pl.semaphore_wait(barrier, devices + groups - 2)

    def lanes(h):
        return pl.ds(h * half_len, half_len)

    def hop(step, h, up):
        block = chan - step if up else chan + step
        source = cot_in if step == 0 else cot_all.at[block]
        sems = up_sem if up else down_sem
        return pltpu.make_async_remote_copy(
            src_ref=source.at[:, lanes(h)],
            dst_ref=cot_all.at[block, :, lanes(h)],
            send_sem=sems.at[h, step],
            recv_sem=line_sem.at[h, block],
            device_id={"chan": chan + 1 if up else chan - 1},
            device_id_type=MESH,
        )

    def sends(step, up):
        if up:
            return jnp.logical_and(chan - step >= 0, chan + 1 < groups)
        return jnp.logical_and(chan + step < groups, chan >= 1)

    def arrives(step, up):
        return chan - step >= 0 if up else chan + step < groups

    def line_start(step, h):
        for up in (True, False):
            @pl.when(sends(step, up))
            def _():
                hop(step, h, up).start()

    def line_arrive(step, h):
        for up in (True, False):
            @pl.when(arrives(step, up))
            def _():
                block = chan - step if up else chan + step
                slot = cot_all.at[block, :, lanes(h)]
                pltpu.make_async_remote_copy(
                    src_ref=slot,
                    dst_ref=slot,
                    send_sem=up_sem.at[h, step],
                    recv_sem=line_sem.at[h, block],
                    device_id={"chan": chan - 1 if up else chan + 1},
                    device_id_type=MESH,
                ).wait_recv()

                @pl.when(sends(step, up))
                def _():
                    hop(step, h, up).start()

    moves = []

    def all_to_all(source, target, landed):
        index = len(moves)

        def start():
            @pl.loop(1, devices)
            def _(k):
                peer = lax.rem(me + k, devices)
                pltpu.make_async_remote_copy(
                    src_ref=source(peer),
                    dst_ref=target(me),
                    send_sem=send_sem.at[index],
                    recv_sem=recv_sem.at[index],
                    device_id={"ctx": peer},
                    device_id_type=MESH,
                ).start()

            pltpu.make_async_copy(source(me), target(me), recv_sem.at[index]).start()

        def arrive():
            everything = landed(devices)
            pltpu.make_async_copy(everything, everything, recv_sem.at[index]).wait()

        def sent():
            others = landed(devices - 1)
            pltpu.make_async_copy(others, others, send_sem.at[index]).wait()

        moves.append(sent)
        return start, arrive

    def by_part(source, target, part, lane=slice(None)):
        at = pl.ds(*part)
        return all_to_all(
            lambda p: source.at[p, at, lane],
            lambda p: target.at[p, at, lane],
            lambda n: target.at[pl.ds(0, n), at, lane],
        )

    sig_moves = [by_part(sig_in, sig_buf, part) for part in early]
    fil_moves = [by_part(fil_in, fil_buf, part) for part in early]
    resp_moves = [by_part(resp_send, resp_buf, part) for part in early]
    grad_moves = [
        [by_part(grad_send, grad_buf, part, lanes(h)) for part in late] for h in range(halves)
    ]
    gfil_moves = [by_part(gfil_send, gfil_out, part) for part in late]
    gsig_moves = [by_part(gsig_send, gsig_out, part) for part in late]
    small_start, small_arrive = all_to_all(
        lambda p: small_send, lambda p: small_land.at[p], lambda n: small_land.at[pl.ds(0, n)]
    )

    for h in range(halves):
        line_start(0, h)
    for sig_move, fil_move in zip(sig_moves, fil_moves):
        sig_move[0]()
        fil_move[0]()

    def dft(read, target, part):
        span = max(part[1], 8)
        at = (slice(None), slice(part[0], part[0] + span))
        high, low = split_bf16(read(at).reshape(classes * span, 2 * length))
        result = jnp.dot(high, low_ref[...], preferred_element_type=F32)
        result = result + jnp.dot(low, high_ref[...], preferred_element_type=F32)
        result = result + jnp.dot(high, high_ref[...], preferred_element_type=F32)
        target[at] = result.reshape(classes, span, 2 * length)

    def plain(at):
        return stage[at]

    def product(first, second, conjugate):
        def read(at):
            a_re, a_im = first[at][:, :, :length], first[at][:, :, length:]
            b_re, b_im = second[at][:, :, :length], second[at][:, :, length:]
            if conjugate:
                real, minus = a_re * b_re + a_im * b_im, a_im * b_re - a_re * b_im
            else:
                real, minus = a_re * b_re - a_im * b_im, -(a_re * b_im + a_im * b_re)
            return jnp.concatenate((real, minus), axis=2)

        return read

    def over_rows(body, part):
        first = part[0] // group_rows

        @pl.loop(first, first + part[1] // group_rows)
        def _(r):
            body(pl.ds(pl.multiple_of(r * group_rows, group_rows), group_rows))

    def stage_store(at):
        def store(q, real, imag):
            stage[q, at, :length] = real
            stage[q, at, length:] = imag

        return store

    def tap_rows(at):
        return taps_ref[me, at, :]

    def delayed(parts, a, j):
        if j == 0:
            return parts[a]
        before = jnp.zeros_like(parts[a][:, :128]) if a == 0 else parts[a - 1][:, length - 128 :]
        joined = jnp.concatenate((before, parts[a]), axis=1)
        return pltpu.roll(joined, j, 1)[:, 128:]

    def advanced(parts, a, j):
        if j == 0:
            return parts[a]
        after = jnp.zeros_like(parts[a][:, :128]) if a == devices - 1 else parts[a + 1][:, :128]
        joined = jnp.concatenate((parts[a], after), axis=1)
        return pltpu.roll(joined, length + 128 - j, 1)[:, :length]

    w_copy.wait()

    @pl.loop(0, groups)
    def _(g):
        turned = w_buf[g].T
        high, low = split_bf16(turned)
        wt_hi[g] = high
        wt_lo[g] = low

    cot_copy.wait()
    for copy in table_copies:
        copy.wait()

    channels = devices * rows
    table = jnp.concatenate(
        (taps_buf[...], skip_buf[...], jnp.zeros((128 - taps - 1, channels), F32)), axis=0
    )
    table = table.T
    for d in range(devices):
        taps_ref[d] = table[d * rows : (d + 1) * rows, :]

    def mix_add(block, h, first):
        high, low = split_bf16(cot_all[block, :, h * half_len : (h + 1) * half_len])
        result = jnp.dot(wt_lo[block], high, preferred_element_type=F32)
        result = result + jnp.dot(wt_hi[block], low, preferred_element_type=F32)
        result = result + jnp.dot(wt_hi[block], high, preferred_element_type=F32)
        at = (slice(None), slice(h * half_len, (h + 1) * half_len))
        mix[at] = result if first else mix[at] + result

    def mix_step(step, h):
        for up in (True, False):
            @pl.when(arrives(step, up))
            def _():
                mix_add(chan - step if up else chan + step, h, False)

    for h in range(halves):
        mix_add(chan, h, True)

    def conv_rows(at):
        tap = tap_rows(at)
        parts = [sig_buf[a, at, :] for a in range(devices)]
        conv = []
        for a in range(devices):
            total = tap[:, :1] * parts[a]
            for j in range(1, taps):
                total = total + tap[:, j : j + 1] * delayed(parts, a, j)
            conv_buf[a, at, :] = total
            conv.append(total)
        forward_blocks(conv, twiddle, stage_store(at))

    def forward_rows(source):
        def body(at):
            forward_blocks(
                [source[a, at, :] for a in range(devices)], twiddle, stage_store(at)
            )

        return body

    def resp_rows(at):
        skip = tap_rows(at)[:, taps : taps + 1]
        conv = inverse_blocks(devices, length, twiddle, lambda q: work[q, at, :])
        for a in range(devices):
            resp_send[a, at, :] = conv[a] + skip * conv_buf[a, at, :]

    for i, part in enumerate(early):
        sig_moves[i][1]()
        over_rows(conv_rows, part)
        dft(plain, val_spec, part)
        fil_moves[i][1]()
        over_rows(forward_rows(fil_buf), part)
        dft(plain, fil_spec, part)
        if groups > 1 and i == 0:
            line_arrive(1, 0)
        dft(product(fil_spec, val_spec, False), work, part)
        over_rows(resp_rows, part)
        resp_moves[i][0]()
        if groups > 1 and i == 0:
            for h in range(1, halves):
                line_arrive(1, h)
    if groups > 1:
        for h in range(halves):
            mix_step(1, h)

    gate_copy.wait()
    for h in range(halves):
        for step in range(2, groups):
            line_arrive(step, h)
            mix_step(step, h)
        here = slice(h * half_len, (h + 1) * half_len)
        for d in range(devices):
            grad_send[d, :, here] = mix[d * rows : (d + 1) * rows, here] * gate_buf[d, :, here]
        for move in grad_moves[h]:
            move[0]()

    for move in resp_moves:
        move[1]()
    for d in range(devices):
        gate_buf[d] = mix[d * rows : (d + 1) * rows, :] * resp_buf[d]
    gate_store = pltpu.make_async_copy(gate_buf, gate_out, load_sem.at[1])
    gate_store.start()

    def filter_rows(at):
        parts = inverse_blocks(devices, length, twiddle, lambda q: work[q, at, :])
        for a in range(devices):
            gfil_send[a, at, :] = parts[a]

    def value_rows(at):
        tap = tap_rows(at)
        skip = tap[:, taps : taps + 1]
        value = inverse_blocks(devices, length, twiddle, lambda q: work[q, at, :])
        grad = [grad_buf[a, at, :] for a in range(devices)]
        value = [value[a] + skip * grad[a] for a in range(devices)]
        sums = [None] * taps
        for a in range(devices):
            signal = sig_buf[a, at, :]
            total = None
            for j in range(taps):
                ahead = advanced(value, a, j)
                term, part_sum = tap[:, j : j + 1] * ahead, ahead * signal
                total = term if total is None else total + term
                sums[j] = part_sum if sums[j] is None else sums[j] + part_sum
            gsig_send[a, at, :] = total
        skip_sum = grad[0] * conv_buf[0, at, :]
        for a in range(1, devices):
            skip_sum = skip_sum + grad[a] * conv_buf[a, at, :]
        lane = lax.broadcasted_iota(jnp.int32, (group_rows, 128), 1)
        placed = jnp.zeros((group_rows, 128), F32)
        for j, each in enumerate(sums + [skip_sum]):
            total = jnp.sum(each, axis=1, keepdims=True) * np.float32(scale)
            placed = jnp.where(lane == j, total, placed)
        small_buf[at, :] = placed

    small_buf[...] = jnp.zeros_like(small_buf)
    for i, part in enumerate(late):
        for h in range(halves):
            grad_moves[h][i][1]()
        over_rows(forward_rows(grad_buf), part)
        dft(plain, grad_spec, part)
        dft(product(val_spec, grad_spec, True), work, part)
        over_rows(filter_rows, part)
        gfil_moves[i][0]()
        dft(product(fil_spec, grad_spec, True), work, part)
        over_rows(value_rows, part)
        if i == len(late) - 1:
            small_send[...] = small_buf[...].T[:8, :]
            small_start()
        gsig_moves[i][0]()

    for step in range(groups):
        for up in (True, False):
            @pl.when(sends(step, up))
            def _():
                for h in range(halves):
                    hop(step, h, up).wait_send()

    small_arrive()
    per_tile = 128 // rows
    for tile in range(-(-channels // 128)):
        total = None
        for i in range(min(per_tile, devices - tile * per_tile)):
            each = small_land[tile * per_tile + i]
            each = each if i == 0 else pltpu.roll(each, i * rows, 1)
            total = each if total is None else total + each
        width = min(128, channels - tile * 128)
        small_all[:, tile * 128 : tile * 128 + width] = total[:, :width]
    small_store = pltpu.make_async_copy(small_all, small_out, load_sem.at[2])
    small_store.start()
    gate_store.wait()
    small_store.wait()
    for sent in moves:
        sent()
    for move in gfil_moves + gsig_moves:
        move[1]()


def handed_on(small_in, *refs):
    count = (len(refs) - 4) // 2
    arrays, results = refs[:count], refs[count : 2 * count]
    taps_out, skip_out, held, sems = refs[2 * count :]
    loads = [
        pltpu.make_async_copy(arrays[i], held.at[i], sems.at[0, i]) for i in range(count)
    ]
    stores = [
        pltpu.make_async_copy(held.at[i], results[i], sems.at[1, i]) for i in range(count)
    ]
    for load in loads:
        load.start()
    taps = taps_out.shape[0]
    taps_out[...] = small_in[:taps, :]
    skip_out[...] = small_in[taps : taps + 1, :]
    for load, store in zip(loads, stores):
        load.wait()
        store.start()
    for store in stores:
        store.wait()


def per_device(signal, gate_in, filter_raw, short_kernel, skip_gain, out_weight, cotangent):
    channels, length = signal.shape
    taps = short_kernel.shape[1]
    devices, groups = lax.axis_size("ctx"), lax.axis_size("chan")
    rows = channels // devices
    rows_pad = max(rows, 8)
    halves = 2
    scale = 1.0 / math.sqrt(length * devices)
    twiddle, high, low = tables(devices, length, scale)
    shape = (devices, rows, length)
    out_rows = cotangent.shape[0]
    early = [(0, rows // 2), (rows // 2, rows // 2)] if rows % 16 == 0 else [(0, rows)]
    late = [(0, rows // 4), (rows // 4, rows // 4), (rows // 2, rows // 2)] if rows % 32 == 0 else [(0, rows)]
    spec_shape = (devices + 1, rows_pad, 2 * length)
    dims = (devices, groups, rows, length, taps, halves, early, late, scale)
    moves = 3 * len(early) + (halves + 2) * len(late) + 1

    def vmem(*size, dtype=F32):
        return pltpu.VMEM(size, dtype)

    in_vmem, anywhere = pl.BlockSpec(memory_space=pltpu.VMEM), pl.BlockSpec(memory_space=pl.ANY)
    block = jax.ShapeDtypeStruct(shape, F32)
    grad_gate, grad_signal, grad_filter, small = pl.pallas_call(
        functools.partial(kernel, dims),
        out_shape=(block, block, block, jax.ShapeDtypeStruct((8, channels), F32)),
        in_specs=[anywhere] * 10,
        out_specs=(anywhere,) * 4,
        scratch_shapes=[
            vmem(groups, out_rows, channels),
            vmem(groups, channels, out_rows, dtype=BF16),
            vmem(groups, channels, out_rows, dtype=BF16),
            vmem(groups, out_rows, length),
            vmem(channels, length),
            *[vmem(*shape) for _ in range(10)],
            vmem(devices, rows, 128),
            vmem(128, 128),
            vmem(8, 128),
            vmem(devices, 8, 128),
            *[vmem(*spec_shape) for _ in range(5)],
            vmem(*twiddle.shape),
            vmem(*high.shape, dtype=BF16),
            vmem(*low.shape, dtype=BF16),
            vmem(taps, channels),
            vmem(1, channels),
            vmem(8, channels),
            pltpu.SemaphoreType.DMA((halves, groups)),
            pltpu.SemaphoreType.DMA((halves, groups)),
            pltpu.SemaphoreType.DMA((halves, groups)),
            pltpu.SemaphoreType.DMA((moves,)),
            pltpu.SemaphoreType.DMA((moves,)),
            pltpu.SemaphoreType.DMA((8,)),
        ],
        compiler_params=pltpu.CompilerParams(
            collective_id=0, has_side_effects=True, vmem_limit_bytes=56 * 2**20
        ),
    )(
        signal.reshape(shape),
        gate_in.reshape(shape),
        filter_raw.reshape(shape),
        short_kernel.T,
        skip_gain[None, :],
        out_weight.reshape(groups, out_rows, channels),
        cotangent,
        jnp.asarray(twiddle),
        jnp.asarray(high),
        jnp.asarray(low),
    )
    grad_gate, grad_signal, grad_filter, grad_kernel, grad_skip = pl.pallas_call(
        handed_on,
        out_shape=(block,) * 3
        + (
            jax.ShapeDtypeStruct((taps, channels), F32),
            jax.ShapeDtypeStruct((1, channels), F32),
        ),
        in_specs=[in_vmem] + [anywhere] * 3,
        out_specs=(anywhere,) * 3 + (in_vmem,) * 2,
        scratch_shapes=[vmem(3, *shape), pltpu.SemaphoreType.DMA((2, 3))],
    )(small, grad_gate, grad_signal, grad_filter)
    whole = (channels, length)
    return (
        grad_gate.reshape(whole),
        grad_signal.reshape(whole),
        grad_filter.reshape(whole),
        grad_kernel.T,
        grad_skip[0],
    )


def solution(mesh):
    placed = (
        P("chan", "ctx"),
        P("chan", "ctx"),
        P("chan", "ctx"),
        P("chan", None),
        P("chan"),
        P(None, "chan"),
        P("chan", "ctx"),
    )
    return jax.shard_map(
        per_device,
        mesh=mesh,
        in_specs=placed,
        out_specs=(
            P("chan", "ctx"),
            P("chan", "ctx"),
            P("chan", "ctx"),
            P("chan", None),
            P("chan"),
        ),
        check_vma=False,
    )
```

```python
import functools
import math

import jax
import jax.numpy as jnp
import numpy as np
from jax import lax
from jax.experimental import pallas as pl
from jax.experimental.pallas import tpu as pltpu
from jax.sharding import PartitionSpec as P

MESH = pl.DeviceIdType.MESH
F32 = jnp.float32
BF16 = jnp.bfloat16


def split_bf16(value):
    high = value.astype(BF16)
    return high, (value - high.astype(F32)).astype(BF16)


def tables(blocks, length, scale):
    total = 2 * blocks * length
    turn = np.arange(blocks + 1)[:, None] * np.arange(length)[None, :] % total
    angle = 2.0 * np.pi / total * turn
    weight = np.full((blocks + 1, 1), 2.0)
    weight[0] = weight[blocks] = 1.0
    weight = weight * (scale / total)
    twiddle = np.stack(
        (np.cos(angle), np.sin(angle), weight * np.cos(angle), weight * np.sin(angle))
    ).astype(np.float32)
    turn = np.arange(length)[:, None] * np.arange(length)[None, :] % length
    angle = 2.0 * np.pi / length * turn
    cosine, sine = np.cos(angle), np.sin(angle)
    matrix = np.block([[cosine, -sine], [sine, cosine]]).astype(np.float32)
    high = matrix.astype(jnp.bfloat16)
    low = (matrix - high.astype(np.float32)).astype(jnp.bfloat16)
    return twiddle, high, low


def weighted_sum(terms):
    total = None
    for factor, value in terms:
        if abs(factor) < 1e-12:
            continue
        if abs(factor - 1.0) < 1e-12:
            part = value
        elif abs(factor + 1.0) < 1e-12:
            part = -value
        else:
            part = np.float32(factor) * value
        total = part if total is None else total + part
    return total


def forward_blocks(parts, twiddle, store):
    blocks = len(parts)

    def put(q, real, imag):
        cosine, sine = twiddle[0, q : q + 1, :], twiddle[1, q : q + 1, :]
        if imag is None:
            store(q, real * cosine, -real * sine)
        else:
            store(q, real * cosine + imag * sine, imag * cosine - real * sine)

    for q in range(blocks // 2 + 1):
        def gather(first, trig, sign):
            return weighted_sum(
                [(sign * trig(math.pi * a * q / blocks), parts[a]) for a in range(first, blocks, 2)]
            )

        even_re, even_im = gather(0, math.cos, 1.0), gather(0, math.sin, -1.0)
        odd_re, odd_im = gather(1, math.cos, 1.0), gather(1, math.sin, -1.0)

        def add(a, b, sign_a, sign_b):
            return weighted_sum([(s, v) for s, v in ((sign_a, a), (sign_b, b)) if v is not None])

        put(q, add(even_re, odd_re, 1.0, 1.0), add(even_im, odd_im, 1.0, 1.0))
        if q != blocks - q:
            put(blocks - q, add(even_re, odd_re, 1.0, -1.0), add(even_im, odd_im, -1.0, 1.0))


def inverse_blocks(blocks, length, twiddle, load):
    def real_imag(q):
        pair = load(q)
        real, minus = pair[:, :length], pair[:, length:]
        cosine, sine = twiddle[2, q : q + 1, :], twiddle[3, q : q + 1, :]
        return real * cosine + minus * sine, real * sine - minus * cosine

    first, last = real_imag(0)[0], real_imag(blocks)[0]
    half_re, half_im = real_imag(blocks // 2)
    pairs = []
    for q in range(1, blocks // 2):
        (re_a, im_a), (re_b, im_b) = real_imag(q), real_imag(blocks - q)
        pairs.append((re_a + re_b, im_a - im_b, re_a - re_b, im_a + im_b))
    result = []
    for a in range(blocks):
        odd = a % 2
        terms = [(1.0, first - last if odd else first + last)]
        terms.append((math.cos(math.pi * a / 2), half_re))
        terms.append((-math.sin(math.pi * a / 2), half_im))
        for q in range(1, blocks // 2):
            angle = math.pi * a * q / blocks
            terms.append((math.cos(angle), pairs[q - 1][2 * odd]))
            terms.append((-math.sin(angle), pairs[q - 1][2 * odd + 1]))
        result.append(weighted_sum(terms))
    return result


def kernel(
    dims,
    sig_in, gate_in, fil_in, taps_in, skip_in, w_in, cot_in, twiddle_in, high_in, low_in,
    gate_out, gsig_out, gfil_out, tap_out, skip_out,
    w_buf, wt_hi, wt_lo, cot_all, mix, gate_buf, sig_buf, fil_buf, conv_buf,
    resp_send, resp_buf, grad_send, grad_buf, gsig_send, gfil_send, taps_ref, small_buf, small_send, small_land,
    stage, fil_spec, val_spec, grad_spec, work, twiddle, high_ref, low_ref, taps_buf, skip_buf,
    up_sem, down_sem, line_sem, send_sem, recv_sem, load_sem,
):
    devices, groups, rows, length, taps, halves, early, late, scale = dims
    me, chan = lax.axis_index("ctx"), lax.axis_index("chan")
    half_len = length // halves
    group_rows = min(8, rows)
    classes = devices + 1

    barrier = pltpu.get_barrier_semaphore()

    @pl.loop(1, devices)
    def _(k):
        pl.semaphore_signal(
            barrier, inc=1, device_id={"ctx": lax.rem(me + k, devices)}, device_id_type=MESH
        )

    for inside, other in ((chan + 1 < groups, chan + 1), (chan >= 1, chan - 1)):
        @pl.when(inside)
        def _():
            pl.semaphore_signal(barrier, inc=1, device_id={"chan": other}, device_id_type=MESH)

    w_copy = pltpu.make_async_copy(w_in, w_buf, load_sem.at[0])
    gate_copy = pltpu.make_async_copy(gate_in, gate_buf, load_sem.at[1])
    cot_copy = pltpu.make_async_copy(cot_in, cot_all.at[chan], load_sem.at[2])
    table_copies = [
        pltpu.make_async_copy(source, target, load_sem.at[3 + i])
        for i, (source, target) in enumerate(
            (
                (taps_in, taps_buf), (skip_in, skip_buf), (twiddle_in, twiddle),
                (high_in, high_ref), (low_in, low_ref),
            )
        )
    ]
    w_copy.start()
    cot_copy.start()
    for copy in table_copies:
        copy.start()
    gate_copy.start()

    beside = (chan + 1 < groups).astype(jnp.int32) + (chan >= 1).astype(jnp.int32)
    pl.semaphore_wait(barrier, devices - 1 + beside)

    def lanes(h):
        return pl.ds(h * half_len, half_len)

    def hop(step, h, up):
        block = chan - step if up else chan + step
        source = cot_in if step == 0 else cot_all.at[block]
        sems = up_sem if up else down_sem
        return pltpu.make_async_remote_copy(
            src_ref=source.at[:, lanes(h)],
            dst_ref=cot_all.at[block, :, lanes(h)],
            send_sem=sems.at[h, step],
            recv_sem=line_sem.at[h, block],
            device_id={"chan": chan + 1 if up else chan - 1},
            device_id_type=MESH,
        )

    def sends(step, up):
        if up:
            return jnp.logical_and(chan - step >= 0, chan + 1 < groups)
        return jnp.logical_and(chan + step < groups, chan >= 1)

    def arrives(step, up):
        return chan - step >= 0 if up else chan + step < groups

    def line_start(step, h):
        for up in (True, False):
            @pl.when(sends(step, up))
            def _():
                hop(step, h, up).start()

    def line_arrive(step, h):
        for up in (True, False):
            @pl.when(arrives(step, up))
            def _():
                block = chan - step if up else chan + step
                slot = cot_all.at[block, :, lanes(h)]
                pltpu.make_async_remote_copy(
                    src_ref=slot,
                    dst_ref=slot,
                    send_sem=up_sem.at[h, step],
                    recv_sem=line_sem.at[h, block],
                    device_id={"chan": chan - 1 if up else chan + 1},
                    device_id_type=MESH,
                ).wait_recv()

                @pl.when(sends(step, up))
                def _():
                    hop(step, h, up).start()

    moves = []

    def all_to_all(source, target, landed):
        index = len(moves)

        def start():
            @pl.loop(1, devices)
            def _(k):
                peer = lax.rem(me + k, devices)
                pltpu.make_async_remote_copy(
                    src_ref=source(peer),
                    dst_ref=target(me),
                    send_sem=send_sem.at[index],
                    recv_sem=recv_sem.at[index],
                    device_id={"ctx": peer},
                    device_id_type=MESH,
                ).start()

            pltpu.make_async_copy(source(me), target(me), recv_sem.at[index]).start()

        def arrive():
            everything = landed(devices)
            pltpu.make_async_copy(everything, everything, recv_sem.at[index]).wait()

        def sent():
            others = landed(devices - 1)
            pltpu.make_async_copy(others, others, send_sem.at[index]).wait()

        moves.append(sent)
        return start, arrive

    def by_part(source, target, part, lane=slice(None)):
        at = pl.ds(*part)
        return all_to_all(
            lambda p: source.at[p, at, lane],
            lambda p: target.at[p, at, lane],
            lambda n: target.at[pl.ds(0, n), at, lane],
        )

    sig_moves = [by_part(sig_in, sig_buf, part) for part in early]
    fil_moves = [by_part(fil_in, fil_buf, part) for part in early]
    resp_moves = [by_part(resp_send, resp_buf, part) for part in early]
    grad_moves = [
        [by_part(grad_send, grad_buf, part, lanes(h)) for part in late] for h in range(halves)
    ]
    gfil_moves = [by_part(gfil_send, gfil_out, part) for part in late]
    gsig_moves = [by_part(gsig_send, gsig_out, part) for part in late]
    small_start, small_arrive = all_to_all(
        lambda p: small_send, lambda p: small_land.at[p], lambda n: small_land.at[pl.ds(0, n)]
    )

    for h in range(halves):
        line_start(0, h)
    for sig_move, fil_move in zip(sig_moves, fil_moves):
        sig_move[0]()
        fil_move[0]()

    def dft(read, target, part):
        span = max(part[1], 8)
        at = (slice(None), slice(part[0], part[0] + span))
        high, low = split_bf16(read(at).reshape(classes * span, 2 * length))
        result = jnp.dot(high, low_ref[...], preferred_element_type=F32)
        result = result + jnp.dot(low, high_ref[...], preferred_element_type=F32)
        result = result + jnp.dot(high, high_ref[...], preferred_element_type=F32)
        target[at] = result.reshape(classes, span, 2 * length)

    def plain(at):
        return stage[at]

    def product(first, second, conjugate):
        def read(at):
            a_re, a_im = first[at][:, :, :length], first[at][:, :, length:]
            b_re, b_im = second[at][:, :, :length], second[at][:, :, length:]
            if conjugate:
                real, minus = a_re * b_re + a_im * b_im, a_im * b_re - a_re * b_im
            else:
                real, minus = a_re * b_re - a_im * b_im, -(a_re * b_im + a_im * b_re)
            return jnp.concatenate((real, minus), axis=2)

        return read

    def over_rows(body, part):
        first = part[0] // group_rows

        @pl.loop(first, first + part[1] // group_rows)
        def _(r):
            body(pl.ds(pl.multiple_of(r * group_rows, group_rows), group_rows))

    def stage_store(at):
        def store(q, real, imag):
            stage[q, at, :length] = real
            stage[q, at, length:] = imag

        return store

    def tap_rows(at):
        return taps_ref[me, at, :]

    def delayed(parts, a, j):
        if j == 0:
            return parts[a]
        before = jnp.zeros_like(parts[a][:, :128]) if a == 0 else parts[a - 1][:, length - 128 :]
        joined = jnp.concatenate((before, parts[a]), axis=1)
        return pltpu.roll(joined, j, 1)[:, 128:]

    def advanced(parts, a, j):
        if j == 0:
            return parts[a]
        after = jnp.zeros_like(parts[a][:, :128]) if a == devices - 1 else parts[a + 1][:, :128]
        joined = jnp.concatenate((parts[a], after), axis=1)
        return pltpu.roll(joined, length + 128 - j, 1)[:, :length]

    w_copy.wait()

    @pl.loop(0, groups)
    def _(g):
        turned = w_buf[g].T
        high, low = split_bf16(turned)
        wt_hi[g] = high
        wt_lo[g] = low

    cot_copy.wait()
    for copy in table_copies:
        copy.wait()

    channels = devices * rows
    table = jnp.concatenate(
        (taps_buf[...], skip_buf[...], jnp.zeros((128 - taps - 1, channels), F32)), axis=0
    )
    table = table.T
    for d in range(devices):
        taps_ref[d] = table[d * rows : (d + 1) * rows, :]

    def mix_add(block, h, first):
        high, low = split_bf16(cot_all[block, :, h * half_len : (h + 1) * half_len])
        result = jnp.dot(wt_lo[block], high, preferred_element_type=F32)
        result = result + jnp.dot(wt_hi[block], low, preferred_element_type=F32)
        result = result + jnp.dot(wt_hi[block], high, preferred_element_type=F32)
        at = (slice(None), slice(h * half_len, (h + 1) * half_len))
        mix[at] = result if first else mix[at] + result

    def mix_step(step, h):
        for up in (True, False):
            @pl.when(arrives(step, up))
            def _():
                mix_add(chan - step if up else chan + step, h, False)

    for h in range(halves):
        mix_add(chan, h, True)

    def conv_rows(at):
        tap = tap_rows(at)
        parts = [sig_buf[a, at, :] for a in range(devices)]
        conv = []
        for a in range(devices):
            total = tap[:, :1] * parts[a]
            for j in range(1, taps):
                total = total + tap[:, j : j + 1] * delayed(parts, a, j)
            conv_buf[a, at, :] = total
            conv.append(total)
        forward_blocks(conv, twiddle, stage_store(at))

    def forward_rows(source):
        def body(at):
            forward_blocks(
                [source[a, at, :] for a in range(devices)], twiddle, stage_store(at)
            )

        return body

    def resp_rows(at):
        skip = tap_rows(at)[:, taps : taps + 1]
        conv = inverse_blocks(devices, length, twiddle, lambda q: work[q, at, :])
        for a in range(devices):
            resp_send[a, at, :] = conv[a] + skip * conv_buf[a, at, :]

    for i, part in enumerate(early):
        sig_moves[i][1]()
        over_rows(conv_rows, part)
        dft(plain, val_spec, part)
        fil_moves[i][1]()
        over_rows(forward_rows(fil_buf), part)
        dft(plain, fil_spec, part)
        if groups > 1 and i == 0:
            line_arrive(1, 0)
        dft(product(fil_spec, val_spec, False), work, part)
        over_rows(resp_rows, part)
        resp_moves[i][0]()
        if groups > 1 and i == 0:
            for h in range(1, halves):
                line_arrive(1, h)
    if groups > 1:
        for h in range(halves):
            mix_step(1, h)

    gate_copy.wait()
    for h in range(halves):
        for step in range(2, groups):
            line_arrive(step, h)
            mix_step(step, h)
        here = slice(h * half_len, (h + 1) * half_len)
        for d in range(devices):
            grad_send[d, :, here] = mix[d * rows : (d + 1) * rows, here] * gate_buf[d, :, here]
        for move in grad_moves[h]:
            move[0]()

    for move in resp_moves:
        move[1]()
    for d in range(devices):
        gate_buf[d] = mix[d * rows : (d + 1) * rows, :] * resp_buf[d]
    gate_store = pltpu.make_async_copy(gate_buf, gate_out, load_sem.at[1])
    gate_store.start()

    def filter_rows(at):
        parts = inverse_blocks(devices, length, twiddle, lambda q: work[q, at, :])
        for a in range(devices):
            gfil_send[a, at, :] = parts[a]

    def value_rows(at):
        tap = tap_rows(at)
        skip = tap[:, taps : taps + 1]
        value = inverse_blocks(devices, length, twiddle, lambda q: work[q, at, :])
        grad = [grad_buf[a, at, :] for a in range(devices)]
        value = [value[a] + skip * grad[a] for a in range(devices)]
        sums = [None] * taps
        for a in range(devices):
            signal = sig_buf[a, at, :]
            total = None
            for j in range(taps):
                ahead = advanced(value, a, j)
                term, part_sum = tap[:, j : j + 1] * ahead, ahead * signal
                total = term if total is None else total + term
                sums[j] = part_sum if sums[j] is None else sums[j] + part_sum
            gsig_send[a, at, :] = total
        skip_sum = grad[0] * conv_buf[0, at, :]
        for a in range(1, devices):
            skip_sum = skip_sum + grad[a] * conv_buf[a, at, :]
        lane = lax.broadcasted_iota(jnp.int32, (group_rows, 128), 1)
        placed = jnp.zeros((group_rows, 128), F32)
        for j, each in enumerate(sums + [skip_sum]):
            total = jnp.sum(each, axis=1, keepdims=True) * np.float32(scale)
            placed = jnp.where(lane == j, total, placed)
        small_buf[at, :] = placed

    small_buf[...] = jnp.zeros_like(small_buf)
    for i, part in enumerate(late):
        for h in range(halves):
            grad_moves[h][i][1]()
        over_rows(forward_rows(grad_buf), part)
        dft(plain, grad_spec, part)
        dft(product(val_spec, grad_spec, True), work, part)
        over_rows(filter_rows, part)
        gfil_moves[i][0]()
        dft(product(fil_spec, grad_spec, True), work, part)
        over_rows(value_rows, part)
        if i == len(late) - 1:
            small_send[...] = small_buf[...].T[:8, :]
            small_start()
        gsig_moves[i][0]()

    for step in range(groups):
        for up in (True, False):
            @pl.when(sends(step, up))
            def _():
                for h in range(halves):
                    hop(step, h, up).wait_send()

    small_arrive()
    per_tile = 128 // rows
    for tile in range(-(-channels // 128)):
        total = None
        for i in range(min(per_tile, devices - tile * per_tile)):
            each = small_land[tile * per_tile + i]
            each = each if i == 0 else pltpu.roll(each, i * rows, 1)
            total = each if total is None else total + each
        width = min(128, channels - tile * 128)
        at = slice(tile * 128, tile * 128 + width)
        taps_buf[:, at] = total[:taps, :width]
        skip_buf[:, at] = total[taps : taps + 1, :width]
    small_stores = [
        pltpu.make_async_copy(source, target, load_sem.at[2 + i])
        for i, (source, target) in enumerate(((taps_buf, tap_out), (skip_buf, skip_out)))
    ]
    for store in small_stores:
        store.start()
    gate_store.wait()
    for store in small_stores:
        store.wait()
    for sent in moves:
        sent()
    for move in gfil_moves + gsig_moves:
        move[1]()


def handed_on(*refs):
    count = (len(refs) - 1) // 3
    loads, stores = [], []
    for source, result, held in zip(refs[:count], refs[count : 2 * count], refs[2 * count : -1]):
        pieces = 2 if source.shape[0] % 2 == 0 else 1
        size = source.shape[0] // pieces
        for piece in range(pieces):
            at, sems = pl.ds(piece * size, size), refs[-1].at[len(loads)]
            loads.append(pltpu.make_async_copy(source.at[at], held.at[at], sems.at[0]))
            stores.append(pltpu.make_async_copy(held.at[at], result.at[at], sems.at[1]))
    for load in loads:
        load.start()
    for load, store in zip(loads, stores):
        load.wait()
        store.start()
    for store in stores:
        store.wait()


def per_device(signal, gate_in, filter_raw, short_kernel, skip_gain, out_weight, cotangent):
    channels, length = signal.shape
    taps = short_kernel.shape[1]
    devices, groups = lax.axis_size("ctx"), lax.axis_size("chan")
    rows = channels // devices
    rows_pad = max(rows, 8)
    halves = 2
    scale = 1.0 / math.sqrt(length * devices)
    twiddle, high, low = tables(devices, length, scale)
    shape = (devices, rows, length)
    out_rows = cotangent.shape[0]
    early = [(0, rows // 2), (rows // 2, rows // 2)] if rows % 16 == 0 else [(0, rows)]
    late = [(0, rows // 4), (rows // 4, rows // 4), (rows // 2, rows // 2)] if rows % 32 == 0 else [(0, rows)]
    spec_shape = (devices + 1, rows_pad, 2 * length)
    dims = (devices, groups, rows, length, taps, halves, early, late, scale)
    moves = 3 * len(early) + (halves + 2) * len(late) + 1

    def vmem(*size, dtype=F32):
        return pltpu.VMEM(size, dtype)

    in_vmem, anywhere = pl.BlockSpec(memory_space=pltpu.VMEM), pl.BlockSpec(memory_space=pl.ANY)
    block = jax.ShapeDtypeStruct(shape, F32)
    results = (block,) * 3 + tuple(
        jax.ShapeDtypeStruct((count, channels), F32) for count in (taps, 1)
    )
    held = pl.pallas_call(
        functools.partial(kernel, dims),
        out_shape=results,
        in_specs=[anywhere] * 10,
        out_specs=(anywhere,) * 5,
        scratch_shapes=[
            vmem(groups, out_rows, channels),
            vmem(groups, channels, out_rows, dtype=BF16),
            vmem(groups, channels, out_rows, dtype=BF16),
            vmem(groups, out_rows, length),
            vmem(channels, length),
            *[vmem(*shape) for _ in range(10)],
            vmem(devices, rows, 128),
            vmem(128, 128),
            vmem(8, 128),
            vmem(devices, 8, 128),
            *[vmem(*spec_shape) for _ in range(5)],
            vmem(*twiddle.shape),
            vmem(*high.shape, dtype=BF16),
            vmem(*low.shape, dtype=BF16),
            vmem(taps, channels),
            vmem(1, channels),
            pltpu.SemaphoreType.DMA((halves, groups)),
            pltpu.SemaphoreType.DMA((halves, groups)),
            pltpu.SemaphoreType.DMA((halves, groups)),
            pltpu.SemaphoreType.DMA((moves,)),
            pltpu.SemaphoreType.DMA((moves,)),
            pltpu.SemaphoreType.DMA((8,)),
        ],
        compiler_params=pltpu.CompilerParams(
            collective_id=0, has_side_effects=True, vmem_limit_bytes=56 * 2**20
        ),
    )(
        signal.reshape(shape),
        gate_in.reshape(shape),
        filter_raw.reshape(shape),
        short_kernel.T,
        skip_gain[None, :],
        out_weight.reshape(groups, out_rows, channels),
        cotangent,
        jnp.asarray(twiddle),
        jnp.asarray(high),
        jnp.asarray(low),
    )
    grad_gate, grad_signal, grad_filter, grad_kernel, grad_skip = pl.pallas_call(
        handed_on,
        out_shape=results,
        in_specs=[anywhere] * 5,
        out_specs=(anywhere,) * 5,
        scratch_shapes=[vmem(*each.shape) for each in results]
        + [pltpu.SemaphoreType.DMA((8, 2))],
    )(*held)
    whole = (channels, length)
    return (
        grad_gate.reshape(whole),
        grad_signal.reshape(whole),
        grad_filter.reshape(whole),
        grad_kernel.T,
        grad_skip[0],
    )


def solution(mesh):
    placed = (
        P("chan", "ctx"),
        P("chan", "ctx"),
        P("chan", "ctx"),
        P("chan", None),
        P("chan"),
        P(None, "chan"),
        P("chan", "ctx"),
    )
    return jax.shard_map(
        per_device,
        mesh=mesh,
        in_specs=placed,
        out_specs=(
            P("chan", "ctx"),
            P("chan", "ctx"),
            P("chan", "ctx"),
            P("chan", None),
            P("chan"),
        ),
        check_vma=False,
    )
```

```python
import functools
import math

import jax
import jax.numpy as jnp
import numpy as np
from jax import lax
from jax.experimental import pallas as pl
from jax.experimental.pallas import tpu as pltpu
from jax.sharding import PartitionSpec as P

MESH = pl.DeviceIdType.MESH
F32 = jnp.float32
BF16 = jnp.bfloat16


def split_bf16(value):
    high = value.astype(BF16)
    return high, (value - high.astype(F32)).astype(BF16)


def tables(blocks, length, scale):
    total = 2 * blocks * length
    turn = np.arange(blocks + 1)[:, None] * np.arange(length)[None, :] % total
    angle = 2.0 * np.pi / total * turn
    weight = np.full((blocks + 1, 1), 2.0)
    weight[0] = weight[blocks] = 1.0
    weight = weight * (scale / total)
    twiddle = np.stack(
        (np.cos(angle), np.sin(angle), weight * np.cos(angle), weight * np.sin(angle))
    ).astype(np.float32)
    turn = np.arange(length)[:, None] * np.arange(length)[None, :] % length
    angle = 2.0 * np.pi / length * turn
    cosine, sine = np.cos(angle), np.sin(angle)
    matrix = np.block([[cosine, -sine], [sine, cosine]]).astype(np.float32)
    high = matrix.astype(jnp.bfloat16)
    low = (matrix - high.astype(np.float32)).astype(jnp.bfloat16)
    return twiddle, high, low


def weighted_sum(terms):
    total = None
    for factor, value in terms:
        if abs(factor) < 1e-12:
            continue
        if abs(factor - 1.0) < 1e-12:
            part = value
        elif abs(factor + 1.0) < 1e-12:
            part = -value
        else:
            part = np.float32(factor) * value
        total = part if total is None else total + part
    return total


def forward_blocks(parts, twiddle, store):
    blocks = len(parts)

    def put(q, real, imag):
        cosine, sine = twiddle[0, q : q + 1, :], twiddle[1, q : q + 1, :]
        if imag is None:
            store(q, real * cosine, -real * sine)
        else:
            store(q, real * cosine + imag * sine, imag * cosine - real * sine)

    for q in range(blocks // 2 + 1):
        def gather(first, trig, sign):
            return weighted_sum(
                [(sign * trig(math.pi * a * q / blocks), parts[a]) for a in range(first, blocks, 2)]
            )

        even_re, even_im = gather(0, math.cos, 1.0), gather(0, math.sin, -1.0)
        odd_re, odd_im = gather(1, math.cos, 1.0), gather(1, math.sin, -1.0)

        def add(a, b, sign_a, sign_b):
            return weighted_sum([(s, v) for s, v in ((sign_a, a), (sign_b, b)) if v is not None])

        put(q, add(even_re, odd_re, 1.0, 1.0), add(even_im, odd_im, 1.0, 1.0))
        if q != blocks - q:
            put(blocks - q, add(even_re, odd_re, 1.0, -1.0), add(even_im, odd_im, -1.0, 1.0))


def inverse_blocks(blocks, length, twiddle, load):
    def real_imag(q):
        pair = load(q)
        real, minus = pair[:, :length], pair[:, length:]
        cosine, sine = twiddle[2, q : q + 1, :], twiddle[3, q : q + 1, :]
        return real * cosine + minus * sine, real * sine - minus * cosine

    first, last = real_imag(0)[0], real_imag(blocks)[0]
    half_re, half_im = real_imag(blocks // 2)
    pairs = []
    for q in range(1, blocks // 2):
        (re_a, im_a), (re_b, im_b) = real_imag(q), real_imag(blocks - q)
        pairs.append((re_a + re_b, im_a - im_b, re_a - re_b, im_a + im_b))
    result = []
    for a in range(blocks):
        odd = a % 2
        terms = [(1.0, first - last if odd else first + last)]
        terms.append((math.cos(math.pi * a / 2), half_re))
        terms.append((-math.sin(math.pi * a / 2), half_im))
        for q in range(1, blocks // 2):
            angle = math.pi * a * q / blocks
            terms.append((math.cos(angle), pairs[q - 1][2 * odd]))
            terms.append((-math.sin(angle), pairs[q - 1][2 * odd + 1]))
        result.append(weighted_sum(terms))
    return result


def kernel(
    dims,
    sig_in, gate_in, fil_in, taps_in, skip_in, w_in, cot_in, twiddle_in, high_in, low_in,
    gate_out, gsig_out, gfil_out, tap_out, skip_out,
    w_buf, wt_hi, wt_lo, cot_all, mix, gate_buf, sig_buf, fil_buf, conv_buf,
    resp_send, resp_buf, grad_send, grad_buf, gsig_send, gfil_send, taps_ref, small_buf, small_send, small_land,
    stage, fil_spec, val_spec, grad_spec, work, twiddle, high_ref, low_ref, taps_buf, skip_buf,
    far_buf, far_hi, far_lo, part_send, part_buf,
    up_sem, down_sem, line_sem, send_sem, recv_sem, load_sem,
):
    devices, groups, rows, length, taps, halves, early, late, shared, scale = dims
    me, chan = lax.axis_index("ctx"), lax.axis_index("chan")
    half_len = length // halves
    group_rows = min(8, rows)
    classes = devices + 1

    barrier = pltpu.get_barrier_semaphore()

    @pl.loop(1, devices)
    def _(k):
        pl.semaphore_signal(
            barrier, inc=1, device_id={"ctx": lax.rem(me + k, devices)}, device_id_type=MESH
        )

    for inside, other in ((chan + 1 < groups, chan + 1), (chan >= 1, chan - 1)):
        @pl.when(inside)
        def _():
            pl.semaphore_signal(barrier, inc=1, device_id={"chan": other}, device_id_type=MESH)

    w_copy = pltpu.make_async_copy(w_in, w_buf, load_sem.at[0])
    gate_copy = pltpu.make_async_copy(gate_in, gate_buf, load_sem.at[1])
    cot_copy = pltpu.make_async_copy(cot_in, cot_all.at[chan], load_sem.at[2])
    table_copies = [
        pltpu.make_async_copy(source, target, load_sem.at[3 + i])
        for i, (source, target) in enumerate(
            (
                (taps_in, taps_buf), (skip_in, skip_buf), (twiddle_in, twiddle),
                (high_in, high_ref), (low_in, low_ref),
            )
        )
    ]
    w_copy.start()
    cot_copy.start()
    for copy in table_copies:
        copy.start()
    gate_copy.start()

    beside = (chan + 1 < groups).astype(jnp.int32) + (chan >= 1).astype(jnp.int32)
    pl.semaphore_wait(barrier, devices - 1 + beside)

    def lanes(h):
        return pl.ds(h * half_len, half_len)

    def hop(step, h, up):
        block = chan - step if up else chan + step
        source = cot_in if step == 0 else cot_all.at[block]
        sems = up_sem if up else down_sem
        return pltpu.make_async_remote_copy(
            src_ref=source.at[:, lanes(h)],
            dst_ref=cot_all.at[block, :, lanes(h)],
            send_sem=sems.at[h, step],
            recv_sem=line_sem.at[h, block],
            device_id={"chan": chan + 1 if up else chan - 1},
            device_id_type=MESH,
        )

    def sends(step, up):
        if up:
            return jnp.logical_and(chan - step >= 0, chan + 1 < groups)
        return jnp.logical_and(chan + step < groups, chan >= 1)

    def arrives(step, up):
        return chan - step >= 0 if up else chan + step < groups

    def line_start(step, h):
        for up in (True, False):
            @pl.when(sends(step, up))
            def _():
                hop(step, h, up).start()

    def line_arrive(step, h):
        for up in (True, False):
            @pl.when(arrives(step, up))
            def _():
                block = chan - step if up else chan + step
                slot = cot_all.at[block, :, lanes(h)]
                pltpu.make_async_remote_copy(
                    src_ref=slot,
                    dst_ref=slot,
                    send_sem=up_sem.at[h, step],
                    recv_sem=line_sem.at[h, block],
                    device_id={"chan": chan - 1 if up else chan + 1},
                    device_id_type=MESH,
                ).wait_recv()

                @pl.when(sends(step, up))
                def _():
                    hop(step, h, up).start()

    moves = []

    def all_to_all(source, target, landed):
        index = len(moves)

        def start():
            @pl.loop(1, devices)
            def _(k):
                peer = lax.rem(me + k, devices)
                pltpu.make_async_remote_copy(
                    src_ref=source(peer),
                    dst_ref=target(me),
                    send_sem=send_sem.at[index],
                    recv_sem=recv_sem.at[index],
                    device_id={"ctx": peer},
                    device_id_type=MESH,
                ).start()

            pltpu.make_async_copy(source(me), target(me), recv_sem.at[index]).start()

        def arrive():
            everything = landed(devices)
            pltpu.make_async_copy(everything, everything, recv_sem.at[index]).wait()

        def sent():
            others = landed(devices - 1)
            pltpu.make_async_copy(others, others, send_sem.at[index]).wait()

        moves.append(sent)
        return start, arrive

    def by_part(source, target, part, lane=slice(None)):
        at = pl.ds(*part)
        return all_to_all(
            lambda p: source.at[p, at, lane],
            lambda p: target.at[p, at, lane],
            lambda n: target.at[pl.ds(0, n), at, lane],
        )

    sig_moves = [by_part(sig_in, sig_buf, part) for part in early]
    fil_moves = [by_part(fil_in, fil_buf, part) for part in early]
    resp_moves = [by_part(resp_send, resp_buf, part) for part in early]
    grad_moves = [
        [by_part(grad_send, grad_buf, part, lanes(h)) for part in late] for h in range(halves)
    ]
    gfil_moves = [by_part(gfil_send, gfil_out, part) for part in late]
    gsig_moves = [by_part(gsig_send, gsig_out, part) for part in late]
    small_start, small_arrive = all_to_all(
        lambda p: small_send, lambda p: small_land.at[p], lambda n: small_land.at[pl.ds(0, n)]
    )

    side = chan // 2
    edge, near, far, last = 3 * side, 1 + side, 2 - side, 3 - 3 * side
    on_edge, inside = chan % 3 == 0, chan % 3 != 0
    core = me % 2
    across_x, across_y = me + 2 - 4 * (me // 2 % 2), me + 4 - 8 * (me // 4)
    first_peer = (1 - core) * across_x + core * across_y
    second_peer = (1 - core) * across_y + core * across_x
    sibling, opposite = me + 1 - 2 * core, across_x + across_y - me
    line_copies = []

    def line_copy(index, where, source, target, other):
        copy = pltpu.make_async_remote_copy(
            src_ref=source,
            dst_ref=target,
            send_sem=up_sem.at[index],
            recv_sem=down_sem.at[index],
            device_id={"chan": other},
            device_id_type=MESH,
        )
        line_copies.append((where, copy))
        return copy

    def half_block(index, where, block, h, other, own=False):
        slot = cot_all.at[block, :, lanes(h)]
        return line_copy(index, where, cot_in.at[:, lanes(h)] if own else slot, slot, other)

    def landed(sem, ref):
        pltpu.make_async_copy(ref, ref, sem).wait()

    def half_landed(index, block, h):
        landed(down_sem.at[index], cot_all.at[block, :, lanes(h)])

    def far_piece(index):
        return far_buf.at[index // 2, index % 2]

    def far_copy(source, send, recv, peer):
        return pltpu.make_async_remote_copy(
            src_ref=source,
            dst_ref=source,
            send_sem=line_sem.at[send],
            recv_sem=line_sem.at[recv],
            device_id={"ctx": peer},
            device_id_type=MESH,
        )

    if shared:
        piece_rows = far_buf.shape[2]
        per_block = devices // 2
        piece_at = pl.ds(pl.multiple_of(me % per_block * piece_rows, piece_rows), piece_rows)
        weight_copy = line_copy(
            0, on_edge,
            w_in.at[far + (last - far) * (me // per_block), piece_at],
            far_piece(me), near,
        )
        edge_out = [half_block(1 + h, on_edge, edge, h, near, own=True) for h in range(2)]
        near_to_edge = [half_block(3 + h, inside, near, h, edge, own=True) for h in range(2)]
        near_to_far = [half_block(5 + h, inside, near, h, far, own=True) for h in range(2)]
        far_to_edge = half_block(7, inside, far, 0, edge)
        edge_to_far = [half_block(8 + h, inside, edge, h, far) for h in range(2)]
        last_to_edge = half_block(10, inside, last, 0, edge)
        pieces = [(0, rows // 2), (rows // 2, rows // 2)]
        part_copies = [
            line_copy(11 + i, inside, part_send.at[:, pl.ds(*p)], part_buf.at[:, pl.ds(*p)], edge)
            for i, p in enumerate(pieces)
        ]

        @pl.when(on_edge)
        def _():
            weight_copy.start()
            for copy in edge_out:
                copy.start()

        @pl.when(inside)
        def _():
            for h in range(2):
                near_to_edge[h].start()
                near_to_far[h].start()

        sig_moves[0][0]()
        fil_moves[0][0]()
    else:
        for h in range(halves):
            line_start(0, h)
        for sig_move, fil_move in zip(sig_moves, fil_moves):
            sig_move[0]()
            fil_move[0]()

    def dft(read, target, part):
        span = max(part[1], 8)
        at = (slice(None), slice(part[0], part[0] + span))
        high, low = split_bf16(read(at).reshape(classes * span, 2 * length))
        result = jnp.dot(high, low_ref[...], preferred_element_type=F32)
        result = result + jnp.dot(low, high_ref[...], preferred_element_type=F32)
        result = result + jnp.dot(high, high_ref[...], preferred_element_type=F32)
        target[at] = result.reshape(classes, span, 2 * length)

    def plain(at):
        return stage[at]

    def product(first, second, conjugate):
        def read(at):
            a_re, a_im = first[at][:, :, :length], first[at][:, :, length:]
            b_re, b_im = second[at][:, :, :length], second[at][:, :, length:]
            if conjugate:
                real, minus = a_re * b_re + a_im * b_im, a_im * b_re - a_re * b_im
            else:
                real, minus = a_re * b_re - a_im * b_im, -(a_re * b_im + a_im * b_re)
            return jnp.concatenate((real, minus), axis=2)

        return read

    def over_rows(body, part):
        first = part[0] // group_rows

        @pl.loop(first, first + part[1] // group_rows)
        def _(r):
            body(pl.ds(pl.multiple_of(r * group_rows, group_rows), group_rows))

    def stage_store(at):
        def store(q, real, imag):
            stage[q, at, :length] = real
            stage[q, at, length:] = imag

        return store

    def tap_rows(at):
        return taps_ref[me, at, :]

    def delayed(parts, a, j):
        if j == 0:
            return parts[a]
        before = jnp.zeros_like(parts[a][:, :128]) if a == 0 else parts[a - 1][:, length - 128 :]
        joined = jnp.concatenate((before, parts[a]), axis=1)
        return pltpu.roll(joined, j, 1)[:, 128:]

    def advanced(parts, a, j):
        if j == 0:
            return parts[a]
        after = jnp.zeros_like(parts[a][:, :128]) if a == devices - 1 else parts[a + 1][:, :128]
        joined = jnp.concatenate((parts[a], after), axis=1)
        return pltpu.roll(joined, length + 128 - j, 1)[:, :length]

    w_copy.wait()

    @pl.loop(0, groups)
    def _(g):
        turned = w_buf[g].T
        high, low = split_bf16(turned)
        wt_hi[g] = high
        wt_lo[g] = low

    cot_copy.wait()
    for copy in table_copies:
        copy.wait()

    channels = devices * rows
    table = jnp.concatenate(
        (taps_buf[...], skip_buf[...], jnp.zeros((128 - taps - 1, channels), F32)), axis=0
    )
    table = table.T
    for d in range(devices):
        taps_ref[d] = table[d * rows : (d + 1) * rows, :]

    def mix_add(block, h, first):
        high, low = split_bf16(cot_all[block, :, h * half_len : (h + 1) * half_len])
        result = jnp.dot(wt_lo[block], high, preferred_element_type=F32)
        result = result + jnp.dot(wt_hi[block], low, preferred_element_type=F32)
        result = result + jnp.dot(wt_hi[block], high, preferred_element_type=F32)
        at = (slice(None), slice(h * half_len, (h + 1) * half_len))
        mix[at] = result if first else mix[at] + result

    def mix_step(step, h):
        for up in (True, False):
            @pl.when(arrives(step, up))
            def _():
                mix_add(chan - step if up else chan + step, h, False)

    for h in range(halves):
        mix_add(chan, h, True)

    def conv_rows(at):
        tap = tap_rows(at)
        parts = [sig_buf[a, at, :] for a in range(devices)]
        conv = []
        for a in range(devices):
            total = tap[:, :1] * parts[a]
            for j in range(1, taps):
                total = total + tap[:, j : j + 1] * delayed(parts, a, j)
            conv_buf[a, at, :] = total
            conv.append(total)
        forward_blocks(conv, twiddle, stage_store(at))

    def forward_rows(source):
        def body(at):
            forward_blocks(
                [source[a, at, :] for a in range(devices)], twiddle, stage_store(at)
            )

        return body

    def resp_rows(at):
        skip = tap_rows(at)[:, taps : taps + 1]
        conv = inverse_blocks(devices, length, twiddle, lambda q: work[q, at, :])
        for a in range(devices):
            resp_send[a, at, :] = conv[a] + skip * conv_buf[a, at, :]

    def value_part(i):
        sig_moves[i][1]()
        over_rows(conv_rows, early[i])
        dft(plain, val_spec, early[i])

    def filter_part(i):
        fil_moves[i][1]()
        over_rows(forward_rows(fil_buf), early[i])
        dft(plain, fil_spec, early[i])

    def resp_part(i):
        dft(product(fil_spec, val_spec, False), work, early[i])
        over_rows(resp_rows, early[i])

    def grad_rows(h, first, count):
        here = slice(h * half_len, (h + 1) * half_len)
        for d in range(devices):
            at = slice(d * rows + first, d * rows + first + count)
            grad_send[d, first : first + count, here] = (
                mix[at, here] * gate_buf[d, first : first + count, here]
            )

    def grad_piece(i):
        first, count = pieces[i]
        grad_rows(1, first, count)
        for part, move in zip(late, grad_moves[1]):
            if first <= part[0] < first + count:
                move[0]()

    def partial(j, block):
        high, low = split_bf16(cot_all[block, :, half_len:])
        result = jnp.dot(far_lo[j], high, preferred_element_type=F32)
        result = result + jnp.dot(far_hi[j], low, preferred_element_type=F32)
        result = result + jnp.dot(far_hi[j], high, preferred_element_type=F32)
        result = result.reshape(devices, rows, half_len)
        part_send[...] = part_send[...] + result if j else result

    if shared:
        value_part(0)

        @pl.when(inside)
        def _():
            landed(down_sem.at[0], far_piece(me))
            far_copy(far_piece(me), 0, 3, first_peer).start()
            far_copy(far_piece(me), 1, 4, second_peer).start()

        filter_part(0)

        @pl.when(inside)
        def _():
            half_landed(5, far, 0)
            far_to_edge.start()

        resp_part(0)

        @pl.when(inside)
        def _():
            landed(line_sem.at[3], far_piece(first_peer))
            far_copy(far_piece(first_peer), 1, 4, second_peer).start()
            for index in (me, first_peer):
                far_copy(far_piece(index), 2, 5, sibling).start()

        def start_rest():
            for i in range(1, len(early)):
                sig_moves[i][0]()
                fil_moves[i][0]()
            resp_moves[0][0]()

        pl.when(on_edge)(start_rest)

        @pl.when(on_edge)
        def _():
            for h in range(2):
                half_landed(3 + h, near, h)
                mix_add(near, h, False)

        @pl.when(inside)
        def _():
            mix_add(far, 0, False)
            half_landed(1, edge, 0)
            edge_to_far[0].start()
            mix_add(edge, 0, False)
            half_landed(6, far, 1)
            mix_add(far, 1, False)
            half_landed(2, edge, 1)
            edge_to_far[1].start()
            landed(line_sem.at[4], far_buf.at[pl.ds(0, 2), 0])
            for index in (second_peer, opposite):
                far_copy(far_piece(index), 2, 5, sibling).start()
            start_rest()
            half_landed(8, last, 0)
            last_to_edge.start()
            mix_add(last, 0, False)
            mix_add(edge, 1, False)

        gate_copy.wait()

        @pl.when(on_edge)
        def _():
            half_landed(7, far, 0)
            mix_add(far, 0, False)
            half_landed(10, last, 0)
            mix_add(last, 0, False)

        grad_rows(0, 0, rows)
        for move in grad_moves[0]:
            move[0]()

        @pl.when(inside)
        def _():
            landed(line_sem.at[5], far_buf.at[:, 1 - core])

            @pl.loop(0, 2)
            def _(j):
                block = far_buf[pl.ds(j * (per_block // 2), per_block // 2)]
                high, low = split_bf16(block.reshape(block.shape[0] * 2 * piece_rows, -1).T)
                far_hi[j] = high
                far_lo[j] = low

            partial(0, far)
            half_landed(9, last, 1)
            partial(1, last)
            for copy in part_copies:
                copy.start()
            mix_add(last, 1, False)
            for i in range(2):
                grad_piece(i)

        for i in range(1, len(early)):
            value_part(i)
            filter_part(i)
            resp_part(i)

        @pl.when(on_edge)
        def _():
            for i, (first, count) in enumerate(pieces):
                landed(down_sem.at[11 + i], part_buf.at[:, pl.ds(first, count)])
                for d in range(devices):
                    at = slice(d * rows + first, d * rows + first + count)
                    mix[at, half_len:] = mix[at, half_len:] + part_buf[d, first : first + count, :]
                grad_piece(i)

        for i in range(1, len(early)):
            resp_moves[i][0]()
    else:
        for i, part in enumerate(early):
            value_part(i)
            filter_part(i)
            if groups > 1 and i == 0:
                line_arrive(1, 0)
            resp_part(i)
            resp_moves[i][0]()
            if groups > 1 and i == 0:
                for h in range(1, halves):
                    line_arrive(1, h)
        if groups > 1:
            for h in range(halves):
                mix_step(1, h)
        gate_copy.wait()
        for h in range(halves):
            for step in range(2, groups):
                line_arrive(step, h)
                mix_step(step, h)
            grad_rows(h, 0, rows)
            for move in grad_moves[h]:
                move[0]()

    def gate_part():
        for move in resp_moves:
            move[1]()
        for d in range(devices):
            gate_buf[d] = mix[d * rows : (d + 1) * rows, :] * resp_buf[d]
        gate_store.start()

    gate_store = pltpu.make_async_copy(gate_buf, gate_out, load_sem.at[1])

    def filter_rows(at):
        parts = inverse_blocks(devices, length, twiddle, lambda q: work[q, at, :])
        for a in range(devices):
            gfil_send[a, at, :] = parts[a]

    def value_rows(at):
        tap = tap_rows(at)
        skip = tap[:, taps : taps + 1]
        value = inverse_blocks(devices, length, twiddle, lambda q: work[q, at, :])
        grad = [grad_buf[a, at, :] for a in range(devices)]
        value = [value[a] + skip * grad[a] for a in range(devices)]
        sums = [None] * taps
        for a in range(devices):
            signal = sig_buf[a, at, :]
            total = None
            for j in range(taps):
                ahead = advanced(value, a, j)
                term, part_sum = tap[:, j : j + 1] * ahead, ahead * signal
                total = term if total is None else total + term
                sums[j] = part_sum if sums[j] is None else sums[j] + part_sum
            gsig_send[a, at, :] = total
        skip_sum = grad[0] * conv_buf[0, at, :]
        for a in range(1, devices):
            skip_sum = skip_sum + grad[a] * conv_buf[a, at, :]
        lane = lax.broadcasted_iota(jnp.int32, (group_rows, 128), 1)
        placed = jnp.zeros((group_rows, 128), F32)
        for j, each in enumerate(sums + [skip_sum]):
            total = jnp.sum(each, axis=1, keepdims=True) * np.float32(scale)
            placed = jnp.where(lane == j, total, placed)
        small_buf[at, :] = placed

    small_buf[...] = jnp.zeros_like(small_buf)
    for i, part in enumerate(late):
        for h in range(halves):
            grad_moves[h][i][1]()
        over_rows(forward_rows(grad_buf), part)
        dft(plain, grad_spec, part)
        dft(product(val_spec, grad_spec, True), work, part)
        over_rows(filter_rows, part)
        gfil_moves[i][0]()
        dft(product(fil_spec, grad_spec, True), work, part)
        over_rows(value_rows, part)
        if i == len(late) - 1:
            small_send[...] = small_buf[...].T[:8, :]
            small_start()
        gsig_moves[i][0]()
        if i == (len(late) - 1) // 2:
            gate_part()

    for where, copy in line_copies:
        @pl.when(where)
        def _():
            copy.wait_send()

    if shared:
        @pl.when(inside)
        def _():
            landed(line_sem.at[0], far_piece(me))
            landed(line_sem.at[1], far_buf.at[pl.ds(0, 2), 0])
            landed(line_sem.at[2], far_buf.at[:, 0])

    for step in range(0 if shared else groups):
        for up in (True, False):
            @pl.when(sends(step, up))
            def _():
                for h in range(halves):
                    hop(step, h, up).wait_send()

    small_arrive()
    per_tile = 128 // rows
    for tile in range(-(-channels // 128)):
        total = None
        for i in range(min(per_tile, devices - tile * per_tile)):
            each = small_land[tile * per_tile + i]
            each = each if i == 0 else pltpu.roll(each, i * rows, 1)
            total = each if total is None else total + each
        width = min(128, channels - tile * 128)
        at = slice(tile * 128, tile * 128 + width)
        taps_buf[:, at] = total[:taps, :width]
        skip_buf[:, at] = total[taps : taps + 1, :width]
    small_stores = [
        pltpu.make_async_copy(source, target, load_sem.at[2 + i])
        for i, (source, target) in enumerate(((taps_buf, tap_out), (skip_buf, skip_out)))
    ]
    for store in small_stores:
        store.start()
    gate_store.wait()
    for store in small_stores:
        store.wait()
    for sent in moves:
        sent()
    for move in gfil_moves + gsig_moves:
        move[1]()


def handed_on(*refs):
    count = (len(refs) - 1) // 3
    loads, stores = [], []
    for source, result, held in zip(refs[:count], refs[count : 2 * count], refs[2 * count : -1]):
        pieces = 2 if source.shape[0] % 2 == 0 else 1
        size = source.shape[0] // pieces
        for piece in range(pieces):
            at, sems = pl.ds(piece * size, size), refs[-1].at[len(loads)]
            loads.append(pltpu.make_async_copy(source.at[at], held.at[at], sems.at[0]))
            stores.append(pltpu.make_async_copy(held.at[at], result.at[at], sems.at[1]))
    for load in loads:
        load.start()
    for load, store in zip(loads, stores):
        load.wait()
        store.start()
    for store in stores:
        store.wait()


def per_device(signal, gate_in, filter_raw, short_kernel, skip_gain, out_weight, cotangent):
    channels, length = signal.shape
    taps = short_kernel.shape[1]
    devices, groups = lax.axis_size("ctx"), lax.axis_size("chan")
    rows = channels // devices
    rows_pad = max(rows, 8)
    halves = 2
    scale = 1.0 / math.sqrt(length * devices)
    twiddle, high, low = tables(devices, length, scale)
    shape = (devices, rows, length)
    out_rows = cotangent.shape[0]
    early = [(0, rows // 2), (rows // 2, rows // 2)] if rows % 16 == 0 else [(0, rows)]
    late = [(0, rows // 4), (rows // 4, rows // 4), (rows // 2, rows // 2)] if rows % 32 == 0 else [(0, rows)]
    spec_shape = (devices + 1, rows_pad, 2 * length)
    shared = groups == 4 and devices == 8 and len(early) == 2 and len(late) == 3
    far_shape = (4, 2, out_rows // 4, channels) if shared else (1, 2, 8, 128)
    half_shape = (devices, rows, length // 2) if shared else (1, 8, 128)
    dims = (devices, groups, rows, length, taps, halves, early, late, shared, scale)
    moves = 3 * len(early) + (halves + 2) * len(late) + 1

    def vmem(*size, dtype=F32):
        return pltpu.VMEM(size, dtype)

    in_vmem, anywhere = pl.BlockSpec(memory_space=pltpu.VMEM), pl.BlockSpec(memory_space=pl.ANY)
    block = jax.ShapeDtypeStruct(shape, F32)
    results = (block,) * 3 + tuple(
        jax.ShapeDtypeStruct((count, channels), F32) for count in (taps, 1)
    )
    held = pl.pallas_call(
        functools.partial(kernel, dims),
        out_shape=results,
        in_specs=[anywhere] * 10,
        out_specs=(anywhere,) * 5,
        scratch_shapes=[
            vmem(groups, out_rows, channels),
            vmem(groups, channels, out_rows, dtype=BF16),
            vmem(groups, channels, out_rows, dtype=BF16),
            vmem(groups, out_rows, length),
            vmem(channels, length),
            *[vmem(*shape) for _ in range(10)],
            vmem(devices, rows, 128),
            vmem(128, 128),
            vmem(8, 128),
            vmem(devices, 8, 128),
            *[vmem(*spec_shape) for _ in range(5)],
            vmem(*twiddle.shape),
            vmem(*high.shape, dtype=BF16),
            vmem(*low.shape, dtype=BF16),
            vmem(taps, channels),
            vmem(1, channels),
            vmem(*far_shape),
            vmem(2, channels, out_rows, dtype=BF16) if shared else vmem(8, 128),
            vmem(2, channels, out_rows, dtype=BF16) if shared else vmem(8, 128),
            vmem(*half_shape),
            vmem(*half_shape),
            pltpu.SemaphoreType.DMA((13,) if shared else (halves, groups)),
            pltpu.SemaphoreType.DMA((13,) if shared else (halves, groups)),
            pltpu.SemaphoreType.DMA((6,) if shared else (halves, groups)),
            pltpu.SemaphoreType.DMA((moves,)),
            pltpu.SemaphoreType.DMA((moves,)),
            pltpu.SemaphoreType.DMA((8,)),
        ],
        compiler_params=pltpu.CompilerParams(
            collective_id=0, has_side_effects=True, vmem_limit_bytes=56 * 2**20
        ),
    )(
        signal.reshape(shape),
        gate_in.reshape(shape),
        filter_raw.reshape(shape),
        short_kernel.T,
        skip_gain[None, :],
        out_weight.reshape(groups, out_rows, channels),
        cotangent,
        jnp.asarray(twiddle),
        jnp.asarray(high),
        jnp.asarray(low),
    )
    grad_gate, grad_signal, grad_filter, grad_kernel, grad_skip = pl.pallas_call(
        handed_on,
        out_shape=results,
        in_specs=[anywhere] * 5,
        out_specs=(anywhere,) * 5,
        scratch_shapes=[vmem(*each.shape) for each in results]
        + [pltpu.SemaphoreType.DMA((8, 2))],
    )(*held)
    whole = (channels, length)
    return (
        grad_gate.reshape(whole),
        grad_signal.reshape(whole),
        grad_filter.reshape(whole),
        grad_kernel.T,
        grad_skip[0],
    )


def solution(mesh):
    placed = (
        P("chan", "ctx"),
        P("chan", "ctx"),
        P("chan", "ctx"),
        P("chan", None),
        P("chan"),
        P(None, "chan"),
        P("chan", "ctx"),
    )
    return jax.shard_map(
        per_device,
        mesh=mesh,
        in_specs=placed,
        out_specs=(
            P("chan", "ctx"),
            P("chan", "ctx"),
            P("chan", "ctx"),
            P("chan", None),
            P("chan"),
        ),
        check_vma=False,
    )
```

```python
import functools
import math

import jax
import jax.numpy as jnp
import numpy as np
from jax import lax
from jax.experimental import pallas as pl
from jax.experimental.pallas import tpu as pltpu
from jax.sharding import PartitionSpec as P

MESH = pl.DeviceIdType.MESH
F32 = jnp.float32
BF16 = jnp.bfloat16


def split_bf16(value):
    high = value.astype(BF16)
    return high, (value - high.astype(F32)).astype(BF16)


def tables(blocks, length, scale):
    total = 2 * blocks * length
    turn = np.arange(blocks + 1)[:, None] * np.arange(length)[None, :] % total
    angle = 2.0 * np.pi / total * turn
    weight = np.full((blocks + 1, 1), 2.0)
    weight[0] = weight[blocks] = 1.0
    weight = weight * (scale / total)
    twiddle = np.stack(
        (np.cos(angle), np.sin(angle), weight * np.cos(angle), weight * np.sin(angle))
    ).astype(np.float32)
    turn = np.arange(length)[:, None] * np.arange(length)[None, :] % length
    angle = 2.0 * np.pi / length * turn
    cosine, sine = np.cos(angle), np.sin(angle)
    matrix = np.block([[cosine, -sine], [sine, cosine]]).astype(np.float32)
    high = matrix.astype(jnp.bfloat16)
    low = (matrix - high.astype(np.float32)).astype(jnp.bfloat16)
    return twiddle, high, low


def weighted_sum(terms):
    total = None
    for factor, value in terms:
        if abs(factor) < 1e-12:
            continue
        if abs(factor - 1.0) < 1e-12:
            part = value
        elif abs(factor + 1.0) < 1e-12:
            part = -value
        else:
            part = np.float32(factor) * value
        total = part if total is None else total + part
    return total


def forward_blocks(parts, twiddle, store):
    blocks = len(parts)

    def put(q, real, imag):
        cosine, sine = twiddle[0, q : q + 1, :], twiddle[1, q : q + 1, :]
        if imag is None:
            store(q, real * cosine, -real * sine)
        else:
            store(q, real * cosine + imag * sine, imag * cosine - real * sine)

    for q in range(blocks // 2 + 1):
        def gather(first, trig, sign):
            return weighted_sum(
                [(sign * trig(math.pi * a * q / blocks), parts[a]) for a in range(first, blocks, 2)]
            )

        even_re, even_im = gather(0, math.cos, 1.0), gather(0, math.sin, -1.0)
        odd_re, odd_im = gather(1, math.cos, 1.0), gather(1, math.sin, -1.0)

        def add(a, b, sign_a, sign_b):
            return weighted_sum([(s, v) for s, v in ((sign_a, a), (sign_b, b)) if v is not None])

        put(q, add(even_re, odd_re, 1.0, 1.0), add(even_im, odd_im, 1.0, 1.0))
        if q != blocks - q:
            put(blocks - q, add(even_re, odd_re, 1.0, -1.0), add(even_im, odd_im, -1.0, 1.0))


def inverse_blocks(blocks, length, twiddle, load):
    def real_imag(q):
        pair = load(q)
        real, minus = pair[:, :length], pair[:, length:]
        cosine, sine = twiddle[2, q : q + 1, :], twiddle[3, q : q + 1, :]
        return real * cosine + minus * sine, real * sine - minus * cosine

    first, last = real_imag(0)[0], real_imag(blocks)[0]
    half_re, half_im = real_imag(blocks // 2)
    pairs = []
    for q in range(1, blocks // 2):
        (re_a, im_a), (re_b, im_b) = real_imag(q), real_imag(blocks - q)
        pairs.append((re_a + re_b, im_a - im_b, re_a - re_b, im_a + im_b))
    result = []
    for a in range(blocks):
        odd = a % 2
        terms = [(1.0, first - last if odd else first + last)]
        terms.append((math.cos(math.pi * a / 2), half_re))
        terms.append((-math.sin(math.pi * a / 2), half_im))
        for q in range(1, blocks // 2):
            angle = math.pi * a * q / blocks
            terms.append((math.cos(angle), pairs[q - 1][2 * odd]))
            terms.append((-math.sin(angle), pairs[q - 1][2 * odd + 1]))
        result.append(weighted_sum(terms))
    return result


def kernel(
    dims,
    sig_in, gate_in, fil_in, taps_in, skip_in, w_in, cot_in, twiddle_in, high_in, low_in,
    gate_out, gsig_out, gfil_out, tap_out, skip_out,
    w_buf, wt_hi, wt_lo, cot_all, mix, gate_buf, sig_buf, fil_buf, conv_buf,
    resp_send, resp_buf, grad_send, grad_buf, gsig_send, gfil_send, taps_ref, small_buf, small_send, small_land,
    stage, fil_spec, val_spec, grad_spec, work, twiddle, high_ref, low_ref, taps_buf, skip_buf,
    far_buf, far_hi, far_lo, part_send, part_buf,
    up_sem, down_sem, line_sem, send_sem, recv_sem, load_sem,
):
    devices, groups, rows, length, taps, halves, early, late, shared, scale = dims
    me, chan = lax.axis_index("ctx"), lax.axis_index("chan")
    half_len = length // halves
    group_rows = min(8, rows)
    classes = devices + 1

    barrier = pltpu.get_barrier_semaphore()

    @pl.loop(1, devices)
    def _(k):
        pl.semaphore_signal(
            barrier, inc=1, device_id={"ctx": lax.rem(me + k, devices)}, device_id_type=MESH
        )

    for inside, other in ((chan + 1 < groups, chan + 1), (chan >= 1, chan - 1)):
        @pl.when(inside)
        def _():
            pl.semaphore_signal(barrier, inc=1, device_id={"chan": other}, device_id_type=MESH)

    w_copy = pltpu.make_async_copy(w_in, w_buf, load_sem.at[0])
    gate_copy = pltpu.make_async_copy(gate_in, gate_buf, load_sem.at[1])
    cot_copy = pltpu.make_async_copy(cot_in, cot_all.at[chan], load_sem.at[2])
    table_copies = [
        pltpu.make_async_copy(source, target, load_sem.at[3 + i])
        for i, (source, target) in enumerate(
            (
                (taps_in, taps_buf), (skip_in, skip_buf), (twiddle_in, twiddle),
                (high_in, high_ref), (low_in, low_ref),
            )
        )
    ]
    w_copy.start()
    cot_copy.start()
    for copy in table_copies:
        copy.start()
    gate_copy.start()

    beside = (chan + 1 < groups).astype(jnp.int32) + (chan >= 1).astype(jnp.int32)
    pl.semaphore_wait(barrier, devices - 1 + beside)

    def lanes(h):
        return pl.ds(h * half_len, half_len)

    def hop(step, h, up):
        block = chan - step if up else chan + step
        source = cot_in if step == 0 else cot_all.at[block]
        sems = up_sem if up else down_sem
        return pltpu.make_async_remote_copy(
            src_ref=source.at[:, lanes(h)],
            dst_ref=cot_all.at[block, :, lanes(h)],
            send_sem=sems.at[h, step],
            recv_sem=line_sem.at[h, block],
            device_id={"chan": chan + 1 if up else chan - 1},
            device_id_type=MESH,
        )

    def sends(step, up):
        if up:
            return jnp.logical_and(chan - step >= 0, chan + 1 < groups)
        return jnp.logical_and(chan + step < groups, chan >= 1)

    def arrives(step, up):
        return chan - step >= 0 if up else chan + step < groups

    def line_start(step, h):
        for up in (True, False):
            @pl.when(sends(step, up))
            def _():
                hop(step, h, up).start()

    def line_arrive(step, h):
        for up in (True, False):
            @pl.when(arrives(step, up))
            def _():
                block = chan - step if up else chan + step
                slot = cot_all.at[block, :, lanes(h)]
                pltpu.make_async_remote_copy(
                    src_ref=slot,
                    dst_ref=slot,
                    send_sem=up_sem.at[h, step],
                    recv_sem=line_sem.at[h, block],
                    device_id={"chan": chan - 1 if up else chan + 1},
                    device_id_type=MESH,
                ).wait_recv()

                @pl.when(sends(step, up))
                def _():
                    hop(step, h, up).start()

    moves = []

    def all_to_all(source, target, landed):
        index = len(moves)

        def start():
            @pl.loop(1, devices)
            def _(k):
                peer = lax.rem(me + k, devices)
                pltpu.make_async_remote_copy(
                    src_ref=source(peer),
                    dst_ref=target(me),
                    send_sem=send_sem.at[index],
                    recv_sem=recv_sem.at[index],
                    device_id={"ctx": peer},
                    device_id_type=MESH,
                ).start()

            pltpu.make_async_copy(source(me), target(me), recv_sem.at[index]).start()

        def arrive():
            everything = landed(devices)
            pltpu.make_async_copy(everything, everything, recv_sem.at[index]).wait()

        def sent():
            others = landed(devices - 1)
            pltpu.make_async_copy(others, others, send_sem.at[index]).wait()

        moves.append(sent)
        return start, arrive

    def by_part(source, target, part, lane=slice(None)):
        at = pl.ds(*part)
        return all_to_all(
            lambda p: source.at[p, at, lane],
            lambda p: target.at[p, at, lane],
            lambda n: target.at[pl.ds(0, n), at, lane],
        )

    sig_moves = [by_part(sig_in, sig_buf, part) for part in early]
    fil_moves = [by_part(fil_in, fil_buf, part) for part in early]
    resp_moves = [by_part(resp_send, resp_buf, part) for part in early]
    grad_moves = [
        [by_part(grad_send, grad_buf, part, lanes(h)) for part in late] for h in range(halves)
    ]
    gfil_moves = [by_part(gfil_send, gfil_out, part) for part in late]
    gsig_moves = [by_part(gsig_send, gsig_out, part) for part in late]
    small_start, small_arrive = all_to_all(
        lambda p: small_send, lambda p: small_land.at[p], lambda n: small_land.at[pl.ds(0, n)]
    )

    side = chan // 2
    edge, near, far, last = 3 * side, 1 + side, 2 - side, 3 - 3 * side
    on_edge, inside = chan % 3 == 0, chan % 3 != 0
    core = me % 2
    across_x, across_y = me + 2 - 4 * (me // 2 % 2), me + 4 - 8 * (me // 4)
    first_peer = (1 - core) * across_x + core * across_y
    second_peer = (1 - core) * across_y + core * across_x
    sibling, opposite = me + 1 - 2 * core, across_x + across_y - me
    line_copies = []

    def line_copy(index, where, source, target, other):
        copy = pltpu.make_async_remote_copy(
            src_ref=source,
            dst_ref=target,
            send_sem=up_sem.at[index],
            recv_sem=down_sem.at[index],
            device_id={"chan": other},
            device_id_type=MESH,
        )
        line_copies.append((where, copy))
        return copy

    def half_block(index, where, block, h, other, own=False):
        slot = cot_all.at[block, :, lanes(h)]
        return line_copy(index, where, cot_in.at[:, lanes(h)] if own else slot, slot, other)

    def landed(sem, ref):
        pltpu.make_async_copy(ref, ref, sem).wait()

    def half_landed(index, block, h):
        landed(down_sem.at[index], cot_all.at[block, :, lanes(h)])

    def far_piece(index):
        return far_buf.at[index // 2, index % 2]

    def far_copy(source, send, recv, peer):
        return pltpu.make_async_remote_copy(
            src_ref=source,
            dst_ref=source,
            send_sem=line_sem.at[send],
            recv_sem=line_sem.at[recv],
            device_id={"ctx": peer},
            device_id_type=MESH,
        )

    if shared:
        piece_rows = far_buf.shape[2]
        per_block = devices // 2
        piece_at = pl.ds(pl.multiple_of(me % per_block * piece_rows, piece_rows), piece_rows)
        weight_copy = line_copy(
            0, on_edge,
            w_in.at[far + (last - far) * (me // per_block), piece_at],
            far_piece(me), near,
        )
        edge_out = [half_block(1 + h, on_edge, edge, h, near, own=True) for h in range(2)]
        near_to_edge = [half_block(3 + h, inside, near, h, edge, own=True) for h in range(2)]
        near_to_far = [half_block(5 + h, inside, near, h, far, own=True) for h in range(2)]
        far_to_edge = half_block(7, inside, far, 0, edge)
        edge_to_far = [half_block(8 + h, inside, edge, h, far) for h in range(2)]
        last_to_edge = half_block(10, inside, last, 0, edge)
        pieces = late
        part_copies = [
            line_copy(11 + i, inside, part_send.at[:, pl.ds(*p)], part_buf.at[:, pl.ds(*p)], edge)
            for i, p in enumerate(pieces)
        ]

        @pl.when(on_edge)
        def _():
            weight_copy.start()
            for copy in edge_out:
                copy.start()

        @pl.when(inside)
        def _():
            for h in range(2):
                near_to_edge[h].start()
                near_to_far[h].start()

        sig_moves[0][0]()
        fil_moves[0][0]()
    else:
        for h in range(halves):
            line_start(0, h)
        for sig_move, fil_move in zip(sig_moves, fil_moves):
            sig_move[0]()
            fil_move[0]()

    def dft(read, target, part):
        span = max(part[1], 8)
        at = (slice(None), slice(part[0], part[0] + span))
        high, low = split_bf16(read(at).reshape(classes * span, 2 * length))
        result = jnp.dot(high, low_ref[...], preferred_element_type=F32)
        result = result + jnp.dot(low, high_ref[...], preferred_element_type=F32)
        result = result + jnp.dot(high, high_ref[...], preferred_element_type=F32)
        target[at] = result.reshape(classes, span, 2 * length)

    def plain(at):
        return stage[at]

    def product(first, second, conjugate):
        def read(at):
            a_re, a_im = first[at][:, :, :length], first[at][:, :, length:]
            b_re, b_im = second[at][:, :, :length], second[at][:, :, length:]
            if conjugate:
                real, minus = a_re * b_re + a_im * b_im, a_im * b_re - a_re * b_im
            else:
                real, minus = a_re * b_re - a_im * b_im, -(a_re * b_im + a_im * b_re)
            return jnp.concatenate((real, minus), axis=2)

        return read

    def over_rows(body, part):
        first = part[0] // group_rows

        @pl.loop(first, first + part[1] // group_rows)
        def _(r):
            body(pl.ds(pl.multiple_of(r * group_rows, group_rows), group_rows))

    def stage_store(at):
        def store(q, real, imag):
            stage[q, at, :length] = real
            stage[q, at, length:] = imag

        return store

    def tap_rows(at):
        return taps_ref[me, at, :]

    def delayed(parts, a, j):
        if j == 0:
            return parts[a]
        before = jnp.zeros_like(parts[a][:, :128]) if a == 0 else parts[a - 1][:, length - 128 :]
        joined = jnp.concatenate((before, parts[a]), axis=1)
        return pltpu.roll(joined, j, 1)[:, 128:]

    def advanced(parts, a, j):
        if j == 0:
            return parts[a]
        after = jnp.zeros_like(parts[a][:, :128]) if a == devices - 1 else parts[a + 1][:, :128]
        joined = jnp.concatenate((parts[a], after), axis=1)
        return pltpu.roll(joined, length + 128 - j, 1)[:, :length]

    w_copy.wait()

    @pl.loop(0, groups)
    def _(g):
        turned = w_buf[g].T
        high, low = split_bf16(turned)
        wt_hi[g] = high
        wt_lo[g] = low

    cot_copy.wait()
    for copy in table_copies:
        copy.wait()

    channels = devices * rows
    table = jnp.concatenate(
        (taps_buf[...], skip_buf[...], jnp.zeros((128 - taps - 1, channels), F32)), axis=0
    )
    table = table.T
    for d in range(devices):
        taps_ref[d] = table[d * rows : (d + 1) * rows, :]

    def mix_add(block, h, first):
        high, low = split_bf16(cot_all[block, :, h * half_len : (h + 1) * half_len])
        result = jnp.dot(wt_lo[block], high, preferred_element_type=F32)
        result = result + jnp.dot(wt_hi[block], low, preferred_element_type=F32)
        result = result + jnp.dot(wt_hi[block], high, preferred_element_type=F32)
        at = (slice(None), slice(h * half_len, (h + 1) * half_len))
        mix[at] = result if first else mix[at] + result

    def mix_step(step, h):
        for up in (True, False):
            @pl.when(arrives(step, up))
            def _():
                mix_add(chan - step if up else chan + step, h, False)

    for h in range(halves):
        mix_add(chan, h, True)

    def conv_rows(at):
        tap = tap_rows(at)
        parts = [sig_buf[a, at, :] for a in range(devices)]
        conv = []
        for a in range(devices):
            total = tap[:, :1] * parts[a]
            for j in range(1, taps):
                total = total + tap[:, j : j + 1] * delayed(parts, a, j)
            conv_buf[a, at, :] = total
            conv.append(total)
        forward_blocks(conv, twiddle, stage_store(at))

    def forward_rows(source):
        def body(at):
            forward_blocks(
                [source[a, at, :] for a in range(devices)], twiddle, stage_store(at)
            )

        return body

    def resp_rows(at):
        skip = tap_rows(at)[:, taps : taps + 1]
        conv = inverse_blocks(devices, length, twiddle, lambda q: work[q, at, :])
        for a in range(devices):
            resp_send[a, at, :] = conv[a] + skip * conv_buf[a, at, :]

    def value_part(i):
        sig_moves[i][1]()
        over_rows(conv_rows, early[i])
        dft(plain, val_spec, early[i])

    def filter_part(i):
        fil_moves[i][1]()
        over_rows(forward_rows(fil_buf), early[i])
        dft(plain, fil_spec, early[i])

    def resp_part(i):
        dft(product(fil_spec, val_spec, False), work, early[i])
        over_rows(resp_rows, early[i])

    def grad_rows(h, first, count):
        here = slice(h * half_len, (h + 1) * half_len)
        for d in range(devices):
            at = slice(d * rows + first, d * rows + first + count)
            grad_send[d, first : first + count, here] = (
                mix[at, here] * gate_buf[d, first : first + count, here]
            )

    def grad_piece(i):
        first, count = pieces[i]
        grad_rows(1, first, count)
        grad_moves[1][i][0]()

    def partial(j, block, sent):
        high, low = split_bf16(cot_all[block, :, half_len:])
        for i, (first, count) in enumerate(pieces):
            at = slice(devices * first, devices * (first + count))
            result = jnp.dot(far_lo[j, at, :], high, preferred_element_type=F32)
            result = result + jnp.dot(far_hi[j, at, :], low, preferred_element_type=F32)
            result = result + jnp.dot(far_hi[j, at, :], high, preferred_element_type=F32)
            result = result.reshape(devices, count, half_len)
            at = (slice(None), slice(first, first + count))
            part_send[at] = part_send[at] + result if j else result
            if sent:
                part_copies[i].start()

    if shared:
        value_part(0)

        @pl.when(inside)
        def _():
            landed(down_sem.at[0], far_piece(me))
            far_copy(far_piece(me), 0, 3, first_peer).start()
            far_copy(far_piece(me), 1, 4, second_peer).start()

        filter_part(0)

        @pl.when(inside)
        def _():
            half_landed(5, far, 0)
            far_to_edge.start()

        resp_part(0)

        @pl.when(inside)
        def _():
            landed(line_sem.at[3], far_piece(first_peer))
            far_copy(far_piece(first_peer), 1, 4, second_peer).start()
            for index in (me, first_peer):
                far_copy(far_piece(index), 2, 5, sibling).start()

        def start_rest():
            for i in range(1, len(early)):
                sig_moves[i][0]()
                fil_moves[i][0]()
            resp_moves[0][0]()

        pl.when(on_edge)(start_rest)

        @pl.when(on_edge)
        def _():
            for h in range(2):
                half_landed(3 + h, near, h)
                mix_add(near, h, False)

        @pl.when(inside)
        def _():
            mix_add(far, 0, False)
            half_landed(1, edge, 0)
            edge_to_far[0].start()
            mix_add(edge, 0, False)
            half_landed(6, far, 1)
            mix_add(far, 1, False)
            half_landed(2, edge, 1)
            edge_to_far[1].start()
            landed(line_sem.at[4], far_buf.at[pl.ds(0, 2), 0])
            for index in (second_peer, opposite):
                far_copy(far_piece(index), 2, 5, sibling).start()
            start_rest()
            half_landed(8, last, 0)
            last_to_edge.start()
            mix_add(last, 0, False)
            mix_add(edge, 1, False)

        gate_copy.wait()

        def first_grads():
            grad_rows(0, 0, rows)
            for move in grad_moves[0]:
                move[0]()

        @pl.when(on_edge)
        def _():
            half_landed(7, far, 0)
            mix_add(far, 0, False)

        @pl.when(inside)
        def _():
            first_grads()
            landed(line_sem.at[5], far_buf.at[:, 1 - core])

            @pl.loop(0, 2)
            def _(j):
                block = far_buf[pl.ds(j * (per_block // 2), per_block // 2)]
                turned = block.reshape(block.shape[0] * 2 * piece_rows, -1).T
                turned = turned.reshape(devices, rows, -1)
                for first, count in pieces:
                    high, low = split_bf16(
                        turned[:, first : first + count, :].reshape(devices * count, -1)
                    )
                    at = slice(devices * first, devices * (first + count))
                    far_hi[j, at, :] = high
                    far_lo[j, at, :] = low

            partial(0, far, False)
            half_landed(9, last, 1)
            partial(1, last, True)
            mix_add(last, 1, False)
            for i in range(len(pieces)):
                grad_piece(i)

        for i in range(1, len(early)):
            value_part(i)
            filter_part(i)
            resp_part(i)
            resp_moves[i][0]()

        @pl.when(on_edge)
        def _():
            half_landed(10, last, 0)
            mix_add(last, 0, False)
            first_grads()
            for i, (first, count) in enumerate(pieces):
                landed(down_sem.at[11 + i], part_buf.at[:, pl.ds(first, count)])
                for d in range(devices):
                    at = slice(d * rows + first, d * rows + first + count)
                    mix[at, half_len:] = mix[at, half_len:] + part_buf[d, first : first + count, :]
                grad_piece(i)

    else:
        for i, part in enumerate(early):
            value_part(i)
            filter_part(i)
            if groups > 1 and i == 0:
                line_arrive(1, 0)
            resp_part(i)
            resp_moves[i][0]()
            if groups > 1 and i == 0:
                for h in range(1, halves):
                    line_arrive(1, h)
        if groups > 1:
            for h in range(halves):
                mix_step(1, h)
        gate_copy.wait()
        for h in range(halves):
            for step in range(2, groups):
                line_arrive(step, h)
                mix_step(step, h)
            grad_rows(h, 0, rows)
            for move in grad_moves[h]:
                move[0]()

    def gate_part():
        for move in resp_moves:
            move[1]()
        for d in range(devices):
            gate_buf[d] = mix[d * rows : (d + 1) * rows, :] * resp_buf[d]
        gate_store.start()

    gate_store = pltpu.make_async_copy(gate_buf, gate_out, load_sem.at[1])

    def filter_rows(at):
        parts = inverse_blocks(devices, length, twiddle, lambda q: work[q, at, :])
        for a in range(devices):
            gfil_send[a, at, :] = parts[a]

    def value_rows(at):
        tap = tap_rows(at)
        skip = tap[:, taps : taps + 1]
        value = inverse_blocks(devices, length, twiddle, lambda q: work[q, at, :])
        grad = [grad_buf[a, at, :] for a in range(devices)]
        value = [value[a] + skip * grad[a] for a in range(devices)]
        sums = [None] * taps
        for a in range(devices):
            signal = sig_buf[a, at, :]
            total = None
            for j in range(taps):
                ahead = advanced(value, a, j)
                term, part_sum = tap[:, j : j + 1] * ahead, ahead * signal
                total = term if total is None else total + term
                sums[j] = part_sum if sums[j] is None else sums[j] + part_sum
            gsig_send[a, at, :] = total
        skip_sum = grad[0] * conv_buf[0, at, :]
        for a in range(1, devices):
            skip_sum = skip_sum + grad[a] * conv_buf[a, at, :]
        lane = lax.broadcasted_iota(jnp.int32, (group_rows, 128), 1)
        placed = jnp.zeros((group_rows, 128), F32)
        for j, each in enumerate(sums + [skip_sum]):
            total = jnp.sum(each, axis=1, keepdims=True) * np.float32(scale)
            placed = jnp.where(lane == j, total, placed)
        small_buf[at, :] = placed

    small_buf[...] = jnp.zeros_like(small_buf)
    for i, part in enumerate(late):
        for h in range(halves):
            grad_moves[h][i][1]()
        over_rows(forward_rows(grad_buf), part)
        dft(plain, grad_spec, part)
        dft(product(val_spec, grad_spec, True), work, part)
        over_rows(filter_rows, part)
        gfil_moves[i][0]()
        dft(product(fil_spec, grad_spec, True), work, part)
        over_rows(value_rows, part)
        if i == len(late) - 1:
            small_send[...] = small_buf[...].T[:8, :]
            small_start()
        gsig_moves[i][0]()
        if i == (len(late) - 1) // 2:
            gate_part()

    for where, copy in line_copies:
        @pl.when(where)
        def _():
            copy.wait_send()

    if shared:
        @pl.when(inside)
        def _():
            landed(line_sem.at[0], far_piece(me))
            landed(line_sem.at[1], far_buf.at[pl.ds(0, 2), 0])
            landed(line_sem.at[2], far_buf.at[:, 0])

    for step in range(0 if shared else groups):
        for up in (True, False):
            @pl.when(sends(step, up))
            def _():
                for h in range(halves):
                    hop(step, h, up).wait_send()

    small_arrive()
    per_tile = 128 // rows
    for tile in range(-(-channels // 128)):
        total = None
        for i in range(min(per_tile, devices - tile * per_tile)):
            each = small_land[tile * per_tile + i]
            each = each if i == 0 else pltpu.roll(each, i * rows, 1)
            total = each if total is None else total + each
        width = min(128, channels - tile * 128)
        at = slice(tile * 128, tile * 128 + width)
        taps_buf[:, at] = total[:taps, :width]
        skip_buf[:, at] = total[taps : taps + 1, :width]
    small_stores = [
        pltpu.make_async_copy(source, target, load_sem.at[2 + i])
        for i, (source, target) in enumerate(((taps_buf, tap_out), (skip_buf, skip_out)))
    ]
    for store in small_stores:
        store.start()
    gate_store.wait()
    for store in small_stores:
        store.wait()
    for sent in moves:
        sent()
    for move in gfil_moves + gsig_moves:
        move[1]()


def handed_on(*refs):
    count = (len(refs) - 1) // 3
    loads, stores = [], []
    for source, result, held in zip(refs[:count], refs[count : 2 * count], refs[2 * count : -1]):
        pieces = 2 if source.shape[0] % 2 == 0 else 1
        size = source.shape[0] // pieces
        for piece in range(pieces):
            at, sems = pl.ds(piece * size, size), refs[-1].at[len(loads)]
            loads.append(pltpu.make_async_copy(source.at[at], held.at[at], sems.at[0]))
            stores.append(pltpu.make_async_copy(held.at[at], result.at[at], sems.at[1]))
    for load in loads:
        load.start()
    for load, store in zip(loads, stores):
        load.wait()
        store.start()
    for store in stores:
        store.wait()


def per_device(signal, gate_in, filter_raw, short_kernel, skip_gain, out_weight, cotangent):
    channels, length = signal.shape
    taps = short_kernel.shape[1]
    devices, groups = lax.axis_size("ctx"), lax.axis_size("chan")
    rows = channels // devices
    rows_pad = max(rows, 8)
    halves = 2
    scale = 1.0 / math.sqrt(length * devices)
    twiddle, high, low = tables(devices, length, scale)
    shape = (devices, rows, length)
    out_rows = cotangent.shape[0]
    early = [(0, rows // 2), (rows // 2, rows // 2)] if rows % 16 == 0 else [(0, rows)]
    late = [(0, rows // 4), (rows // 4, rows // 4), (rows // 2, rows // 2)] if rows % 32 == 0 else [(0, rows)]
    spec_shape = (devices + 1, rows_pad, 2 * length)
    shared = groups == 4 and devices == 8 and len(early) == 2 and len(late) == 3
    far_shape = (4, 2, out_rows // 4, channels) if shared else (1, 2, 8, 128)
    half_shape = (devices, rows, length // 2) if shared else (1, 8, 128)
    dims = (devices, groups, rows, length, taps, halves, early, late, shared, scale)
    moves = 3 * len(early) + (halves + 2) * len(late) + 1

    def vmem(*size, dtype=F32):
        return pltpu.VMEM(size, dtype)

    in_vmem, anywhere = pl.BlockSpec(memory_space=pltpu.VMEM), pl.BlockSpec(memory_space=pl.ANY)
    block = jax.ShapeDtypeStruct(shape, F32)
    results = (block,) * 3 + tuple(
        jax.ShapeDtypeStruct((count, channels), F32) for count in (taps, 1)
    )
    held = pl.pallas_call(
        functools.partial(kernel, dims),
        out_shape=results,
        in_specs=[anywhere] * 10,
        out_specs=(anywhere,) * 5,
        scratch_shapes=[
            vmem(groups, out_rows, channels),
            vmem(groups, channels, out_rows, dtype=BF16),
            vmem(groups, channels, out_rows, dtype=BF16),
            vmem(groups, out_rows, length),
            vmem(channels, length),
            *[vmem(*shape) for _ in range(10)],
            vmem(devices, rows, 128),
            vmem(128, 128),
            vmem(8, 128),
            vmem(devices, 8, 128),
            *[vmem(*spec_shape) for _ in range(5)],
            vmem(*twiddle.shape),
            vmem(*high.shape, dtype=BF16),
            vmem(*low.shape, dtype=BF16),
            vmem(taps, channels),
            vmem(1, channels),
            vmem(*far_shape),
            vmem(2, channels, out_rows, dtype=BF16) if shared else vmem(8, 128),
            vmem(2, channels, out_rows, dtype=BF16) if shared else vmem(8, 128),
            vmem(*half_shape),
            vmem(*half_shape),
            pltpu.SemaphoreType.DMA((14,) if shared else (halves, groups)),
            pltpu.SemaphoreType.DMA((14,) if shared else (halves, groups)),
            pltpu.SemaphoreType.DMA((6,) if shared else (halves, groups)),
            pltpu.SemaphoreType.DMA((moves,)),
            pltpu.SemaphoreType.DMA((moves,)),
            pltpu.SemaphoreType.DMA((8,)),
        ],
        compiler_params=pltpu.CompilerParams(
            collective_id=0, has_side_effects=True, vmem_limit_bytes=56 * 2**20
        ),
    )(
        signal.reshape(shape),
        gate_in.reshape(shape),
        filter_raw.reshape(shape),
        short_kernel.T,
        skip_gain[None, :],
        out_weight.reshape(groups, out_rows, channels),
        cotangent,
        jnp.asarray(twiddle),
        jnp.asarray(high),
        jnp.asarray(low),
    )
    grad_gate, grad_signal, grad_filter, grad_kernel, grad_skip = pl.pallas_call(
        handed_on,
        out_shape=results,
        in_specs=[anywhere] * 5,
        out_specs=(anywhere,) * 5,
        scratch_shapes=[vmem(*each.shape) for each in results]
        + [pltpu.SemaphoreType.DMA((8, 2))],
    )(*held)
    whole = (channels, length)
    return (
        grad_gate.reshape(whole),
        grad_signal.reshape(whole),
        grad_filter.reshape(whole),
        grad_kernel.T,
        grad_skip[0],
    )


def solution(mesh):
    placed = (
        P("chan", "ctx"),
        P("chan", "ctx"),
        P("chan", "ctx"),
        P("chan", None),
        P("chan"),
        P(None, "chan"),
        P("chan", "ctx"),
    )
    return jax.shard_map(
        per_device,
        mesh=mesh,
        in_specs=placed,
        out_specs=(
            P("chan", "ctx"),
            P("chan", "ctx"),
            P("chan", "ctx"),
            P("chan", None),
            P("chan"),
        ),
        check_vma=False,
    )
```

```python
import functools
import math

import jax
import jax.numpy as jnp
import numpy as np
from jax import lax
from jax.experimental import pallas as pl
from jax.experimental.pallas import tpu as pltpu
from jax.sharding import PartitionSpec as P

MESH = pl.DeviceIdType.MESH
F32 = jnp.float32
BF16 = jnp.bfloat16


def split_bf16(value):
    high = value.astype(BF16)
    return high, (value - high.astype(F32)).astype(BF16)


def tables(blocks, length, scale):
    total = 2 * blocks * length
    turn = np.arange(blocks + 1)[:, None] * np.arange(length)[None, :] % total
    angle = 2.0 * np.pi / total * turn
    weight = np.full((blocks + 1, 1), 2.0)
    weight[0] = weight[blocks] = 1.0
    weight = weight * (scale / total)
    twiddle = np.stack(
        (np.cos(angle), np.sin(angle), weight * np.cos(angle), weight * np.sin(angle))
    ).astype(np.float32)
    turn = np.arange(length)[:, None] * np.arange(length)[None, :] % length
    angle = 2.0 * np.pi / length * turn
    cosine, sine = np.cos(angle), np.sin(angle)
    matrix = np.block([[cosine, -sine], [sine, cosine]]).astype(np.float32)
    high = matrix.astype(jnp.bfloat16)
    low = (matrix - high.astype(np.float32)).astype(jnp.bfloat16)
    return twiddle, high, low


def weighted_sum(terms):
    total = None
    for factor, value in terms:
        if abs(factor) < 1e-12:
            continue
        if abs(factor - 1.0) < 1e-12:
            part = value
        elif abs(factor + 1.0) < 1e-12:
            part = -value
        else:
            part = np.float32(factor) * value
        total = part if total is None else total + part
    return total


def forward_blocks(parts, twiddle, store):
    blocks = len(parts)

    def put(q, real, imag):
        cosine, sine = twiddle[0, q : q + 1, :], twiddle[1, q : q + 1, :]
        if imag is None:
            store(q, real * cosine, -real * sine)
        else:
            store(q, real * cosine + imag * sine, imag * cosine - real * sine)

    for q in range(blocks // 2 + 1):
        def gather(first, trig, sign):
            return weighted_sum(
                [(sign * trig(math.pi * a * q / blocks), parts[a]) for a in range(first, blocks, 2)]
            )

        even_re, even_im = gather(0, math.cos, 1.0), gather(0, math.sin, -1.0)
        odd_re, odd_im = gather(1, math.cos, 1.0), gather(1, math.sin, -1.0)

        def add(a, b, sign_a, sign_b):
            return weighted_sum([(s, v) for s, v in ((sign_a, a), (sign_b, b)) if v is not None])

        put(q, add(even_re, odd_re, 1.0, 1.0), add(even_im, odd_im, 1.0, 1.0))
        if q != blocks - q:
            put(blocks - q, add(even_re, odd_re, 1.0, -1.0), add(even_im, odd_im, -1.0, 1.0))


def inverse_blocks(blocks, length, twiddle, load):
    def real_imag(q):
        pair = load(q)
        real, minus = pair[:, :length], pair[:, length:]
        cosine, sine = twiddle[2, q : q + 1, :], twiddle[3, q : q + 1, :]
        return real * cosine + minus * sine, real * sine - minus * cosine

    first, last = real_imag(0)[0], real_imag(blocks)[0]
    half_re, half_im = real_imag(blocks // 2)
    pairs = []
    for q in range(1, blocks // 2):
        (re_a, im_a), (re_b, im_b) = real_imag(q), real_imag(blocks - q)
        pairs.append((re_a + re_b, im_a - im_b, re_a - re_b, im_a + im_b))
    result = []
    for a in range(blocks):
        odd = a % 2
        terms = [(1.0, first - last if odd else first + last)]
        terms.append((math.cos(math.pi * a / 2), half_re))
        terms.append((-math.sin(math.pi * a / 2), half_im))
        for q in range(1, blocks // 2):
            angle = math.pi * a * q / blocks
            terms.append((math.cos(angle), pairs[q - 1][2 * odd]))
            terms.append((-math.sin(angle), pairs[q - 1][2 * odd + 1]))
        result.append(weighted_sum(terms))
    return result


def kernel(
    dims,
    sig_in, gate_in, fil_in, taps_in, skip_in, w_in, cot_in, twiddle_in, high_in, low_in,
    gate_out, gsig_out, gfil_out, tap_out, skip_out,
    w_buf, wt_hi, wt_lo, cot_all, mix, gate_buf, sig_buf, fil_buf, conv_buf,
    resp_send, resp_buf, grad_send, grad_buf, gsig_send, gfil_send, taps_ref, small_buf, small_send, small_land,
    stage, fil_spec, val_spec, grad_spec, work, twiddle, high_ref, low_ref, taps_buf, skip_buf,
    far_buf, far_hi, far_lo, part_send, part_buf,
    up_sem, down_sem, line_sem, send_sem, recv_sem, load_sem,
):
    devices, groups, rows, length, taps, halves, early, late, shared, scale = dims
    me, chan = lax.axis_index("ctx"), lax.axis_index("chan")
    half_len = length // halves
    group_rows = min(8, rows)
    classes = devices + 1

    barrier = pltpu.get_barrier_semaphore()

    @pl.loop(1, devices)
    def _(k):
        pl.semaphore_signal(
            barrier, inc=1, device_id={"ctx": lax.rem(me + k, devices)}, device_id_type=MESH
        )

    for inside, other in ((chan + 1 < groups, chan + 1), (chan >= 1, chan - 1)):
        @pl.when(inside)
        def _():
            pl.semaphore_signal(barrier, inc=1, device_id={"chan": other}, device_id_type=MESH)

    w_copy = pltpu.make_async_copy(w_in, w_buf, load_sem.at[0])
    gate_copy = pltpu.make_async_copy(gate_in, gate_buf, load_sem.at[1])
    cot_copy = pltpu.make_async_copy(cot_in, cot_all.at[chan], load_sem.at[2])
    table_copies = [
        pltpu.make_async_copy(source, target, load_sem.at[3 + i])
        for i, (source, target) in enumerate(
            (
                (taps_in, taps_buf), (skip_in, skip_buf), (twiddle_in, twiddle),
                (high_in, high_ref), (low_in, low_ref),
            )
        )
    ]
    w_copy.start()
    cot_copy.start()
    for copy in table_copies:
        copy.start()
    gate_copy.start()

    beside = (chan + 1 < groups).astype(jnp.int32) + (chan >= 1).astype(jnp.int32)
    pl.semaphore_wait(barrier, devices - 1 + beside)

    def lanes(h):
        return pl.ds(h * half_len, half_len)

    def hop(step, h, up):
        block = chan - step if up else chan + step
        source = cot_in if step == 0 else cot_all.at[block]
        sems = up_sem if up else down_sem
        return pltpu.make_async_remote_copy(
            src_ref=source.at[:, lanes(h)],
            dst_ref=cot_all.at[block, :, lanes(h)],
            send_sem=sems.at[h, step],
            recv_sem=line_sem.at[h, block],
            device_id={"chan": chan + 1 if up else chan - 1},
            device_id_type=MESH,
        )

    def sends(step, up):
        if up:
            return jnp.logical_and(chan - step >= 0, chan + 1 < groups)
        return jnp.logical_and(chan + step < groups, chan >= 1)

    def arrives(step, up):
        return chan - step >= 0 if up else chan + step < groups

    def line_start(step, h):
        for up in (True, False):
            @pl.when(sends(step, up))
            def _():
                hop(step, h, up).start()

    def line_arrive(step, h):
        for up in (True, False):
            @pl.when(arrives(step, up))
            def _():
                block = chan - step if up else chan + step
                slot = cot_all.at[block, :, lanes(h)]
                pltpu.make_async_remote_copy(
                    src_ref=slot,
                    dst_ref=slot,
                    send_sem=up_sem.at[h, step],
                    recv_sem=line_sem.at[h, block],
                    device_id={"chan": chan - 1 if up else chan + 1},
                    device_id_type=MESH,
                ).wait_recv()

                @pl.when(sends(step, up))
                def _():
                    hop(step, h, up).start()

    moves = []

    def all_to_all(source, target, landed):
        index = len(moves)

        def start():
            @pl.loop(1, devices)
            def _(k):
                peer = lax.rem(me + k, devices)
                pltpu.make_async_remote_copy(
                    src_ref=source(peer),
                    dst_ref=target(me),
                    send_sem=send_sem.at[index],
                    recv_sem=recv_sem.at[index],
                    device_id={"ctx": peer},
                    device_id_type=MESH,
                ).start()

            pltpu.make_async_copy(source(me), target(me), recv_sem.at[index]).start()

        def arrive():
            everything = landed(devices)
            pltpu.make_async_copy(everything, everything, recv_sem.at[index]).wait()

        def sent():
            others = landed(devices - 1)
            pltpu.make_async_copy(others, others, send_sem.at[index]).wait()

        moves.append(sent)
        return start, arrive

    def by_part(source, target, part, lane=slice(None)):
        at = pl.ds(*part)
        return all_to_all(
            lambda p: source.at[p, at, lane],
            lambda p: target.at[p, at, lane],
            lambda n: target.at[pl.ds(0, n), at, lane],
        )

    sig_moves = [by_part(sig_in, sig_buf, part) for part in early]
    fil_moves = [by_part(fil_in, fil_buf, part) for part in early]
    resp_moves = [by_part(resp_send, resp_buf, part) for part in early]
    grad_moves = [
        [by_part(grad_send, grad_buf, part, lanes(h)) for part in late] for h in range(halves)
    ]
    gfil_moves = [by_part(gfil_send, gfil_out, part) for part in late]
    gsig_moves = [by_part(gsig_send, gsig_out, part) for part in late]
    small_start, small_arrive = all_to_all(
        lambda p: small_send, lambda p: small_land.at[p], lambda n: small_land.at[pl.ds(0, n)]
    )

    side = chan // 2
    edge, near, far, last = 3 * side, 1 + side, 2 - side, 3 - 3 * side
    on_edge, inside = chan % 3 == 0, chan % 3 != 0
    core = me % 2
    across_x, across_y = me + 2 - 4 * (me // 2 % 2), me + 4 - 8 * (me // 4)
    first_peer = (1 - core) * across_x + core * across_y
    second_peer = (1 - core) * across_y + core * across_x
    sibling, opposite = me + 1 - 2 * core, across_x + across_y - me
    line_copies = []

    def line_copy(index, where, source, target, other):
        copy = pltpu.make_async_remote_copy(
            src_ref=source,
            dst_ref=target,
            send_sem=up_sem.at[index],
            recv_sem=down_sem.at[index],
            device_id={"chan": other},
            device_id_type=MESH,
        )
        line_copies.append((where, copy))
        return copy

    half_rows = cot_all.shape[1] // 2

    def half_block(index, where, block, h, other, own=False, q=None):
        at = slice(None) if q is None else pl.ds(q * half_rows, half_rows)
        slot = cot_all.at[block, at, lanes(h)]
        return line_copy(index, where, cot_in.at[at, lanes(h)] if own else slot, slot, other)

    def landed(sem, ref):
        pltpu.make_async_copy(ref, ref, sem).wait()

    def half_landed(index, block, h, q=None):
        at = slice(None) if q is None else pl.ds(q * half_rows, half_rows)
        landed(down_sem.at[index], cot_all.at[block, at, lanes(h)])

    def far_piece(index):
        return far_buf.at[index // 2, index % 2]

    def far_copy(source, send, recv, peer):
        return pltpu.make_async_remote_copy(
            src_ref=source,
            dst_ref=source,
            send_sem=line_sem.at[send],
            recv_sem=line_sem.at[recv],
            device_id={"ctx": peer},
            device_id_type=MESH,
        )

    if shared:
        piece_rows = far_buf.shape[2]
        per_block = devices // 2
        piece_at = pl.ds(pl.multiple_of(me % per_block * piece_rows, piece_rows), piece_rows)
        weight_copy = line_copy(
            0, on_edge,
            w_in.at[far + (last - far) * (me // per_block), piece_at],
            far_piece(me), near,
        )
        edge_out = [
            half_block(1 + 2 * h + q, on_edge, edge, h, near, own=True, q=q)
            for h in range(2)
            for q in range(2)
        ]
        near_to_edge = [half_block(5 + h, inside, near, h, edge, own=True) for h in range(2)]
        near_to_far = [half_block(7 + h, inside, near, h, far, own=True) for h in range(2)]
        far_to_edge = half_block(9, inside, far, 0, edge)
        edge_to_far = [
            half_block(10 + 2 * h + q, inside, edge, h, far, q=q)
            for h in range(2)
            for q in range(2)
        ]
        last_to_edge = [half_block(14 + q, inside, last, 0, edge, q=q) for q in range(2)]

        def pass_edge(h, q):
            half_landed(1 + 2 * h + q, edge, h, q)
            edge_to_far[2 * h + q].start()

        def pass_last(q):
            half_landed(10 + q, last, 0, q)
            last_to_edge[q].start()

        pieces = late
        part_copies = [
            line_copy(16 + i, inside, part_send.at[:, pl.ds(*p)], part_buf.at[:, pl.ds(*p)], edge)
            for i, p in enumerate(pieces)
        ]

        @pl.when(on_edge)
        def _():
            weight_copy.start()
            for copy in edge_out:
                copy.start()

        @pl.when(inside)
        def _():
            for h in range(2):
                near_to_edge[h].start()
                near_to_far[h].start()

        sig_moves[0][0]()
        fil_moves[0][0]()
    else:
        for h in range(halves):
            line_start(0, h)
        for sig_move, fil_move in zip(sig_moves, fil_moves):
            sig_move[0]()
            fil_move[0]()

    def dft(read, target, part):
        span = max(part[1], 8)
        at = (slice(None), slice(part[0], part[0] + span))
        high, low = split_bf16(read(at).reshape(classes * span, 2 * length))
        result = jnp.dot(high, low_ref[...], preferred_element_type=F32)
        result = result + jnp.dot(low, high_ref[...], preferred_element_type=F32)
        result = result + jnp.dot(high, high_ref[...], preferred_element_type=F32)
        target[at] = result.reshape(classes, span, 2 * length)

    def plain(at):
        return stage[at]

    def product(first, second, conjugate):
        def read(at):
            a_re, a_im = first[at][:, :, :length], first[at][:, :, length:]
            b_re, b_im = second[at][:, :, :length], second[at][:, :, length:]
            if conjugate:
                real, minus = a_re * b_re + a_im * b_im, a_im * b_re - a_re * b_im
            else:
                real, minus = a_re * b_re - a_im * b_im, -(a_re * b_im + a_im * b_re)
            return jnp.concatenate((real, minus), axis=2)

        return read

    def over_rows(body, part):
        first = part[0] // group_rows

        @pl.loop(first, first + part[1] // group_rows)
        def _(r):
            body(pl.ds(pl.multiple_of(r * group_rows, group_rows), group_rows))

    def stage_store(at):
        def store(q, real, imag):
            stage[q, at, :length] = real
            stage[q, at, length:] = imag

        return store

    def tap_rows(at):
        return taps_ref[me, at, :]

    def delayed(parts, a, j):
        if j == 0:
            return parts[a]
        before = jnp.zeros_like(parts[a][:, :128]) if a == 0 else parts[a - 1][:, length - 128 :]
        joined = jnp.concatenate((before, parts[a]), axis=1)
        return pltpu.roll(joined, j, 1)[:, 128:]

    def advanced(parts, a, j):
        if j == 0:
            return parts[a]
        after = jnp.zeros_like(parts[a][:, :128]) if a == devices - 1 else parts[a + 1][:, :128]
        joined = jnp.concatenate((parts[a], after), axis=1)
        return pltpu.roll(joined, length + 128 - j, 1)[:, :length]

    w_copy.wait()

    @pl.loop(0, groups)
    def _(g):
        turned = w_buf[g].T
        high, low = split_bf16(turned)
        wt_hi[g] = high
        wt_lo[g] = low

    cot_copy.wait()
    for copy in table_copies:
        copy.wait()

    channels = devices * rows
    table = jnp.concatenate(
        (taps_buf[...], skip_buf[...], jnp.zeros((128 - taps - 1, channels), F32)), axis=0
    )
    table = table.T
    for d in range(devices):
        taps_ref[d] = table[d * rows : (d + 1) * rows, :]

    def mix_add(block, h, first):
        high, low = split_bf16(cot_all[block, :, h * half_len : (h + 1) * half_len])
        result = jnp.dot(wt_lo[block], high, preferred_element_type=F32)
        result = result + jnp.dot(wt_hi[block], low, preferred_element_type=F32)
        result = result + jnp.dot(wt_hi[block], high, preferred_element_type=F32)
        at = (slice(None), slice(h * half_len, (h + 1) * half_len))
        mix[at] = result if first else mix[at] + result

    def mix_step(step, h):
        for up in (True, False):
            @pl.when(arrives(step, up))
            def _():
                mix_add(chan - step if up else chan + step, h, False)

    for h in range(halves):
        mix_add(chan, h, True)

    def conv_rows(at):
        tap = tap_rows(at)
        parts = [sig_buf[a, at, :] for a in range(devices)]
        conv = []
        for a in range(devices):
            total = tap[:, :1] * parts[a]
            for j in range(1, taps):
                total = total + tap[:, j : j + 1] * delayed(parts, a, j)
            conv_buf[a, at, :] = total
            conv.append(total)
        forward_blocks(conv, twiddle, stage_store(at))

    def forward_rows(source):
        def body(at):
            forward_blocks(
                [source[a, at, :] for a in range(devices)], twiddle, stage_store(at)
            )

        return body

    def resp_rows(at):
        skip = tap_rows(at)[:, taps : taps + 1]
        conv = inverse_blocks(devices, length, twiddle, lambda q: work[q, at, :])
        for a in range(devices):
            resp_send[a, at, :] = conv[a] + skip * conv_buf[a, at, :]

    def value_part(i):
        sig_moves[i][1]()
        over_rows(conv_rows, early[i])
        dft(plain, val_spec, early[i])

    def filter_part(i):
        fil_moves[i][1]()
        over_rows(forward_rows(fil_buf), early[i])
        dft(plain, fil_spec, early[i])

    def resp_part(i):
        dft(product(fil_spec, val_spec, False), work, early[i])
        over_rows(resp_rows, early[i])

    def grad_rows(h, first, count):
        here = slice(h * half_len, (h + 1) * half_len)
        for d in range(devices):
            at = slice(d * rows + first, d * rows + first + count)
            grad_send[d, first : first + count, here] = (
                mix[at, here] * gate_buf[d, first : first + count, here]
            )

    def grad_piece(i):
        first, count = pieces[i]
        grad_rows(1, first, count)
        grad_moves[1][i][0]()

    def partial(j, block, sent):
        high, low = split_bf16(cot_all[block, :, half_len:])
        for i, (first, count) in enumerate(pieces):
            at = slice(devices * first, devices * (first + count))
            result = jnp.dot(far_lo[j, at, :], high, preferred_element_type=F32)
            result = result + jnp.dot(far_hi[j, at, :], low, preferred_element_type=F32)
            result = result + jnp.dot(far_hi[j, at, :], high, preferred_element_type=F32)
            result = result.reshape(devices, count, half_len)
            at = (slice(None), slice(first, first + count))
            part_send[at] = part_send[at] + result if j else result
            if sent:
                part_copies[i].start()

    if shared:
        value_part(0)

        @pl.when(inside)
        def _():
            landed(down_sem.at[0], far_piece(me))
            far_copy(far_piece(me), 0, 3, first_peer).start()
            far_copy(far_piece(me), 1, 4, second_peer).start()

        filter_part(0)

        @pl.when(inside)
        def _():
            half_landed(7, far, 0)
            far_to_edge.start()

        resp_part(0)

        @pl.when(inside)
        def _():
            pass_edge(0, 0)
            landed(line_sem.at[3], far_piece(first_peer))
            far_copy(far_piece(first_peer), 1, 4, second_peer).start()
            for index in (me, first_peer):
                far_copy(far_piece(index), 2, 5, sibling).start()

        def start_rest():
            for i in range(1, len(early)):
                fil_moves[i][0]()
            resp_moves[0][0]()

        for i in range(1, len(early)):
            sig_moves[i][0]()
        pl.when(on_edge)(start_rest)

        @pl.when(on_edge)
        def _():
            for h in range(2):
                half_landed(5 + h, near, h)
                mix_add(near, h, False)

        @pl.when(inside)
        def _():
            pass_edge(0, 1)
            mix_add(far, 0, False)
            half_landed(8, far, 1)
            mix_add(far, 1, False)
            pass_edge(1, 0)
            pass_last(0)
            pass_edge(1, 1)
            landed(line_sem.at[4], far_buf.at[pl.ds(0, 2), 0])
            for index in (second_peer, opposite):
                far_copy(far_piece(index), 2, 5, sibling).start()
            start_rest()
            pass_last(1)
            mix_add(edge, 0, False)
            mix_add(last, 0, False)
            mix_add(edge, 1, False)

        gate_copy.wait()

        def first_grads():
            grad_rows(0, 0, rows)
            for move in grad_moves[0]:
                move[0]()

        @pl.when(on_edge)
        def _():
            half_landed(9, far, 0)
            mix_add(far, 0, False)

        @pl.when(inside)
        def _():
            first_grads()
            landed(line_sem.at[5], far_buf.at[:, 1 - core])

            @pl.loop(0, 2)
            def _(j):
                block = far_buf[pl.ds(j * (per_block // 2), per_block // 2)]
                turned = block.reshape(block.shape[0] * 2 * piece_rows, -1).T
                turned = turned.reshape(devices, rows, -1)
                for first, count in pieces:
                    high, low = split_bf16(
                        turned[:, first : first + count, :].reshape(devices * count, -1)
                    )
                    at = slice(devices * first, devices * (first + count))
                    far_hi[j, at, :] = high
                    far_lo[j, at, :] = low

            partial(0, far, False)
            for q in range(2):
                half_landed(12 + q, last, 1, q)
            partial(1, last, True)
            mix_add(last, 1, False)
            for i in range(len(pieces)):
                grad_piece(i)

        for i in range(1, len(early)):
            value_part(i)
            filter_part(i)
            resp_part(i)
            resp_moves[i][0]()

        @pl.when(on_edge)
        def _():
            for q in range(2):
                half_landed(14 + q, last, 0, q)
            mix_add(last, 0, False)
            first_grads()
            for i, (first, count) in enumerate(pieces):
                landed(down_sem.at[16 + i], part_buf.at[:, pl.ds(first, count)])
                for d in range(devices):
                    at = slice(d * rows + first, d * rows + first + count)
                    mix[at, half_len:] = mix[at, half_len:] + part_buf[d, first : first + count, :]
                grad_piece(i)

    else:
        for i, part in enumerate(early):
            value_part(i)
            filter_part(i)
            if groups > 1 and i == 0:
                line_arrive(1, 0)
            resp_part(i)
            resp_moves[i][0]()
            if groups > 1 and i == 0:
                for h in range(1, halves):
                    line_arrive(1, h)
        if groups > 1:
            for h in range(halves):
                mix_step(1, h)
        gate_copy.wait()
        for h in range(halves):
            for step in range(2, groups):
                line_arrive(step, h)
                mix_step(step, h)
            grad_rows(h, 0, rows)
            for move in grad_moves[h]:
                move[0]()

    def gate_part():
        for move in resp_moves:
            move[1]()
        for d in range(devices):
            gate_buf[d] = mix[d * rows : (d + 1) * rows, :] * resp_buf[d]
        gate_store.start()

    gate_store = pltpu.make_async_copy(gate_buf, gate_out, load_sem.at[1])

    def filter_rows(at):
        parts = inverse_blocks(devices, length, twiddle, lambda q: work[q, at, :])
        for a in range(devices):
            gfil_send[a, at, :] = parts[a]

    def value_rows(at):
        tap = tap_rows(at)
        skip = tap[:, taps : taps + 1]
        value = inverse_blocks(devices, length, twiddle, lambda q: work[q, at, :])
        grad = [grad_buf[a, at, :] for a in range(devices)]
        value = [value[a] + skip * grad[a] for a in range(devices)]
        sums = [None] * taps
        for a in range(devices):
            signal = sig_buf[a, at, :]
            total = None
            for j in range(taps):
                ahead = advanced(value, a, j)
                term, part_sum = tap[:, j : j + 1] * ahead, ahead * signal
                total = term if total is None else total + term
                sums[j] = part_sum if sums[j] is None else sums[j] + part_sum
            gsig_send[a, at, :] = total
        skip_sum = grad[0] * conv_buf[0, at, :]
        for a in range(1, devices):
            skip_sum = skip_sum + grad[a] * conv_buf[a, at, :]
        lane = lax.broadcasted_iota(jnp.int32, (group_rows, 128), 1)
        placed = jnp.zeros((group_rows, 128), F32)
        for j, each in enumerate(sums + [skip_sum]):
            total = jnp.sum(each, axis=1, keepdims=True) * np.float32(scale)
            placed = jnp.where(lane == j, total, placed)
        small_buf[at, :] = placed

    small_buf[...] = jnp.zeros_like(small_buf)
    for i, part in enumerate(late):
        for h in range(halves):
            grad_moves[h][i][1]()
        over_rows(forward_rows(grad_buf), part)
        dft(plain, grad_spec, part)
        dft(product(val_spec, grad_spec, True), work, part)
        over_rows(filter_rows, part)
        gfil_moves[i][0]()
        dft(product(fil_spec, grad_spec, True), work, part)
        over_rows(value_rows, part)
        if i == len(late) - 1:
            small_send[...] = small_buf[...].T[:8, :]
            small_start()
        gsig_moves[i][0]()
        if i == (len(late) - 1) // 2:
            gate_part()

    for where, copy in line_copies:
        @pl.when(where)
        def _():
            copy.wait_send()

    if shared:
        @pl.when(inside)
        def _():
            landed(line_sem.at[0], far_piece(me))
            landed(line_sem.at[1], far_buf.at[pl.ds(0, 2), 0])
            landed(line_sem.at[2], far_buf.at[:, 0])

    for step in range(0 if shared else groups):
        for up in (True, False):
            @pl.when(sends(step, up))
            def _():
                for h in range(halves):
                    hop(step, h, up).wait_send()

    small_arrive()
    per_tile = 128 // rows
    for tile in range(-(-channels // 128)):
        total = None
        for i in range(min(per_tile, devices - tile * per_tile)):
            each = small_land[tile * per_tile + i]
            each = each if i == 0 else pltpu.roll(each, i * rows, 1)
            total = each if total is None else total + each
        width = min(128, channels - tile * 128)
        at = slice(tile * 128, tile * 128 + width)
        taps_buf[:, at] = total[:taps, :width]
        skip_buf[:, at] = total[taps : taps + 1, :width]
    small_stores = [
        pltpu.make_async_copy(source, target, load_sem.at[2 + i])
        for i, (source, target) in enumerate(((taps_buf, tap_out), (skip_buf, skip_out)))
    ]
    for store in small_stores:
        store.start()
    gate_store.wait()
    for store in small_stores:
        store.wait()
    for sent in moves:
        sent()
    for move in gfil_moves + gsig_moves:
        move[1]()


def handed_on(*refs):
    count = (len(refs) - 1) // 3
    loads, stores = [], []
    for source, result, held in zip(refs[:count], refs[count : 2 * count], refs[2 * count : -1]):
        pieces = 2 if source.shape[0] % 2 == 0 else 1
        size = source.shape[0] // pieces
        for piece in range(pieces):
            at, sems = pl.ds(piece * size, size), refs[-1].at[len(loads)]
            loads.append(pltpu.make_async_copy(source.at[at], held.at[at], sems.at[0]))
            stores.append(pltpu.make_async_copy(held.at[at], result.at[at], sems.at[1]))
    for load in loads:
        load.start()
    for load, store in zip(loads, stores):
        load.wait()
        store.start()
    for store in stores:
        store.wait()


def per_device(signal, gate_in, filter_raw, short_kernel, skip_gain, out_weight, cotangent):
    channels, length = signal.shape
    taps = short_kernel.shape[1]
    devices, groups = lax.axis_size("ctx"), lax.axis_size("chan")
    rows = channels // devices
    rows_pad = max(rows, 8)
    halves = 2
    scale = 1.0 / math.sqrt(length * devices)
    twiddle, high, low = tables(devices, length, scale)
    shape = (devices, rows, length)
    out_rows = cotangent.shape[0]
    early = [(0, rows // 2), (rows // 2, rows // 2)] if rows % 16 == 0 else [(0, rows)]
    late = [(0, rows // 4), (rows // 4, rows // 4), (rows // 2, rows // 2)] if rows % 32 == 0 else [(0, rows)]
    spec_shape = (devices + 1, rows_pad, 2 * length)
    shared = groups == 4 and devices == 8 and len(early) == 2 and len(late) == 3
    far_shape = (4, 2, out_rows // 4, channels) if shared else (1, 2, 8, 128)
    half_shape = (devices, rows, length // 2) if shared else (1, 8, 128)
    dims = (devices, groups, rows, length, taps, halves, early, late, shared, scale)
    moves = 3 * len(early) + (halves + 2) * len(late) + 1

    def vmem(*size, dtype=F32):
        return pltpu.VMEM(size, dtype)

    in_vmem, anywhere = pl.BlockSpec(memory_space=pltpu.VMEM), pl.BlockSpec(memory_space=pl.ANY)
    block = jax.ShapeDtypeStruct(shape, F32)
    results = (block,) * 3 + tuple(
        jax.ShapeDtypeStruct((count, channels), F32) for count in (taps, 1)
    )
    held = pl.pallas_call(
        functools.partial(kernel, dims),
        out_shape=results,
        in_specs=[anywhere] * 10,
        out_specs=(anywhere,) * 5,
        scratch_shapes=[
            vmem(groups, out_rows, channels),
            vmem(groups, channels, out_rows, dtype=BF16),
            vmem(groups, channels, out_rows, dtype=BF16),
            vmem(groups, out_rows, length),
            vmem(channels, length),
            *[vmem(*shape) for _ in range(10)],
            vmem(devices, rows, 128),
            vmem(128, 128),
            vmem(8, 128),
            vmem(devices, 8, 128),
            *[vmem(*spec_shape) for _ in range(5)],
            vmem(*twiddle.shape),
            vmem(*high.shape, dtype=BF16),
            vmem(*low.shape, dtype=BF16),
            vmem(taps, channels),
            vmem(1, channels),
            vmem(*far_shape),
            vmem(2, channels, out_rows, dtype=BF16) if shared else vmem(8, 128),
            vmem(2, channels, out_rows, dtype=BF16) if shared else vmem(8, 128),
            vmem(*half_shape),
            vmem(*half_shape),
            pltpu.SemaphoreType.DMA((19,) if shared else (halves, groups)),
            pltpu.SemaphoreType.DMA((19,) if shared else (halves, groups)),
            pltpu.SemaphoreType.DMA((6,) if shared else (halves, groups)),
            pltpu.SemaphoreType.DMA((moves,)),
            pltpu.SemaphoreType.DMA((moves,)),
            pltpu.SemaphoreType.DMA((8,)),
        ],
        compiler_params=pltpu.CompilerParams(
            collective_id=0, has_side_effects=True, vmem_limit_bytes=56 * 2**20
        ),
    )(
        signal.reshape(shape),
        gate_in.reshape(shape),
        filter_raw.reshape(shape),
        short_kernel.T,
        skip_gain[None, :],
        out_weight.reshape(groups, out_rows, channels),
        cotangent,
        jnp.asarray(twiddle),
        jnp.asarray(high),
        jnp.asarray(low),
    )
    grad_gate, grad_signal, grad_filter, grad_kernel, grad_skip = pl.pallas_call(
        handed_on,
        out_shape=results,
        in_specs=[anywhere] * 5,
        out_specs=(anywhere,) * 5,
        scratch_shapes=[vmem(*each.shape) for each in results]
        + [pltpu.SemaphoreType.DMA((8, 2))],
    )(*held)
    whole = (channels, length)
    return (
        grad_gate.reshape(whole),
        grad_signal.reshape(whole),
        grad_filter.reshape(whole),
        grad_kernel.T,
        grad_skip[0],
    )


def solution(mesh):
    placed = (
        P("chan", "ctx"),
        P("chan", "ctx"),
        P("chan", "ctx"),
        P("chan", None),
        P("chan"),
        P(None, "chan"),
        P("chan", "ctx"),
    )
    return jax.shard_map(
        per_device,
        mesh=mesh,
        in_specs=placed,
        out_specs=(
            P("chan", "ctx"),
            P("chan", "ctx"),
            P("chan", "ctx"),
            P("chan", None),
            P("chan"),
        ),
        check_vma=False,
    )
```

```python
import functools
import math

import jax
import jax.numpy as jnp
import numpy as np
from jax import lax
from jax.experimental import pallas as pl
from jax.experimental.pallas import tpu as pltpu
from jax.sharding import PartitionSpec as P

MESH = pl.DeviceIdType.MESH
F32 = jnp.float32
BF16 = jnp.bfloat16


def split_bf16(value):
    high = value.astype(BF16)
    return high, (value - high.astype(F32)).astype(BF16)


def tables(blocks, length, scale):
    total = 2 * blocks * length
    turn = np.arange(blocks + 1)[:, None] * np.arange(length)[None, :] % total
    angle = 2.0 * np.pi / total * turn
    weight = np.full((blocks + 1, 1), 2.0)
    weight[0] = weight[blocks] = 1.0
    weight = weight * (scale / total)
    twiddle = np.stack(
        (np.cos(angle), np.sin(angle), weight * np.cos(angle), weight * np.sin(angle))
    ).astype(np.float32)
    turn = np.arange(length)[:, None] * np.arange(length)[None, :] % length
    angle = 2.0 * np.pi / length * turn
    cosine, sine = np.cos(angle), np.sin(angle)
    matrix = np.block([[cosine, -sine], [sine, cosine]]).astype(np.float32)
    high = matrix.astype(jnp.bfloat16)
    low = (matrix - high.astype(np.float32)).astype(jnp.bfloat16)
    return twiddle, high, low


def weighted_sum(terms):
    total = None
    for factor, value in terms:
        if abs(factor) < 1e-12:
            continue
        if abs(factor - 1.0) < 1e-12:
            part = value
        elif abs(factor + 1.0) < 1e-12:
            part = -value
        else:
            part = np.float32(factor) * value
        total = part if total is None else total + part
    return total


def forward_blocks(parts, twiddle, store):
    blocks = len(parts)

    def put(q, real, imag):
        cosine, sine = twiddle[0, q : q + 1, :], twiddle[1, q : q + 1, :]
        if imag is None:
            store(q, real * cosine, -real * sine)
        else:
            store(q, real * cosine + imag * sine, imag * cosine - real * sine)

    for q in range(blocks // 2 + 1):
        def gather(first, trig, sign):
            return weighted_sum(
                [(sign * trig(math.pi * a * q / blocks), parts[a]) for a in range(first, blocks, 2)]
            )

        even_re, even_im = gather(0, math.cos, 1.0), gather(0, math.sin, -1.0)
        odd_re, odd_im = gather(1, math.cos, 1.0), gather(1, math.sin, -1.0)

        def add(a, b, sign_a, sign_b):
            return weighted_sum([(s, v) for s, v in ((sign_a, a), (sign_b, b)) if v is not None])

        put(q, add(even_re, odd_re, 1.0, 1.0), add(even_im, odd_im, 1.0, 1.0))
        if q != blocks - q:
            put(blocks - q, add(even_re, odd_re, 1.0, -1.0), add(even_im, odd_im, -1.0, 1.0))


def inverse_blocks(blocks, length, twiddle, load):
    def real_imag(q):
        pair = load(q)
        real, minus = pair[:, :length], pair[:, length:]
        cosine, sine = twiddle[2, q : q + 1, :], twiddle[3, q : q + 1, :]
        return real * cosine + minus * sine, real * sine - minus * cosine

    first, last = real_imag(0)[0], real_imag(blocks)[0]
    half_re, half_im = real_imag(blocks // 2)
    pairs = []
    for q in range(1, blocks // 2):
        (re_a, im_a), (re_b, im_b) = real_imag(q), real_imag(blocks - q)
        pairs.append((re_a + re_b, im_a - im_b, re_a - re_b, im_a + im_b))
    result = []
    for a in range(blocks):
        odd = a % 2
        terms = [(1.0, first - last if odd else first + last)]
        terms.append((math.cos(math.pi * a / 2), half_re))
        terms.append((-math.sin(math.pi * a / 2), half_im))
        for q in range(1, blocks // 2):
            angle = math.pi * a * q / blocks
            terms.append((math.cos(angle), pairs[q - 1][2 * odd]))
            terms.append((-math.sin(angle), pairs[q - 1][2 * odd + 1]))
        result.append(weighted_sum(terms))
    return result


def kernel(
    dims,
    sig_in, gate_in, fil_in, taps_in, skip_in, w_in, cot_in, twiddle_in, high_in, low_in,
    gate_out, gsig_out, gfil_out, tap_out, skip_out,
    w_buf, wt_hi, wt_lo, cot_all, mix, gate_buf, sig_buf, fil_buf, conv_buf,
    resp_send, resp_buf, grad_send, grad_buf, gsig_send, gfil_send, taps_ref, small_buf, small_send, small_land,
    stage, fil_spec, val_spec, grad_spec, work, twiddle, high_ref, low_ref, taps_buf, skip_buf,
    far_buf, far_hi, far_lo, part_send, part_buf,
    up_sem, down_sem, line_sem, send_sem, recv_sem, load_sem,
):
    devices, groups, rows, length, taps, halves, early, late, shared, scale = dims
    me, chan = lax.axis_index("ctx"), lax.axis_index("chan")
    half_len = length // halves
    group_rows = min(8, rows)
    classes = devices + 1

    barrier = pltpu.get_barrier_semaphore()

    @pl.loop(1, devices)
    def _(k):
        pl.semaphore_signal(
            barrier, inc=1, device_id={"ctx": lax.rem(me + k, devices)}, device_id_type=MESH
        )

    for inside, other in ((chan + 1 < groups, chan + 1), (chan >= 1, chan - 1)):
        @pl.when(inside)
        def _():
            pl.semaphore_signal(barrier, inc=1, device_id={"chan": other}, device_id_type=MESH)

    w_copy = pltpu.make_async_copy(w_in, w_buf, load_sem.at[0])
    gate_copy = pltpu.make_async_copy(gate_in, gate_buf, load_sem.at[1])
    cot_copy = pltpu.make_async_copy(cot_in, cot_all.at[chan], load_sem.at[2])
    table_copies = [
        pltpu.make_async_copy(source, target, load_sem.at[3 + i])
        for i, (source, target) in enumerate(
            (
                (taps_in, taps_buf), (skip_in, skip_buf), (twiddle_in, twiddle),
                (high_in, high_ref), (low_in, low_ref),
            )
        )
    ]
    w_copy.start()
    cot_copy.start()
    for copy in table_copies:
        copy.start()
    gate_copy.start()

    beside = (chan + 1 < groups).astype(jnp.int32) + (chan >= 1).astype(jnp.int32)
    pl.semaphore_wait(barrier, devices - 1 + beside)

    def lanes(h):
        return pl.ds(h * half_len, half_len)

    def hop(step, h, up):
        block = chan - step if up else chan + step
        source = cot_in if step == 0 else cot_all.at[block]
        sems = up_sem if up else down_sem
        return pltpu.make_async_remote_copy(
            src_ref=source.at[:, lanes(h)],
            dst_ref=cot_all.at[block, :, lanes(h)],
            send_sem=sems.at[h, step],
            recv_sem=line_sem.at[h, block],
            device_id={"chan": chan + 1 if up else chan - 1},
            device_id_type=MESH,
        )

    def sends(step, up):
        if up:
            return jnp.logical_and(chan - step >= 0, chan + 1 < groups)
        return jnp.logical_and(chan + step < groups, chan >= 1)

    def arrives(step, up):
        return chan - step >= 0 if up else chan + step < groups

    def line_start(step, h):
        for up in (True, False):
            @pl.when(sends(step, up))
            def _():
                hop(step, h, up).start()

    def line_arrive(step, h):
        for up in (True, False):
            @pl.when(arrives(step, up))
            def _():
                block = chan - step if up else chan + step
                slot = cot_all.at[block, :, lanes(h)]
                pltpu.make_async_remote_copy(
                    src_ref=slot,
                    dst_ref=slot,
                    send_sem=up_sem.at[h, step],
                    recv_sem=line_sem.at[h, block],
                    device_id={"chan": chan - 1 if up else chan + 1},
                    device_id_type=MESH,
                ).wait_recv()

                @pl.when(sends(step, up))
                def _():
                    hop(step, h, up).start()

    moves = []

    def all_to_all(source, target, landed):
        index = len(moves)

        def start():
            @pl.loop(1, devices)
            def _(k):
                peer = lax.rem(me + k, devices)
                pltpu.make_async_remote_copy(
                    src_ref=source(peer),
                    dst_ref=target(me),
                    send_sem=send_sem.at[index],
                    recv_sem=recv_sem.at[index],
                    device_id={"ctx": peer},
                    device_id_type=MESH,
                ).start()

            pltpu.make_async_copy(source(me), target(me), recv_sem.at[index]).start()

        def arrive():
            everything = landed(devices)
            pltpu.make_async_copy(everything, everything, recv_sem.at[index]).wait()

        def sent():
            others = landed(devices - 1)
            pltpu.make_async_copy(others, others, send_sem.at[index]).wait()

        moves.append(sent)
        return start, arrive

    def by_part(source, target, part, lane=slice(None)):
        at = pl.ds(*part)
        return all_to_all(
            lambda p: source.at[p, at, lane],
            lambda p: target.at[p, at, lane],
            lambda n: target.at[pl.ds(0, n), at, lane],
        )

    sig_moves = [by_part(sig_in, sig_buf, part) for part in early]
    fil_moves = [by_part(fil_in, fil_buf, part) for part in early]
    resp_moves = [by_part(resp_send, resp_buf, part) for part in early]
    grad_moves = [
        [by_part(grad_send, grad_buf, part, lanes(h)) for part in late] for h in range(halves)
    ]
    gfil_moves = [by_part(gfil_send, gfil_out, part) for part in late]
    gsig_moves = [by_part(gsig_send, gsig_out, part) for part in late]
    small_start, small_arrive = all_to_all(
        lambda p: small_send, lambda p: small_land.at[p], lambda n: small_land.at[pl.ds(0, n)]
    )

    side = chan // 2
    edge, near, far, last = 3 * side, 1 + side, 2 - side, 3 - 3 * side
    on_edge, inside = chan % 3 == 0, chan % 3 != 0
    core = me % 2
    across_x, across_y = me + 2 - 4 * (me // 2 % 2), me + 4 - 8 * (me // 4)
    first_peer = (1 - core) * across_x + core * across_y
    second_peer = (1 - core) * across_y + core * across_x
    sibling, opposite = me + 1 - 2 * core, across_x + across_y - me
    line_copies = []

    def line_copy(index, where, source, target, other):
        copy = pltpu.make_async_remote_copy(
            src_ref=source,
            dst_ref=target,
            send_sem=up_sem.at[index],
            recv_sem=down_sem.at[index],
            device_id={"chan": other},
            device_id_type=MESH,
        )
        line_copies.append((where, copy))
        return copy

    half_rows = cot_all.shape[1] // 2

    def half_block(index, where, block, h, other, own=False, q=None):
        at = slice(None) if q is None else pl.ds(q * half_rows, half_rows)
        slot = cot_all.at[block, at, lanes(h)]
        return line_copy(index, where, cot_in.at[at, lanes(h)] if own else slot, slot, other)

    def landed(sem, ref):
        pltpu.make_async_copy(ref, ref, sem).wait()

    def half_landed(index, block, h, q=None):
        at = slice(None) if q is None else pl.ds(q * half_rows, half_rows)
        landed(down_sem.at[index], cot_all.at[block, at, lanes(h)])

    def far_piece(index):
        return far_buf.at[index // 2, index % 2]

    def far_copy(source, send, recv, peer):
        return pltpu.make_async_remote_copy(
            src_ref=source,
            dst_ref=source,
            send_sem=line_sem.at[send],
            recv_sem=line_sem.at[recv],
            device_id={"ctx": peer},
            device_id_type=MESH,
        )

    if shared:
        piece_rows = far_buf.shape[2]
        per_block = devices // 2
        piece_at = pl.ds(pl.multiple_of(me % per_block * piece_rows, piece_rows), piece_rows)
        weight_copy = line_copy(
            0, on_edge,
            w_in.at[far + (last - far) * (me // per_block), piece_at],
            far_piece(me), near,
        )
        edge_out = [
            half_block(1 + 2 * h + q, on_edge, edge, h, near, own=True, q=q)
            for h in range(2)
            for q in range(2)
        ]
        near_to_edge = [half_block(5 + h, inside, near, h, edge, own=True) for h in range(2)]
        near_to_far = [half_block(7 + h, inside, near, h, far, own=True) for h in range(2)]
        far_to_edge = half_block(9, inside, far, 0, edge)
        edge_to_far = [
            half_block(10 + 2 * h + q, inside, edge, h, far, q=q)
            for h in range(2)
            for q in range(2)
        ]
        last_to_edge = [half_block(14 + q, inside, last, 0, edge, q=q) for q in range(2)]

        def pass_edge(h, q):
            half_landed(1 + 2 * h + q, edge, h, q)
            edge_to_far[2 * h + q].start()

        def pass_last(q):
            half_landed(10 + q, last, 0, q)
            last_to_edge[q].start()

        pieces = late
        part_copies = [
            line_copy(16 + i, inside, part_send.at[:, pl.ds(*p)], part_buf.at[:, pl.ds(*p)], edge)
            for i, p in enumerate(pieces)
        ]

        @pl.when(on_edge)
        def _():
            weight_copy.start()
            for copy in edge_out:
                copy.start()

        @pl.when(inside)
        def _():
            for h in range(2):
                near_to_edge[h].start()
                near_to_far[h].start()

        sig_moves[0][0]()
        fil_moves[0][0]()
    else:
        for h in range(halves):
            line_start(0, h)
        for sig_move, fil_move in zip(sig_moves, fil_moves):
            sig_move[0]()
            fil_move[0]()

    def dft(read, target, part):
        span = max(part[1], 8)
        at = (slice(None), slice(part[0], part[0] + span))
        high, low = split_bf16(read(at).reshape(classes * span, 2 * length))
        result = jnp.dot(high, low_ref[...], preferred_element_type=F32)
        result = result + jnp.dot(low, high_ref[...], preferred_element_type=F32)
        result = result + jnp.dot(high, high_ref[...], preferred_element_type=F32)
        target[at] = result.reshape(classes, span, 2 * length)

    def plain(at):
        return stage[at]

    def product(first, second, conjugate):
        def read(at):
            a_re, a_im = first[at][:, :, :length], first[at][:, :, length:]
            b_re, b_im = second[at][:, :, :length], second[at][:, :, length:]
            if conjugate:
                real, minus = a_re * b_re + a_im * b_im, a_im * b_re - a_re * b_im
            else:
                real, minus = a_re * b_re - a_im * b_im, -(a_re * b_im + a_im * b_re)
            return jnp.concatenate((real, minus), axis=2)

        return read

    def over_rows(body, part):
        first = part[0] // group_rows

        @pl.loop(first, first + part[1] // group_rows)
        def _(r):
            body(pl.ds(pl.multiple_of(r * group_rows, group_rows), group_rows))

    def stage_store(at):
        def store(q, real, imag):
            stage[q, at, :length] = real
            stage[q, at, length:] = imag

        return store

    def tap_rows(at):
        return taps_ref[me, at, :]

    def delayed(parts, a, j):
        if j == 0:
            return parts[a]
        before = jnp.zeros_like(parts[a][:, :128]) if a == 0 else parts[a - 1][:, length - 128 :]
        joined = jnp.concatenate((before, parts[a]), axis=1)
        return pltpu.roll(joined, j, 1)[:, 128:]

    def advanced(parts, a, j):
        if j == 0:
            return parts[a]
        after = jnp.zeros_like(parts[a][:, :128]) if a == devices - 1 else parts[a + 1][:, :128]
        joined = jnp.concatenate((parts[a], after), axis=1)
        return pltpu.roll(joined, length + 128 - j, 1)[:, :length]

    w_copy.wait()

    @pl.loop(0, groups)
    def _(g):
        turned = w_buf[g].T
        high, low = split_bf16(turned)
        wt_hi[g] = high
        wt_lo[g] = low

    cot_copy.wait()
    for copy in table_copies:
        copy.wait()

    channels = devices * rows
    table = jnp.concatenate(
        (taps_buf[...], skip_buf[...], jnp.zeros((128 - taps - 1, channels), F32)), axis=0
    )
    table = table.T
    for d in range(devices):
        taps_ref[d] = table[d * rows : (d + 1) * rows, :]

    def mix_add(block, h, first):
        high, low = split_bf16(cot_all[block, :, h * half_len : (h + 1) * half_len])
        result = jnp.dot(wt_lo[block], high, preferred_element_type=F32)
        result = result + jnp.dot(wt_hi[block], low, preferred_element_type=F32)
        result = result + jnp.dot(wt_hi[block], high, preferred_element_type=F32)
        at = (slice(None), slice(h * half_len, (h + 1) * half_len))
        mix[at] = result if first else mix[at] + result

    def mix_step(step, h):
        for up in (True, False):
            @pl.when(arrives(step, up))
            def _():
                mix_add(chan - step if up else chan + step, h, False)

    for h in range(halves):
        mix_add(chan, h, True)

    def conv_rows(at):
        tap = tap_rows(at)
        parts = [sig_buf[a, at, :] for a in range(devices)]
        conv = []
        for a in range(devices):
            total = tap[:, :1] * parts[a]
            for j in range(1, taps):
                total = total + tap[:, j : j + 1] * delayed(parts, a, j)
            conv_buf[a, at, :] = total
            conv.append(total)
        forward_blocks(conv, twiddle, stage_store(at))

    def forward_rows(source):
        def body(at):
            forward_blocks(
                [source[a, at, :] for a in range(devices)], twiddle, stage_store(at)
            )

        return body

    def resp_rows(at):
        skip = tap_rows(at)[:, taps : taps + 1]
        conv = inverse_blocks(devices, length, twiddle, lambda q: work[q, at, :])
        for a in range(devices):
            resp_send[a, at, :] = conv[a] + skip * conv_buf[a, at, :]

    def value_part(i):
        sig_moves[i][1]()
        over_rows(conv_rows, early[i])
        dft(plain, val_spec, early[i])

    def filter_part(i):
        fil_moves[i][1]()
        over_rows(forward_rows(fil_buf), early[i])
        dft(plain, fil_spec, early[i])

    def resp_part(i):
        dft(product(fil_spec, val_spec, False), work, early[i])
        over_rows(resp_rows, early[i])

    def grad_rows(h, first, count):
        here = slice(h * half_len, (h + 1) * half_len)
        for d in range(devices):
            at = slice(d * rows + first, d * rows + first + count)
            grad_send[d, first : first + count, here] = (
                mix[at, here] * gate_buf[d, first : first + count, here]
            )

    def grad_piece(i):
        first, count = pieces[i]
        grad_rows(1, first, count)
        grad_moves[1][i][0]()

    def partial(j, block, sent):
        high, low = split_bf16(cot_all[block, :, half_len:])
        for i, (first, count) in enumerate(pieces):
            at = slice(devices * first, devices * (first + count))
            result = jnp.dot(far_lo[j, at, :], high, preferred_element_type=F32)
            result = result + jnp.dot(far_hi[j, at, :], low, preferred_element_type=F32)
            result = result + jnp.dot(far_hi[j, at, :], high, preferred_element_type=F32)
            result = result.reshape(devices, count, half_len)
            at = (slice(None), slice(first, first + count))
            part_send[at] = part_send[at] + result if j else result
            if sent:
                part_copies[i].start()

    if shared:
        value_part(0)

        @pl.when(inside)
        def _():
            landed(down_sem.at[0], far_piece(me))
            far_copy(far_piece(me), 0, 3, first_peer).start()
            far_copy(far_piece(me), 1, 4, second_peer).start()

        filter_part(0)

        @pl.when(inside)
        def _():
            half_landed(7, far, 0)
            far_to_edge.start()

        resp_part(0)

        @pl.when(inside)
        def _():
            pass_edge(0, 0)
            landed(line_sem.at[3], far_piece(first_peer))
            far_copy(far_piece(first_peer), 1, 4, second_peer).start()
            for index in (me, first_peer):
                far_copy(far_piece(index), 2, 5, sibling).start()

        def start_rest():
            for i in range(1, len(early)):
                fil_moves[i][0]()

        for i in range(1, len(early)):
            sig_moves[i][0]()

        @pl.when(on_edge)
        def _():
            start_rest()
            resp_moves[0][0]()

        @pl.when(on_edge)
        def _():
            for h in range(2):
                half_landed(5 + h, near, h)
                mix_add(near, h, False)

        @pl.when(inside)
        def _():
            pass_edge(0, 1)
            mix_add(far, 0, False)
            half_landed(8, far, 1)
            mix_add(far, 1, False)
            pass_edge(1, 0)
            pass_last(0)
            pass_edge(1, 1)
            landed(line_sem.at[4], far_buf.at[pl.ds(0, 2), 0])
            for index in (second_peer, opposite):
                far_copy(far_piece(index), 2, 5, sibling).start()
            start_rest()
            pass_last(1)
            mix_add(edge, 0, False)
            mix_add(last, 0, False)
            mix_add(edge, 1, False)

        gate_copy.wait()

        def first_grads():
            grad_rows(0, 0, rows)
            for move in grad_moves[0]:
                move[0]()

        @pl.when(on_edge)
        def _():
            half_landed(9, far, 0)
            mix_add(far, 0, False)

        @pl.when(inside)
        def _():
            first_grads()
            landed(line_sem.at[5], far_buf.at[:, 1 - core])

            @pl.loop(0, 2)
            def _(j):
                block = far_buf[pl.ds(j * (per_block // 2), per_block // 2)]
                turned = block.reshape(block.shape[0] * 2 * piece_rows, -1).T
                turned = turned.reshape(devices, rows, -1)
                for first, count in pieces:
                    high, low = split_bf16(
                        turned[:, first : first + count, :].reshape(devices * count, -1)
                    )
                    at = slice(devices * first, devices * (first + count))
                    far_hi[j, at, :] = high
                    far_lo[j, at, :] = low

            partial(0, far, False)
            for q in range(2):
                half_landed(12 + q, last, 1, q)
            partial(1, last, True)
            mix_add(last, 1, False)
            for i in range(len(pieces)):
                grad_piece(i)
            resp_moves[0][0]()

        for i in range(1, len(early)):
            value_part(i)
            filter_part(i)
            resp_part(i)
            resp_moves[i][0]()

        @pl.when(on_edge)
        def _():
            for q in range(2):
                half_landed(14 + q, last, 0, q)
            mix_add(last, 0, False)
            first_grads()
            for i, (first, count) in enumerate(pieces):
                landed(down_sem.at[16 + i], part_buf.at[:, pl.ds(first, count)])
                for d in range(devices):
                    at = slice(d * rows + first, d * rows + first + count)
                    mix[at, half_len:] = mix[at, half_len:] + part_buf[d, first : first + count, :]
                grad_piece(i)

    else:
        for i, part in enumerate(early):
            value_part(i)
            filter_part(i)
            if groups > 1 and i == 0:
                line_arrive(1, 0)
            resp_part(i)
            resp_moves[i][0]()
            if groups > 1 and i == 0:
                for h in range(1, halves):
                    line_arrive(1, h)
        if groups > 1:
            for h in range(halves):
                mix_step(1, h)
        gate_copy.wait()
        for h in range(halves):
            for step in range(2, groups):
                line_arrive(step, h)
                mix_step(step, h)
            grad_rows(h, 0, rows)
            for move in grad_moves[h]:
                move[0]()

    def gate_part():
        for move in resp_moves:
            move[1]()
        for d in range(devices):
            gate_buf[d] = mix[d * rows : (d + 1) * rows, :] * resp_buf[d]
        gate_store.start()

    gate_store = pltpu.make_async_copy(gate_buf, gate_out, load_sem.at[1])

    def filter_rows(at):
        parts = inverse_blocks(devices, length, twiddle, lambda q: work[q, at, :])
        for a in range(devices):
            gfil_send[a, at, :] = parts[a]

    def value_rows(at):
        tap = tap_rows(at)
        skip = tap[:, taps : taps + 1]
        value = inverse_blocks(devices, length, twiddle, lambda q: work[q, at, :])
        grad = [grad_buf[a, at, :] for a in range(devices)]
        value = [value[a] + skip * grad[a] for a in range(devices)]
        sums = [None] * taps
        for a in range(devices):
            signal = sig_buf[a, at, :]
            total = None
            for j in range(taps):
                ahead = advanced(value, a, j)
                term, part_sum = tap[:, j : j + 1] * ahead, ahead * signal
                total = term if total is None else total + term
                sums[j] = part_sum if sums[j] is None else sums[j] + part_sum
            gsig_send[a, at, :] = total
        skip_sum = grad[0] * conv_buf[0, at, :]
        for a in range(1, devices):
            skip_sum = skip_sum + grad[a] * conv_buf[a, at, :]
        lane = lax.broadcasted_iota(jnp.int32, (group_rows, 128), 1)
        placed = jnp.zeros((group_rows, 128), F32)
        for j, each in enumerate(sums + [skip_sum]):
            total = jnp.sum(each, axis=1, keepdims=True) * np.float32(scale)
            placed = jnp.where(lane == j, total, placed)
        small_buf[at, :] = placed

    small_buf[...] = jnp.zeros_like(small_buf)
    for i, part in enumerate(late):
        for h in range(halves):
            grad_moves[h][i][1]()
        over_rows(forward_rows(grad_buf), part)
        dft(plain, grad_spec, part)
        dft(product(val_spec, grad_spec, True), work, part)
        over_rows(filter_rows, part)
        gfil_moves[i][0]()
        dft(product(fil_spec, grad_spec, True), work, part)
        over_rows(value_rows, part)
        if i == len(late) - 1:
            small_send[...] = small_buf[...].T[:8, :]
            small_start()
        gsig_moves[i][0]()
        if i == (len(late) - 1) // 2:
            gate_part()

    for where, copy in line_copies:
        @pl.when(where)
        def _():
            copy.wait_send()

    if shared:
        @pl.when(inside)
        def _():
            landed(line_sem.at[0], far_piece(me))
            landed(line_sem.at[1], far_buf.at[pl.ds(0, 2), 0])
            landed(line_sem.at[2], far_buf.at[:, 0])

    for step in range(0 if shared else groups):
        for up in (True, False):
            @pl.when(sends(step, up))
            def _():
                for h in range(halves):
                    hop(step, h, up).wait_send()

    small_arrive()
    per_tile = 128 // rows
    for tile in range(-(-channels // 128)):
        total = None
        for i in range(min(per_tile, devices - tile * per_tile)):
            each = small_land[tile * per_tile + i]
            each = each if i == 0 else pltpu.roll(each, i * rows, 1)
            total = each if total is None else total + each
        width = min(128, channels - tile * 128)
        at = slice(tile * 128, tile * 128 + width)
        taps_buf[:, at] = total[:taps, :width]
        skip_buf[:, at] = total[taps : taps + 1, :width]
    small_stores = [
        pltpu.make_async_copy(source, target, load_sem.at[2 + i])
        for i, (source, target) in enumerate(((taps_buf, tap_out), (skip_buf, skip_out)))
    ]
    for store in small_stores:
        store.start()
    gate_store.wait()
    for store in small_stores:
        store.wait()
    for sent in moves:
        sent()
    for move in gfil_moves + gsig_moves:
        move[1]()


def handed_on(*refs):
    count = (len(refs) - 1) // 3
    loads, stores = [], []
    for source, result, held in zip(refs[:count], refs[count : 2 * count], refs[2 * count : -1]):
        pieces = 2 if source.shape[0] % 2 == 0 else 1
        size = source.shape[0] // pieces
        for piece in range(pieces):
            at, sems = pl.ds(piece * size, size), refs[-1].at[len(loads)]
            loads.append(pltpu.make_async_copy(source.at[at], held.at[at], sems.at[0]))
            stores.append(pltpu.make_async_copy(held.at[at], result.at[at], sems.at[1]))
    for load in loads:
        load.start()
    for load, store in zip(loads, stores):
        load.wait()
        store.start()
    for store in stores:
        store.wait()


def per_device(signal, gate_in, filter_raw, short_kernel, skip_gain, out_weight, cotangent):
    channels, length = signal.shape
    taps = short_kernel.shape[1]
    devices, groups = lax.axis_size("ctx"), lax.axis_size("chan")
    rows = channels // devices
    rows_pad = max(rows, 8)
    halves = 2
    scale = 1.0 / math.sqrt(length * devices)
    twiddle, high, low = tables(devices, length, scale)
    shape = (devices, rows, length)
    out_rows = cotangent.shape[0]
    early = [(0, rows // 2), (rows // 2, rows // 2)] if rows % 16 == 0 else [(0, rows)]
    late = [(0, rows // 4), (rows // 4, rows // 4), (rows // 2, rows // 2)] if rows % 32 == 0 else [(0, rows)]
    spec_shape = (devices + 1, rows_pad, 2 * length)
    shared = groups == 4 and devices == 8 and len(early) == 2 and len(late) == 3
    far_shape = (4, 2, out_rows // 4, channels) if shared else (1, 2, 8, 128)
    half_shape = (devices, rows, length // 2) if shared else (1, 8, 128)
    dims = (devices, groups, rows, length, taps, halves, early, late, shared, scale)
    moves = 3 * len(early) + (halves + 2) * len(late) + 1

    def vmem(*size, dtype=F32):
        return pltpu.VMEM(size, dtype)

    in_vmem, anywhere = pl.BlockSpec(memory_space=pltpu.VMEM), pl.BlockSpec(memory_space=pl.ANY)
    block = jax.ShapeDtypeStruct(shape, F32)
    results = (block,) * 3 + tuple(
        jax.ShapeDtypeStruct((count, channels), F32) for count in (taps, 1)
    )
    held = pl.pallas_call(
        functools.partial(kernel, dims),
        out_shape=results,
        in_specs=[anywhere] * 10,
        out_specs=(anywhere,) * 5,
        scratch_shapes=[
            vmem(groups, out_rows, channels),
            vmem(groups, channels, out_rows, dtype=BF16),
            vmem(groups, channels, out_rows, dtype=BF16),
            vmem(groups, out_rows, length),
            vmem(channels, length),
            *[vmem(*shape) for _ in range(10)],
            vmem(devices, rows, 128),
            vmem(128, 128),
            vmem(8, 128),
            vmem(devices, 8, 128),
            *[vmem(*spec_shape) for _ in range(5)],
            vmem(*twiddle.shape),
            vmem(*high.shape, dtype=BF16),
            vmem(*low.shape, dtype=BF16),
            vmem(taps, channels),
            vmem(1, channels),
            vmem(*far_shape),
            vmem(2, channels, out_rows, dtype=BF16) if shared else vmem(8, 128),
            vmem(2, channels, out_rows, dtype=BF16) if shared else vmem(8, 128),
            vmem(*half_shape),
            vmem(*half_shape),
            pltpu.SemaphoreType.DMA((19,) if shared else (halves, groups)),
            pltpu.SemaphoreType.DMA((19,) if shared else (halves, groups)),
            pltpu.SemaphoreType.DMA((6,) if shared else (halves, groups)),
            pltpu.SemaphoreType.DMA((moves,)),
            pltpu.SemaphoreType.DMA((moves,)),
            pltpu.SemaphoreType.DMA((8,)),
        ],
        compiler_params=pltpu.CompilerParams(
            collective_id=0, has_side_effects=True, vmem_limit_bytes=56 * 2**20
        ),
    )(
        signal.reshape(shape),
        gate_in.reshape(shape),
        filter_raw.reshape(shape),
        short_kernel.T,
        skip_gain[None, :],
        out_weight.reshape(groups, out_rows, channels),
        cotangent,
        jnp.asarray(twiddle),
        jnp.asarray(high),
        jnp.asarray(low),
    )
    grad_gate, grad_signal, grad_filter, grad_kernel, grad_skip = pl.pallas_call(
        handed_on,
        out_shape=results,
        in_specs=[anywhere] * 5,
        out_specs=(anywhere,) * 5,
        scratch_shapes=[vmem(*each.shape) for each in results]
        + [pltpu.SemaphoreType.DMA((8, 2))],
    )(*held)
    whole = (channels, length)
    return (
        grad_gate.reshape(whole),
        grad_signal.reshape(whole),
        grad_filter.reshape(whole),
        grad_kernel.T,
        grad_skip[0],
    )


def solution(mesh):
    placed = (
        P("chan", "ctx"),
        P("chan", "ctx"),
        P("chan", "ctx"),
        P("chan", None),
        P("chan"),
        P(None, "chan"),
        P("chan", "ctx"),
    )
    return jax.shard_map(
        per_device,
        mesh=mesh,
        in_specs=placed,
        out_specs=(
            P("chan", "ctx"),
            P("chan", "ctx"),
            P("chan", "ctx"),
            P("chan", None),
            P("chan"),
        ),
        check_vma=False,
    )
```

```python
import functools
import math

import jax
import jax.numpy as jnp
import numpy as np
from jax import lax
from jax.experimental import pallas as pl
from jax.experimental.pallas import tpu as pltpu
from jax.sharding import PartitionSpec as P

MESH = pl.DeviceIdType.MESH
F32 = jnp.float32
BF16 = jnp.bfloat16


def split_bf16(value):
    high = value.astype(BF16)
    return high, (value - high.astype(F32)).astype(BF16)


def tables(blocks, length, scale):
    total = 2 * blocks * length
    turn = np.arange(blocks + 1)[:, None] * np.arange(length)[None, :] % total
    angle = 2.0 * np.pi / total * turn
    weight = np.full((blocks + 1, 1), 2.0)
    weight[0] = weight[blocks] = 1.0
    weight = weight * (scale / total)
    twiddle = np.stack(
        (np.cos(angle), np.sin(angle), weight * np.cos(angle), weight * np.sin(angle))
    ).astype(np.float32)
    turn = np.arange(length)[:, None] * np.arange(length)[None, :] % length
    angle = 2.0 * np.pi / length * turn
    cosine, sine = np.cos(angle), np.sin(angle)
    matrix = np.block([[cosine, -sine], [sine, cosine]]).astype(np.float32)
    high = matrix.astype(jnp.bfloat16)
    low = (matrix - high.astype(np.float32)).astype(jnp.bfloat16)
    return twiddle, high, low


def weighted_sum(terms):
    total = None
    for factor, value in terms:
        if abs(factor) < 1e-12:
            continue
        if abs(factor - 1.0) < 1e-12:
            part = value
        elif abs(factor + 1.0) < 1e-12:
            part = -value
        else:
            part = np.float32(factor) * value
        total = part if total is None else total + part
    return total


def forward_blocks(parts, twiddle, store):
    blocks = len(parts)

    def put(q, real, imag):
        cosine, sine = twiddle[0, q : q + 1, :], twiddle[1, q : q + 1, :]
        if imag is None:
            store(q, real * cosine, -real * sine)
        else:
            store(q, real * cosine + imag * sine, imag * cosine - real * sine)

    for q in range(blocks // 2 + 1):
        def gather(first, trig, sign):
            return weighted_sum(
                [(sign * trig(math.pi * a * q / blocks), parts[a]) for a in range(first, blocks, 2)]
            )

        even_re, even_im = gather(0, math.cos, 1.0), gather(0, math.sin, -1.0)
        odd_re, odd_im = gather(1, math.cos, 1.0), gather(1, math.sin, -1.0)

        def add(a, b, sign_a, sign_b):
            return weighted_sum([(s, v) for s, v in ((sign_a, a), (sign_b, b)) if v is not None])

        put(q, add(even_re, odd_re, 1.0, 1.0), add(even_im, odd_im, 1.0, 1.0))
        if q != blocks - q:
            put(blocks - q, add(even_re, odd_re, 1.0, -1.0), add(even_im, odd_im, -1.0, 1.0))


def inverse_blocks(blocks, length, twiddle, load):
    def real_imag(q):
        pair = load(q)
        real, minus = pair[:, :length], pair[:, length:]
        cosine, sine = twiddle[2, q : q + 1, :], twiddle[3, q : q + 1, :]
        return real * cosine + minus * sine, real * sine - minus * cosine

    first, last = real_imag(0)[0], real_imag(blocks)[0]
    half_re, half_im = real_imag(blocks // 2)
    pairs = []
    for q in range(1, blocks // 2):
        (re_a, im_a), (re_b, im_b) = real_imag(q), real_imag(blocks - q)
        pairs.append((re_a + re_b, im_a - im_b, re_a - re_b, im_a + im_b))
    result = []
    for a in range(blocks):
        odd = a % 2
        terms = [(1.0, first - last if odd else first + last)]
        terms.append((math.cos(math.pi * a / 2), half_re))
        terms.append((-math.sin(math.pi * a / 2), half_im))
        for q in range(1, blocks // 2):
            angle = math.pi * a * q / blocks
            terms.append((math.cos(angle), pairs[q - 1][2 * odd]))
            terms.append((-math.sin(angle), pairs[q - 1][2 * odd + 1]))
        result.append(weighted_sum(terms))
    return result


def kernel(
    dims,
    sig_in, gate_in, fil_in, taps_in, skip_in, w_in, cot_in, twiddle_in, high_in, low_in,
    gate_out, gsig_out, gfil_out, tap_out, skip_out,
    w_buf, wt_hi, wt_lo, cot_all, mix, gate_buf, sig_buf, fil_buf, conv_buf,
    resp_send, resp_buf, grad_send, grad_buf, gsig_send, gfil_send, taps_ref, small_buf, small_send, small_land,
    stage, fil_spec, val_spec, grad_spec, work, twiddle, high_ref, low_ref, taps_buf, skip_buf,
    far_buf, far_hi, far_lo, part_send, part_buf,
    up_sem, down_sem, line_sem, send_sem, recv_sem, load_sem,
):
    devices, groups, rows, length, taps, halves, early, late, shared, scale = dims
    me, chan = lax.axis_index("ctx"), lax.axis_index("chan")
    half_len = length // halves
    group_rows = min(8, rows)
    classes = devices + 1

    barrier = pltpu.get_barrier_semaphore()

    @pl.loop(1, devices)
    def _(k):
        pl.semaphore_signal(
            barrier, inc=1, device_id={"ctx": lax.rem(me + k, devices)}, device_id_type=MESH
        )

    for inside, other in ((chan + 1 < groups, chan + 1), (chan >= 1, chan - 1)):
        @pl.when(inside)
        def _():
            pl.semaphore_signal(barrier, inc=1, device_id={"chan": other}, device_id_type=MESH)

    w_copy = pltpu.make_async_copy(w_in, w_buf, load_sem.at[0])
    gate_copy = pltpu.make_async_copy(gate_in, gate_buf, load_sem.at[1])
    cot_copy = pltpu.make_async_copy(cot_in, cot_all.at[chan], load_sem.at[2])
    table_copies = [
        pltpu.make_async_copy(source, target, load_sem.at[3 + i])
        for i, (source, target) in enumerate(
            (
                (taps_in, taps_buf), (skip_in, skip_buf), (twiddle_in, twiddle),
                (high_in, high_ref), (low_in, low_ref),
            )
        )
    ]
    w_copy.start()
    cot_copy.start()
    for copy in table_copies:
        copy.start()
    gate_copy.start()

    beside = (chan + 1 < groups).astype(jnp.int32) + (chan >= 1).astype(jnp.int32)
    pl.semaphore_wait(barrier, devices - 1 + beside)

    def lanes(h):
        return pl.ds(h * half_len, half_len)

    def hop(step, h, up):
        block = chan - step if up else chan + step
        source = cot_in if step == 0 else cot_all.at[block]
        sems = up_sem if up else down_sem
        return pltpu.make_async_remote_copy(
            src_ref=source.at[:, lanes(h)],
            dst_ref=cot_all.at[block, :, lanes(h)],
            send_sem=sems.at[h, step],
            recv_sem=line_sem.at[h, block],
            device_id={"chan": chan + 1 if up else chan - 1},
            device_id_type=MESH,
        )

    def sends(step, up):
        if up:
            return jnp.logical_and(chan - step >= 0, chan + 1 < groups)
        return jnp.logical_and(chan + step < groups, chan >= 1)

    def arrives(step, up):
        return chan - step >= 0 if up else chan + step < groups

    def line_start(step, h):
        for up in (True, False):
            @pl.when(sends(step, up))
            def _():
                hop(step, h, up).start()

    def line_arrive(step, h):
        for up in (True, False):
            @pl.when(arrives(step, up))
            def _():
                block = chan - step if up else chan + step
                slot = cot_all.at[block, :, lanes(h)]
                pltpu.make_async_remote_copy(
                    src_ref=slot,
                    dst_ref=slot,
                    send_sem=up_sem.at[h, step],
                    recv_sem=line_sem.at[h, block],
                    device_id={"chan": chan - 1 if up else chan + 1},
                    device_id_type=MESH,
                ).wait_recv()

                @pl.when(sends(step, up))
                def _():
                    hop(step, h, up).start()

    moves = []

    def all_to_all(source, target, landed):
        index = len(moves)

        def start():
            @pl.loop(1, devices)
            def _(k):
                peer = lax.rem(me + k, devices)
                pltpu.make_async_remote_copy(
                    src_ref=source(peer),
                    dst_ref=target(me),
                    send_sem=send_sem.at[index],
                    recv_sem=recv_sem.at[index],
                    device_id={"ctx": peer},
                    device_id_type=MESH,
                ).start()

            pltpu.make_async_copy(source(me), target(me), recv_sem.at[index]).start()

        def arrive():
            everything = landed(devices)
            pltpu.make_async_copy(everything, everything, recv_sem.at[index]).wait()

        def sent():
            others = landed(devices - 1)
            pltpu.make_async_copy(others, others, send_sem.at[index]).wait()

        moves.append(sent)
        return start, arrive

    def by_part(source, target, part, lane=slice(None)):
        at = pl.ds(*part)
        return all_to_all(
            lambda p: source.at[p, at, lane],
            lambda p: target.at[p, at, lane],
            lambda n: target.at[pl.ds(0, n), at, lane],
        )

    sig_moves = [by_part(sig_in, sig_buf, part) for part in early]
    fil_moves = [by_part(fil_in, fil_buf, part) for part in early]
    resp_moves = [by_part(resp_send, resp_buf, part) for part in early]
    grad_moves = [
        [by_part(grad_send, grad_buf, part, lanes(h)) for part in late] for h in range(halves)
    ]
    gfil_moves = [by_part(gfil_send, gfil_out, part) for part in late]
    gsig_moves = [by_part(gsig_send, gsig_out, part) for part in late]
    small_start, small_arrive = all_to_all(
        lambda p: small_send, lambda p: small_land.at[p], lambda n: small_land.at[pl.ds(0, n)]
    )

    side = chan // 2
    edge, near, far, last = 3 * side, 1 + side, 2 - side, 3 - 3 * side
    on_edge, inside = chan % 3 == 0, chan % 3 != 0
    core = me % 2
    across_x, across_y = me + 2 - 4 * (me // 2 % 2), me + 4 - 8 * (me // 4)
    first_peer = (1 - core) * across_x + core * across_y
    second_peer = (1 - core) * across_y + core * across_x
    sibling, opposite = me + 1 - 2 * core, across_x + across_y - me
    line_copies = []

    def line_copy(index, where, source, target, other):
        copy = pltpu.make_async_remote_copy(
            src_ref=source,
            dst_ref=target,
            send_sem=up_sem.at[index],
            recv_sem=down_sem.at[index],
            device_id={"chan": other},
            device_id_type=MESH,
        )
        line_copies.append((where, copy))
        return copy

    half_rows = cot_all.shape[1] // 2

    def half_block(index, where, block, h, other, own=False, q=None):
        at = slice(None) if q is None else pl.ds(q * half_rows, half_rows)
        slot = cot_all.at[block, at, lanes(h)]
        return line_copy(index, where, cot_in.at[at, lanes(h)] if own else slot, slot, other)

    def landed(sem, ref):
        pltpu.make_async_copy(ref, ref, sem).wait()

    def half_landed(index, block, h, q=None):
        at = slice(None) if q is None else pl.ds(q * half_rows, half_rows)
        landed(down_sem.at[index], cot_all.at[block, at, lanes(h)])

    def far_piece(index):
        return far_buf.at[index // 2, index % 2]

    def far_copy(source, send, recv, peer):
        return pltpu.make_async_remote_copy(
            src_ref=source,
            dst_ref=source,
            send_sem=line_sem.at[send],
            recv_sem=line_sem.at[recv],
            device_id={"ctx": peer},
            device_id_type=MESH,
        )

    if shared:
        piece_rows = far_buf.shape[2]
        per_block = devices // 2
        piece_at = pl.ds(pl.multiple_of(me % per_block * piece_rows, piece_rows), piece_rows)
        weight_copy = line_copy(
            0, on_edge,
            w_in.at[far + (last - far) * (me // per_block), piece_at],
            far_piece(me), near,
        )
        edge_out = [
            half_block(1 + 2 * h + q, on_edge, edge, h, near, own=True, q=q)
            for h in range(2)
            for q in range(2)
        ]
        near_to_edge = [half_block(5 + h, inside, near, h, edge, own=True) for h in range(2)]
        near_to_far = [half_block(7 + h, inside, near, h, far, own=True) for h in range(2)]
        far_to_edge = half_block(9, inside, far, 0, edge)
        edge_to_far = [
            half_block(10 + 2 * h + q, inside, edge, h, far, q=q)
            for h in range(2)
            for q in range(2)
        ]
        last_to_edge = [half_block(14 + q, inside, last, 0, edge, q=q) for q in range(2)]

        def pass_edge(h, q):
            half_landed(1 + 2 * h + q, edge, h, q)
            edge_to_far[2 * h + q].start()

        def pass_last(q):
            half_landed(10 + q, last, 0, q)
            last_to_edge[q].start()

        pieces = late
        part_copies = [
            line_copy(16 + i, inside, part_send.at[:, pl.ds(*p)], part_buf.at[:, pl.ds(*p)], edge)
            for i, p in enumerate(pieces)
        ]

        @pl.when(on_edge)
        def _():
            weight_copy.start()
            for copy in edge_out:
                copy.start()

        @pl.when(inside)
        def _():
            for h in range(2):
                near_to_edge[h].start()
                near_to_far[h].start()

        sig_moves[0][0]()
        fil_moves[0][0]()
    else:
        for h in range(halves):
            line_start(0, h)
        for sig_move, fil_move in zip(sig_moves, fil_moves):
            sig_move[0]()
            fil_move[0]()

    def dft(read, target, part):
        span = max(part[1], 8)
        at = (slice(None), slice(part[0], part[0] + span))
        high, low = split_bf16(read(at).reshape(classes * span, 2 * length))
        result = jnp.dot(high, low_ref[...], preferred_element_type=F32)
        result = result + jnp.dot(low, high_ref[...], preferred_element_type=F32)
        result = result + jnp.dot(high, high_ref[...], preferred_element_type=F32)
        target[at] = result.reshape(classes, span, 2 * length)

    def plain(at):
        return stage[at]

    def product(first, second, conjugate):
        def read(at):
            a_re, a_im = first[at][:, :, :length], first[at][:, :, length:]
            b_re, b_im = second[at][:, :, :length], second[at][:, :, length:]
            if conjugate:
                real, minus = a_re * b_re + a_im * b_im, a_im * b_re - a_re * b_im
            else:
                real, minus = a_re * b_re - a_im * b_im, -(a_re * b_im + a_im * b_re)
            return jnp.concatenate((real, minus), axis=2)

        return read

    def over_rows(body, part):
        first = part[0] // group_rows

        @pl.loop(first, first + part[1] // group_rows)
        def _(r):
            body(pl.ds(pl.multiple_of(r * group_rows, group_rows), group_rows))

    def stage_store(at):
        def store(q, real, imag):
            stage[q, at, :length] = real
            stage[q, at, length:] = imag

        return store

    def tap_rows(at):
        return taps_ref[me, at, :]

    def delayed(parts, a, j):
        if j == 0:
            return parts[a]
        before = jnp.zeros_like(parts[a][:, :128]) if a == 0 else parts[a - 1][:, length - 128 :]
        joined = jnp.concatenate((before, parts[a]), axis=1)
        return pltpu.roll(joined, j, 1)[:, 128:]

    def advanced(parts, a, j):
        if j == 0:
            return parts[a]
        after = jnp.zeros_like(parts[a][:, :128]) if a == devices - 1 else parts[a + 1][:, :128]
        joined = jnp.concatenate((parts[a], after), axis=1)
        return pltpu.roll(joined, length + 128 - j, 1)[:, :length]

    w_copy.wait()

    @pl.loop(0, groups)
    def _(g):
        turned = w_buf[g].T
        high, low = split_bf16(turned)
        wt_hi[g] = high
        wt_lo[g] = low

    cot_copy.wait()
    for copy in table_copies:
        copy.wait()

    channels = devices * rows
    table = jnp.concatenate(
        (taps_buf[...], skip_buf[...], jnp.zeros((128 - taps - 1, channels), F32)), axis=0
    )
    table = table.T
    for d in range(devices):
        taps_ref[d] = table[d * rows : (d + 1) * rows, :]

    def mix_add(block, h, first):
        high, low = split_bf16(cot_all[block, :, h * half_len : (h + 1) * half_len])
        result = jnp.dot(wt_lo[block], high, preferred_element_type=F32)
        result = result + jnp.dot(wt_hi[block], low, preferred_element_type=F32)
        result = result + jnp.dot(wt_hi[block], high, preferred_element_type=F32)
        at = (slice(None), slice(h * half_len, (h + 1) * half_len))
        mix[at] = result if first else mix[at] + result

    def mix_step(step, h):
        for up in (True, False):
            @pl.when(arrives(step, up))
            def _():
                mix_add(chan - step if up else chan + step, h, False)

    for h in range(halves):
        mix_add(chan, h, True)

    def conv_rows(at):
        tap = tap_rows(at)
        parts = [sig_buf[a, at, :] for a in range(devices)]
        conv = []
        for a in range(devices):
            total = tap[:, :1] * parts[a]
            for j in range(1, taps):
                total = total + tap[:, j : j + 1] * delayed(parts, a, j)
            conv_buf[a, at, :] = total
            conv.append(total)
        forward_blocks(conv, twiddle, stage_store(at))

    def forward_rows(source):
        def body(at):
            forward_blocks(
                [source[a, at, :] for a in range(devices)], twiddle, stage_store(at)
            )

        return body

    def resp_rows(at):
        skip = tap_rows(at)[:, taps : taps + 1]
        conv = inverse_blocks(devices, length, twiddle, lambda q: work[q, at, :])
        for a in range(devices):
            resp_send[a, at, :] = conv[a] + skip * conv_buf[a, at, :]

    def value_part(i):
        sig_moves[i][1]()
        over_rows(conv_rows, early[i])
        dft(plain, val_spec, early[i])

    def filter_part(i):
        fil_moves[i][1]()
        over_rows(forward_rows(fil_buf), early[i])
        dft(plain, fil_spec, early[i])

    def resp_part(i):
        dft(product(fil_spec, val_spec, False), work, early[i])
        over_rows(resp_rows, early[i])

    def grad_rows(h, first, count):
        here = slice(h * half_len, (h + 1) * half_len)
        for d in range(devices):
            at = slice(d * rows + first, d * rows + first + count)
            grad_send[d, first : first + count, here] = (
                mix[at, here] * gate_buf[d, first : first + count, here]
            )

    def grad_piece(i):
        first, count = pieces[i]
        grad_rows(1, first, count)
        grad_moves[1][i][0]()

    def partial(j, block, sent):
        high, low = split_bf16(cot_all[block, :, half_len:])
        for i, (first, count) in enumerate(pieces):
            at = slice(devices * first, devices * (first + count))
            result = jnp.dot(far_lo[j, at, :], high, preferred_element_type=F32)
            result = result + jnp.dot(far_hi[j, at, :], low, preferred_element_type=F32)
            result = result + jnp.dot(far_hi[j, at, :], high, preferred_element_type=F32)
            result = result.reshape(devices, count, half_len)
            at = (slice(None), slice(first, first + count))
            part_send[at] = part_send[at] + result if j else result
            if sent:
                part_copies[i].start()

    if shared:
        value_part(0)

        @pl.when(inside)
        def _():
            landed(down_sem.at[0], far_piece(me))
            far_copy(far_piece(me), 0, 3, first_peer).start()
            far_copy(far_piece(me), 1, 4, second_peer).start()

        filter_part(0)

        @pl.when(inside)
        def _():
            half_landed(7, far, 0)
            far_to_edge.start()

        resp_part(0)

        @pl.when(inside)
        def _():
            pass_edge(0, 0)
            landed(line_sem.at[3], far_piece(first_peer))
            far_copy(far_piece(first_peer), 1, 4, second_peer).start()
            for index in (me, first_peer):
                far_copy(far_piece(index), 2, 5, sibling).start()

        def start_rest():
            for i in range(1, len(early)):
                sig_moves[i][0]()
                fil_moves[i][0]()

        @pl.when(on_edge)
        def _():
            start_rest()
            resp_moves[0][0]()

        @pl.when(on_edge)
        def _():
            for h in range(2):
                half_landed(5 + h, near, h)
                mix_add(near, h, False)

        @pl.when(inside)
        def _():
            pass_edge(0, 1)
            mix_add(far, 0, False)
            half_landed(8, far, 1)
            mix_add(far, 1, False)
            pass_edge(1, 0)
            pass_last(0)
            pass_edge(1, 1)
            start_rest()
            landed(line_sem.at[4], far_buf.at[pl.ds(0, 2), 0])
            for index in (second_peer, opposite):
                far_copy(far_piece(index), 2, 5, sibling).start()
            pass_last(1)
            mix_add(edge, 0, False)
            mix_add(last, 0, False)
            mix_add(edge, 1, False)

        gate_copy.wait()

        def first_grads():
            grad_rows(0, 0, rows)
            for move in grad_moves[0]:
                move[0]()

        @pl.when(on_edge)
        def _():
            half_landed(9, far, 0)
            mix_add(far, 0, False)

        @pl.when(inside)
        def _():
            first_grads()
            landed(line_sem.at[5], far_buf.at[:, 1 - core])

            @pl.loop(0, 2)
            def _(j):
                block = far_buf[pl.ds(j * (per_block // 2), per_block // 2)]
                turned = block.reshape(block.shape[0] * 2 * piece_rows, -1).T
                turned = turned.reshape(devices, rows, -1)
                for first, count in pieces:
                    high, low = split_bf16(
                        turned[:, first : first + count, :].reshape(devices * count, -1)
                    )
                    at = slice(devices * first, devices * (first + count))
                    far_hi[j, at, :] = high
                    far_lo[j, at, :] = low

            partial(0, far, False)
            for q in range(2):
                half_landed(12 + q, last, 1, q)
            partial(1, last, True)
            mix_add(last, 1, False)
            for i in range(len(pieces)):
                grad_piece(i)
            resp_moves[0][0]()

        for i in range(1, len(early)):
            value_part(i)
            filter_part(i)
            resp_part(i)
            resp_moves[i][0]()

        @pl.when(on_edge)
        def _():
            for q in range(2):
                half_landed(14 + q, last, 0, q)
            mix_add(last, 0, False)
            first_grads()
            for i, (first, count) in enumerate(pieces):
                landed(down_sem.at[16 + i], part_buf.at[:, pl.ds(first, count)])
                for d in range(devices):
                    at = slice(d * rows + first, d * rows + first + count)
                    mix[at, half_len:] = mix[at, half_len:] + part_buf[d, first : first + count, :]
                grad_piece(i)

    else:
        for i, part in enumerate(early):
            value_part(i)
            filter_part(i)
            if groups > 1 and i == 0:
                line_arrive(1, 0)
            resp_part(i)
            resp_moves[i][0]()
            if groups > 1 and i == 0:
                for h in range(1, halves):
                    line_arrive(1, h)
        if groups > 1:
            for h in range(halves):
                mix_step(1, h)
        gate_copy.wait()
        for h in range(halves):
            for step in range(2, groups):
                line_arrive(step, h)
                mix_step(step, h)
            grad_rows(h, 0, rows)
            for move in grad_moves[h]:
                move[0]()

    def gate_part():
        for move in resp_moves:
            move[1]()
        for d in range(devices):
            gate_buf[d] = mix[d * rows : (d + 1) * rows, :] * resp_buf[d]
        gate_store.start()

    gate_store = pltpu.make_async_copy(gate_buf, gate_out, load_sem.at[1])

    def filter_rows(at):
        parts = inverse_blocks(devices, length, twiddle, lambda q: work[q, at, :])
        for a in range(devices):
            gfil_send[a, at, :] = parts[a]

    def value_rows(at):
        tap = tap_rows(at)
        skip = tap[:, taps : taps + 1]
        value = inverse_blocks(devices, length, twiddle, lambda q: work[q, at, :])
        grad = [grad_buf[a, at, :] for a in range(devices)]
        value = [value[a] + skip * grad[a] for a in range(devices)]
        sums = [None] * taps
        for a in range(devices):
            signal = sig_buf[a, at, :]
            total = None
            for j in range(taps):
                ahead = advanced(value, a, j)
                term, part_sum = tap[:, j : j + 1] * ahead, ahead * signal
                total = term if total is None else total + term
                sums[j] = part_sum if sums[j] is None else sums[j] + part_sum
            gsig_send[a, at, :] = total
        skip_sum = grad[0] * conv_buf[0, at, :]
        for a in range(1, devices):
            skip_sum = skip_sum + grad[a] * conv_buf[a, at, :]
        lane = lax.broadcasted_iota(jnp.int32, (group_rows, 128), 1)
        placed = jnp.zeros((group_rows, 128), F32)
        for j, each in enumerate(sums + [skip_sum]):
            total = jnp.sum(each, axis=1, keepdims=True) * np.float32(scale)
            placed = jnp.where(lane == j, total, placed)
        small_buf[at, :] = placed

    small_buf[...] = jnp.zeros_like(small_buf)
    for i, part in enumerate(late):
        for h in range(halves):
            grad_moves[h][i][1]()
        over_rows(forward_rows(grad_buf), part)
        dft(plain, grad_spec, part)
        dft(product(val_spec, grad_spec, True), work, part)
        over_rows(filter_rows, part)
        gfil_moves[i][0]()
        dft(product(fil_spec, grad_spec, True), work, part)
        over_rows(value_rows, part)
        if i == len(late) - 1:
            small_send[...] = small_buf[...].T[:8, :]
            small_start()
        gsig_moves[i][0]()
        if i == (len(late) - 1) // 2:
            gate_part()

    for where, copy in line_copies:
        @pl.when(where)
        def _():
            copy.wait_send()

    if shared:
        @pl.when(inside)
        def _():
            landed(line_sem.at[0], far_piece(me))
            landed(line_sem.at[1], far_buf.at[pl.ds(0, 2), 0])
            landed(line_sem.at[2], far_buf.at[:, 0])

    for step in range(0 if shared else groups):
        for up in (True, False):
            @pl.when(sends(step, up))
            def _():
                for h in range(halves):
                    hop(step, h, up).wait_send()

    small_arrive()
    per_tile = 128 // rows
    for tile in range(-(-channels // 128)):
        total = None
        for i in range(min(per_tile, devices - tile * per_tile)):
            each = small_land[tile * per_tile + i]
            each = each if i == 0 else pltpu.roll(each, i * rows, 1)
            total = each if total is None else total + each
        width = min(128, channels - tile * 128)
        at = slice(tile * 128, tile * 128 + width)
        taps_buf[:, at] = total[:taps, :width]
        skip_buf[:, at] = total[taps : taps + 1, :width]
    small_stores = [
        pltpu.make_async_copy(source, target, load_sem.at[2 + i])
        for i, (source, target) in enumerate(((taps_buf, tap_out), (skip_buf, skip_out)))
    ]
    for store in small_stores:
        store.start()
    gate_store.wait()
    for store in small_stores:
        store.wait()
    for sent in moves:
        sent()
    for move in gfil_moves + gsig_moves:
        move[1]()


def handed_on(*refs):
    count = (len(refs) - 1) // 3
    loads, stores = [], []
    for source, result, held in zip(refs[:count], refs[count : 2 * count], refs[2 * count : -1]):
        pieces = 2 if source.shape[0] % 2 == 0 else 1
        size = source.shape[0] // pieces
        for piece in range(pieces):
            at, sems = pl.ds(piece * size, size), refs[-1].at[len(loads)]
            loads.append(pltpu.make_async_copy(source.at[at], held.at[at], sems.at[0]))
            stores.append(pltpu.make_async_copy(held.at[at], result.at[at], sems.at[1]))
    for load in loads:
        load.start()
    for load, store in zip(loads, stores):
        load.wait()
        store.start()
    for store in stores:
        store.wait()


def per_device(signal, gate_in, filter_raw, short_kernel, skip_gain, out_weight, cotangent):
    channels, length = signal.shape
    taps = short_kernel.shape[1]
    devices, groups = lax.axis_size("ctx"), lax.axis_size("chan")
    rows = channels // devices
    rows_pad = max(rows, 8)
    halves = 2
    scale = 1.0 / math.sqrt(length * devices)
    twiddle, high, low = tables(devices, length, scale)
    shape = (devices, rows, length)
    out_rows = cotangent.shape[0]
    early = [(0, rows // 2), (rows // 2, rows // 2)] if rows % 16 == 0 else [(0, rows)]
    late = [(0, rows // 4), (rows // 4, rows // 4), (rows // 2, rows // 2)] if rows % 32 == 0 else [(0, rows)]
    spec_shape = (devices + 1, rows_pad, 2 * length)
    shared = groups == 4 and devices == 8 and len(early) == 2 and len(late) == 3
    far_shape = (4, 2, out_rows // 4, channels) if shared else (1, 2, 8, 128)
    half_shape = (devices, rows, length // 2) if shared else (1, 8, 128)
    dims = (devices, groups, rows, length, taps, halves, early, late, shared, scale)
    moves = 3 * len(early) + (halves + 2) * len(late) + 1

    def vmem(*size, dtype=F32):
        return pltpu.VMEM(size, dtype)

    in_vmem, anywhere = pl.BlockSpec(memory_space=pltpu.VMEM), pl.BlockSpec(memory_space=pl.ANY)
    block = jax.ShapeDtypeStruct(shape, F32)
    results = (block,) * 3 + tuple(
        jax.ShapeDtypeStruct((count, channels), F32) for count in (taps, 1)
    )
    held = pl.pallas_call(
        functools.partial(kernel, dims),
        out_shape=results,
        in_specs=[anywhere] * 10,
        out_specs=(anywhere,) * 5,
        scratch_shapes=[
            vmem(groups, out_rows, channels),
            vmem(groups, channels, out_rows, dtype=BF16),
            vmem(groups, channels, out_rows, dtype=BF16),
            vmem(groups, out_rows, length),
            vmem(channels, length),
            *[vmem(*shape) for _ in range(10)],
            vmem(devices, rows, 128),
            vmem(128, 128),
            vmem(8, 128),
            vmem(devices, 8, 128),
            *[vmem(*spec_shape) for _ in range(5)],
            vmem(*twiddle.shape),
            vmem(*high.shape, dtype=BF16),
            vmem(*low.shape, dtype=BF16),
            vmem(taps, channels),
            vmem(1, channels),
            vmem(*far_shape),
            vmem(2, channels, out_rows, dtype=BF16) if shared else vmem(8, 128),
            vmem(2, channels, out_rows, dtype=BF16) if shared else vmem(8, 128),
            vmem(*half_shape),
            vmem(*half_shape),
            pltpu.SemaphoreType.DMA((19,) if shared else (halves, groups)),
            pltpu.SemaphoreType.DMA((19,) if shared else (halves, groups)),
            pltpu.SemaphoreType.DMA((6,) if shared else (halves, groups)),
            pltpu.SemaphoreType.DMA((moves,)),
            pltpu.SemaphoreType.DMA((moves,)),
            pltpu.SemaphoreType.DMA((8,)),
        ],
        compiler_params=pltpu.CompilerParams(
            collective_id=0, has_side_effects=True, vmem_limit_bytes=56 * 2**20
        ),
    )(
        signal.reshape(shape),
        gate_in.reshape(shape),
        filter_raw.reshape(shape),
        short_kernel.T,
        skip_gain[None, :],
        out_weight.reshape(groups, out_rows, channels),
        cotangent,
        jnp.asarray(twiddle),
        jnp.asarray(high),
        jnp.asarray(low),
    )
    grad_gate, grad_signal, grad_filter, grad_kernel, grad_skip = pl.pallas_call(
        handed_on,
        out_shape=results,
        in_specs=[anywhere] * 5,
        out_specs=(anywhere,) * 5,
        scratch_shapes=[vmem(*each.shape) for each in results]
        + [pltpu.SemaphoreType.DMA((8, 2))],
    )(*held)
    whole = (channels, length)
    return (
        grad_gate.reshape(whole),
        grad_signal.reshape(whole),
        grad_filter.reshape(whole),
        grad_kernel.T,
        grad_skip[0],
    )


def solution(mesh):
    placed = (
        P("chan", "ctx"),
        P("chan", "ctx"),
        P("chan", "ctx"),
        P("chan", None),
        P("chan"),
        P(None, "chan"),
        P("chan", "ctx"),
    )
    return jax.shard_map(
        per_device,
        mesh=mesh,
        in_specs=placed,
        out_specs=(
            P("chan", "ctx"),
            P("chan", "ctx"),
            P("chan", "ctx"),
            P("chan", None),
            P("chan"),
        ),
        check_vma=False,
    )
```
